32 devices in a mesh: dp: 8 (over z, y), tensor: 4 (over x, core).
Axes of the slice: x: 2, y: 2, z: 4, core: 2. Of those that a mesh axis runs over, the one named last changes fastest.
Arguments:
- tokens: bfloat16 [8, 2048, 768], P('dp', 'tensor'), may hold values from -6 to 6
- segment_ids: int32 [8, 2048], P('dp'), may hold values from 0 to 7, never falling along the last dimension, each value on 1 to 1024 neighbouring positions
- cotangent: bfloat16 [8, 2048, 768], P('dp', 'tensor'), may hold values from -6 to 6
- attention_norm1_gain: bfloat16 [768], replicated, may hold values from 0.5 to 1.5
- attention_norm1_bias: bfloat16 [768], replicated, may hold values from -3 to 3
- feedforward_norm2_gain: bfloat16 [768], replicated, may hold values from 0.5 to 1.5
- feedforward_norm2_bias: bfloat16 [768], replicated, may hold values from -3 to 3
- qkv_weight: bfloat16 [768, 2304], P(None, 'tensor'), may hold values from -0.21875 to 0.21875
- qkv_bias: bfloat16 [2304], P('tensor'), may hold values from -3 to 3
- dense_weight: bfloat16 [768, 768], P('tensor'), may hold values from -2.5 to 2.5
- dense_bias: bfloat16 [768], replicated, may hold values from -3 to 3
- fc_in_weight: bfloat16 [768, 3072], P(None, 'tensor'), may hold values from -0.21875 to 0.21875
- fc_in_bias: bfloat16 [3072], P('tensor'), may hold values from -3 to 3
- fc_out_weight: bfloat16 [3072, 768], P('tensor'), may hold values from -0.109375 to 0.109375
- fc_out_bias: bfloat16 [768], replicated, may hold values from -3 to 3
Outputs:
- result: bfloat16 [8, 2048, 768], P('dp', 'tensor')
- tokens_grad: float32 [8, 2048, 768], P('dp', 'tensor')
- ln1_gain_grad: float32 [768], replicated
- ln1_bias_grad: float32 [768], replicated
- ln2_gain_grad: float32 [768], replicated
- ln2_bias_grad: float32 [768], replicated
- qkv_weight_grad: float32 [768, 2304], P(None, 'tensor')
- qkv_bias_grad: float32 [2304], P('tensor')
- dense_weight_grad: float32 [768, 768], P('tensor')
- dense_bias_grad: float32 [768], replicated
- fc_in_weight_grad: float32 [768, 3072], P(None, 'tensor')
- fc_in_bias_grad: float32 [3072], P('tensor')
- fc_out_weight_grad: float32 [3072, 768], P('tensor')
- fc_out_bias_grad: float32 [768], replicated
The draws below stay inside these ranges and needn't reach their ends.
Inputs may be any that keep to these rules, and one draw needn't show every extreme that they name: `segment_ids`: along a row segment numbers never fall; each of the 8 numbers covers 1 to 1024 positions of every row, one exactly 1024.
All inputs are finite; a program needn't handle non-finite values.
Results may differ from the reference program's by a relative error of at most 0.013.
Values may be sent and summed in bfloat16 or wider, within the bound.
No kernel may reach another device: no remote copies, remote signals or barrier semaphores. Data moves between devices by JAX's collectives and lax.ppermute only.
A program may use at most 128 MiB of HBM per device.

```python
import math
import jax
import jax.numpy as jnp
import numpy as np
from jax import lax

D = 768
HEADS = 12
HEAD_DIM = 64
FF = 3072
ROT = 16
SEQ = 2048
ROWS = 8
SEGS = 8
MOST = 1024


def steps_of(rng, shape, pieces, low, top_value):
    gain, own = 1.0, jax.random.fold_in(rng, 6)
    for dim, blocks in pieces:
        draws = jnp.exp(jax.random.uniform(jax.random.fold_in(own, dim), (blocks,), jnp.float32, low / len(pieces), top_value / len(pieces)))
        gain = gain * jnp.repeat(draws, shape[dim] // blocks).reshape([-1 if axis == dim else 1 for axis in range(len(shape))])
    return gain


def profile(count, total, reach, skew):
    weights = [(1 << 20) // math.isqrt(rank ** skew) + 1 for rank in range(2, count + 1)]
    rest, holding = total - reach - (count - 1), [1] * (count - 1)
    while rest > 0:
        candidates = [i for i in range(count - 1) if holding[i] < reach]
        pool, left = sum([weights[i] for i in candidates]), rest
        for i in candidates:
            addition = min(reach - holding[i], max(1, left * weights[i] // pool), rest)
            holding[i] = holding[i] + addition
            rest = rest - addition
    return np.array([reach] + holding)


def ragged(own_key, count, total, limit, skew):
    if count == 2:
        one = jax.random.randint(own_key, (), max(1, total - limit), min(limit, total - 1) + 1)
        return jnp.stack([one, total - one])
    sizes = jnp.asarray(profile(count, total, limit, skew), jnp.int32)
    pairs = (count - 1) // 2
    donor, taker = sizes[1:1 + 2 * pairs:2], sizes[2:2 + 2 * pairs:2]
    slack = jnp.minimum(donor - 1, limit - taker)
    moved = jax.random.randint(jax.random.fold_in(own_key, 1), (pairs,), 0, 1 << 20) % (slack + 1)
    sizes = sizes.at[1:1 + 2 * pairs:2].set(donor - moved).at[2:2 + 2 * pairs:2].set(taker + moved)
    return sizes[jax.random.permutation(jax.random.fold_in(own_key, 2), count)]


def bell_draw(own_key, dims, scale, reach, pieces=(), held_as=jnp.bfloat16):
    array = jax.random.normal(own_key, dims, jnp.float32) * scale
    if len(pieces) > 0:
        array = steps_of(own_key, dims, pieces, -0.22, 0.18) * array
    return jnp.clip(array, min=-reach, max=reach).astype(held_as)


def setup_inputs(seed: int = 0) -> dict:
    key_of = jax.random.split(jax.random.key(seed), 16)
    return {
        "tokens": bell_draw(key_of[0], (ROWS, SEQ, D), 1.0, 6.0, ((0, 8), (1, 4))),
        "segment_ids": jax.vmap(lambda own: jnp.searchsorted(jnp.cumsum(ragged(own, SEGS, SEQ, MOST, 2)), jnp.arange(SEQ), side="right"))(jax.random.split(key_of[1], ROWS)).reshape((ROWS, SEQ)).astype(jnp.int32),
        "cotangent": bell_draw(key_of[2], (ROWS, SEQ, D), 1.0, 6.0, ((0, 8), (1, 4))),
        "attention_norm1_gain": jnp.clip(1.0 + 0.1 * jax.random.normal(key_of[3], (D,), jnp.float32), 0.5, 1.5).astype(jnp.bfloat16),
        "attention_norm1_bias": bell_draw(key_of[4], (D,), 0.5, 3.0),
        "feedforward_norm2_gain": jnp.clip(1.0 + 0.1 * jax.random.normal(key_of[5], (D,), jnp.float32), 0.5, 1.5).astype(jnp.bfloat16),
        "feedforward_norm2_bias": bell_draw(key_of[6], (D,), 0.5, 3.0),
        "qkv_weight": bell_draw(key_of[7], (D, 3 * D), D ** -0.5, 0.21875, ((1, 4),)),
        "qkv_bias": bell_draw(key_of[8], (3 * D,), 0.5, 3.0, ((0, 4),)),
        "dense_weight": bell_draw(key_of[9], (D, D), (max(D // 128, 2)) ** -0.5, 2.5, ((0, 4),)),
        "dense_bias": bell_draw(key_of[10], (D,), 0.5, 3.0),
        "fc_in_weight": bell_draw(key_of[11], (D, FF), D ** -0.5, 0.21875, ((1, 4),)),
        "fc_in_bias": bell_draw(key_of[12], (FF,), 0.5, 3.0, ((0, 4),)),
        "fc_out_weight": bell_draw(key_of[13], (FF, D), FF ** -0.5, 0.109375, ((0, 4),)),
        "fc_out_bias": bell_draw(key_of[14], (D,), 0.5, 3.0),
    }


@jax.custom_vjp
def low(v):
    return lax.optimization_barrier(v.astype(jnp.bfloat16)).astype(jnp.float32)

@jax.custom_vjp
def low_back(v):
    return v

def low_keep(v):
    return (low(v), None)

def low_pass(kept, upstream_gradient):
    return (upstream_gradient,)

def back_keep(v):
    return (v, None)

def back_low(kept, upstream_gradient):
    return (low(upstream_gradient),)
low.defvjp(low_keep, low_pass)
low_back.defvjp(back_keep, back_low)
NEG = -1e+30

def layer_norm(value, norm_gain, shift_bias):
    row_average = lax.optimization_barrier(jnp.mean(value, axis=-1, keepdims=True))
    centered_input = value - row_average
    var = lax.optimization_barrier(jnp.mean(centered_input * centered_input, axis=-1, keepdims=True))
    return centered_input * lax.rsqrt(var + 1e-05) * norm_gain + shift_bias

def rotary_tables(length, rot):
    half = rot // 2
    freq = 10000.0 ** (-(jnp.arange(half, dtype=jnp.float32) * 2.0) / rot)
    angle = jnp.arange(length, dtype=jnp.float32)[:, None] * freq[None, :]
    angle = jnp.concatenate([angle, angle], axis=1)
    return (jnp.cos(angle), jnp.sin(angle))

def rotate(field, cosine, sine):
    rot = cosine.shape[1]
    half = rot // 2
    part = field[..., :rot]
    turned = jnp.concatenate([-part[..., half:], part[..., :half]], axis=-1)
    moved = part * cosine[:, None, :] + turned * sine[:, None, :]
    return jnp.concatenate([moved, field[..., rot:]], axis=-1)

def forward_row(params, row, ids):
    g1, b1, g2, b2, wqkv, bqkv, wdense, bdense, w_one, c_one, w_two, c_two = params
    highest = lax.Precision.HIGHEST
    seq = row.shape[0]
    scale = HEAD_DIM ** (-0.5)
    normed1 = low(layer_norm(row, g1, b1))
    normed2 = low(layer_norm(row, g2, b2))
    qkv = low_back(jnp.dot(normed1, wqkv, precision=highest) + bqkv)
    qkv = qkv.reshape(seq, HEADS, 3, HEAD_DIM)
    cosine, sine = rotary_tables(seq, ROT)
    query = low(rotate(qkv[:, :, 0], cosine, sine))
    keys = low(rotate(qkv[:, :, 1], cosine, sine))
    values = low(qkv[:, :, 2])
    block = min(512, seq)
    count = seq // block
    positions = jnp.arange(seq, dtype=jnp.int32)

    def one_block(items):
        qblock, qpos, qseg = items
        scores = jnp.einsum('qhd,khd->hqk', qblock, keys, precision=highest) * scale
        scores = low_back(scores)
        mask = (qseg[:, None] == ids[None, :]) & (positions[None, :] <= qpos[:, None])
        scores = jnp.where(mask[None], scores, NEG)
        probs = low(jax.nn.softmax(scores, axis=-1))
        return jnp.einsum('hqk,khd->qhd', probs, values, precision=highest)
    mixed = lax.map(jax.checkpoint(one_block), (query.reshape(count, block, HEADS, HEAD_DIM), positions.reshape(count, block), ids.reshape(count, block)))
    mixed = low_back(low(mixed.reshape(seq, HEADS * HEAD_DIM)))
    attn = jnp.dot(mixed, wdense, precision=highest) + bdense
    pre = low_back(jnp.dot(normed2, w_one, precision=highest) + c_one)
    act = low(jax.nn.gelu(pre, approximate=False))
    mlp = jnp.dot(act, w_two, precision=highest) + c_two
    return row + attn + mlp

def reference(tokens, segment_ids, cotangent, attention_norm1_gain, attention_norm1_bias, feedforward_norm2_gain, feedforward_norm2_bias, qkv_weight, qkv_bias, dense_weight, dense_bias, fc_in_weight, fc_in_bias, fc_out_weight, fc_out_bias):
    params = tuple((p.astype(jnp.float32) for p in (attention_norm1_gain, attention_norm1_bias, feedforward_norm2_gain, feedforward_norm2_bias, qkv_weight, qkv_bias, dense_weight, dense_bias, fc_in_weight, fc_in_bias, fc_out_weight, fc_out_bias)))

    def step(grads, item):
        row, ids, grad_row = item
        output, pull = jax.vjp(lambda prm, value: forward_row(prm, value, ids), params, row.astype(jnp.float32))
        grad_params, grad_input = pull(grad_row.astype(jnp.float32))
        grads = jax.tree.map(lambda first_branch, second_branch: first_branch + second_branch, grads, grad_params)
        return (grads, (output.astype(jnp.bfloat16), grad_input))
    zeros = tuple((jnp.zeros_like(p) for p in params))
    grads, (outputs, input_grads) = lax.scan(step, zeros, (tokens, segment_ids, cotangent))
    return (outputs, input_grads, grads[0], grads[1], grads[2], grads[3], grads[4], grads[5], grads[6], grads[7], grads[8], grads[9], grads[10], grads[11])
```

```python
from functools import partial

import jax
import jax.numpy as jnp
import numpy as np
from jax import lax
from jax.experimental import pallas as pl
from jax.experimental.pallas import tpu as pltpu
from jax.sharding import PartitionSpec as P

HEAD_DIM = 64
ROT = 16
SEGS = 8
BLK = 256
NEG = -1e30
LOG2E = 1.4426950408889634
f32, bf16 = jnp.float32, jnp.bfloat16
VMEM = pl.BlockSpec(memory_space=pltpu.VMEM)
SMEM = pl.BlockSpec(memory_space=pltpu.SMEM)


def dot(a, b):
    return jnp.dot(a, b, preferred_element_type=f32)


def dot_nt(a, b):
    return lax.dot_general(a, b, (((1,), (1,)), ((), ())), preferred_element_type=f32)


def dot_tn(a, b):
    return lax.dot_general(a, b, (((0,), (0,)), ((), ())), preferred_element_type=f32)


def swap(value, axis, size, distance):
    return lax.ppermute(value, axis, [(i, i ^ distance) for i in range(size)])


def gather_relative(shard, size):
    pieces = {0: shard}
    bit = size // 2
    while bit:
        for k in sorted(pieces):
            pieces[k | bit] = swap(pieces[k], "tensor", size, bit)
        bit //= 2
    return [pieces[k] for k in range(size)]


def scatter_relative(chunks, size):
    bit = 1
    while bit < size:
        keep = [k for k in sorted(chunks) if not k & bit]
        sent = jnp.concatenate([chunks[k | bit].astype(bf16) for k in keep], axis=0)
        got = swap(sent, "tensor", size, bit).astype(f32)
        rows = got.shape[0] // len(keep)
        chunks = {k: chunks[k] + got[i * rows : (i + 1) * rows] for i, k in enumerate(keep)}
        bit *= 2
    return chunks[0]


def factors(count):
    out = []
    for f in (2, 4):
        if count % f == 0:
            out.append(f)
            count //= f
    if count > 1:
        out.append(count)
    return out


def shifted(value, size, stride, factor, shift):
    pairs = []
    for i in range(size):
        digit = (i // stride) % factor
        pairs.append((i, i + ((digit + shift) % factor - digit) * stride))
    return lax.ppermute(value, "dp", pairs)


def sum_over_rows(value, size):
    index = lax.axis_index("dp")
    trail, stride = [], 1
    for factor in factors(size):
        digit = (index // stride) % factor
        rows = value.shape[0] // factor
        total = lax.dynamic_slice_in_dim(value, digit * rows, rows, 0).astype(f32)
        for shift in range(1, factor):
            part = lax.dynamic_slice_in_dim(value, ((digit + shift) % factor) * rows, rows, 0)
            total = total + shifted(part.astype(bf16), size, stride, factor, shift).astype(f32)
        value = total
        trail.append((factor, stride, digit, rows))
        stride *= factor
    value = value.astype(bf16)
    for factor, stride, digit, rows in reversed(trail):
        full = jnp.zeros((factor * rows, value.shape[1]), bf16)
        full = lax.dynamic_update_slice_in_dim(full, value, digit * rows, 0)
        for shift in range(1, factor):
            got = shifted(value, size, stride, factor, shift)
            full = lax.dynamic_update_slice_in_dim(
                full, got, ((digit - shift + factor) % factor) * rows, 0
            )
        value = full
    return value


def attend_kernel(lo_ref, phys_ref, start_ref, qkv_ref, o_ref, lse_ref, kn_ref):
    heads, seq = qkv_ref.shape[0], qkv_ref.shape[3]
    count = seq // BLK
    for h in range(heads):
        for b in range(count):
            rows = slice(b * BLK, (b + 1) * BLK)
            kn_ref[h, rows, :] = qkv_ref[h, 1, :, rows].T
    ik = lax.broadcasted_iota(jnp.int32, (BLK, BLK), 0)
    iq = lax.broadcasted_iota(jnp.int32, (BLK, BLK), 1)

    @pl.loop(0, count)
    def _(i):
        qs = pl.ds(pl.multiple_of(phys_ref[i] * BLK, BLK), BLK)
        start = start_ref[0:1, pl.ds(pl.multiple_of(i * BLK, BLK), BLK)]

        def step(ks, mask, carry):
            scores = [
                jnp.where(mask, dot(kn_ref[h, ks, :], qkv_ref[h, 0, :, qs]), NEG)
                for h in range(heads)
            ]
            out = []
            for h in range(heads):
                top = jnp.max(scores[h], axis=0, keepdims=True)
                if carry is not None:
                    top = jnp.maximum(top, carry[h][0])
                expo = jnp.exp2(scores[h] * LOG2E - top * LOG2E)
                total = jnp.sum(expo, axis=0, keepdims=True)
                mixed = dot(qkv_ref[h, 2, :, ks], expo.astype(bf16))
                if carry is not None:
                    fade = jnp.exp2((carry[h][0] - top) * LOG2E)
                    total = total + carry[h][1] * fade
                    mixed = mixed + carry[h][2] * fade
                out.append((top, total, mixed))
            return tuple(out)

        def body(j, carry):
            ks = pl.ds(pl.multiple_of(phys_ref[j] * BLK, BLK), BLK)
            return step(ks, ik >= start - j * BLK, carry)

        carry = step(qs, (ik <= iq) & (ik >= start - i * BLK), None)
        carry = lax.fori_loop(lo_ref[i], i, body, carry)
        for h in range(heads):
            top, total, mixed = carry[h]
            o_ref[h, :, qs] = (mixed * (1.0 / total)).astype(bf16)
            lse_ref[h, 0:1, qs] = top * LOG2E + jnp.log2(total)


def attend(lo, phys, start, qkv):
    heads, _, dim, seq = qkv.shape
    return pl.pallas_call(
        attend_kernel,
        out_shape=(
            jax.ShapeDtypeStruct((heads, dim, seq), bf16),
            jax.ShapeDtypeStruct((heads, 1, seq), f32),
        ),
        in_specs=[SMEM, SMEM, VMEM, VMEM],
        out_specs=(VMEM, VMEM),
        scratch_shapes=[pltpu.VMEM((heads, seq, dim), bf16)],
        cost_estimate=pl.CostEstimate(
            flops=12_000_000_000, bytes_accessed=4_000_000, transcendentals=6_000_000
        ),
        name="attend",
    )(lo, phys, start, qkv)


def attend_back_kernel(
    lo_ref, phys_ref, start_ref, qkv_ref, o_ref, do_ref, lse_ref, cos_ref, sin_ref,
    dqkv_ref, kn_ref, vn_ref, dk_ref, dv_ref,
):
    heads, seq = qkv_ref.shape[0], qkv_ref.shape[3]
    count = seq // BLK
    half = ROT // 2
    for h in range(heads):
        for b in range(count):
            rows = slice(b * BLK, (b + 1) * BLK)
            kn_ref[h, rows, :] = qkv_ref[h, 1, :, rows].T
            vn_ref[h, rows, :] = qkv_ref[h, 2, :, rows].T
    dk_ref[...] = jnp.zeros_like(dk_ref)
    dv_ref[...] = jnp.zeros_like(dv_ref)
    ik = lax.broadcasted_iota(jnp.int32, (BLK, BLK), 0)
    iq = lax.broadcasted_iota(jnp.int32, (BLK, BLK), 1)

    def unrotate(grad, cosine, sine):
        one, two = grad[:half], grad[half:ROT]
        return jnp.concatenate(
            [one * cosine + two * sine, two * cosine - one * sine, grad[ROT:]], axis=0
        )

    @pl.loop(0, count)
    def _(i):
        qs = pl.ds(pl.multiple_of(phys_ref[i] * BLK, BLK), BLK)
        here = pl.ds(pl.multiple_of(i * BLK, BLK), BLK)
        start = start_ref[0:1, here]
        delta = [
            jnp.sum(
                do_ref[h, :, qs].astype(f32) * o_ref[h, :, qs].astype(f32), axis=0, keepdims=True
            )
            for h in range(heads)
        ]
        lse = [lse_ref[h, 0:1, qs] for h in range(heads)]

        def step(ks, mask, carry):
            scores = [
                jnp.where(mask, dot(kn_ref[h, ks, :], qkv_ref[h, 0, :, qs]), NEG)
                for h in range(heads)
            ]
            dprobs = [dot(vn_ref[h, ks, :], do_ref[h, :, qs]) for h in range(heads)]
            probs = [jnp.exp2(scores[h] * LOG2E - lse[h]) for h in range(heads)]
            dscores = [(probs[h] * (dprobs[h] - delta[h])).astype(bf16) for h in range(heads)]
            out = []
            for h in range(heads):
                dv_ref[h, :, ks] += dot_nt(do_ref[h, :, qs], probs[h].astype(bf16))
                dk_ref[h, :, ks] += dot_nt(qkv_ref[h, 0, :, qs], dscores[h])
                dq = dot(qkv_ref[h, 1, :, ks], dscores[h])
                out.append(dq if carry is None else carry[h] + dq)
            return tuple(out)

        def body(j, carry):
            ks = pl.ds(pl.multiple_of(phys_ref[j] * BLK, BLK), BLK)
            return step(ks, ik >= start - j * BLK, carry)

        carry = step(qs, (ik <= iq) & (ik >= start - i * BLK), None)
        carry = lax.fori_loop(lo_ref[i], i, body, carry)
        for h in range(heads):
            dq = unrotate(carry[h] * HEAD_DIM ** (-0.5), cos_ref[:, here], sin_ref[:, here])
            dqkv_ref[h, 0, :, qs] = dq.astype(bf16)

    @pl.loop(0, count)
    def _(i):
        qs = pl.ds(pl.multiple_of(phys_ref[i] * BLK, BLK), BLK)
        here = pl.ds(pl.multiple_of(i * BLK, BLK), BLK)
        for h in range(heads):
            dk = unrotate(dk_ref[h, :, qs], cos_ref[:, here], sin_ref[:, here])
            dqkv_ref[h, 1, :, qs] = dk.astype(bf16)
            dqkv_ref[h, 2, :, qs] = dv_ref[h, :, qs].astype(bf16)


def attend_back(lo, phys, start, qkv, mixed, dmixed, lse, cosine, sine):
    heads, _, dim, seq = qkv.shape
    return pl.pallas_call(
        attend_back_kernel,
        out_shape=jax.ShapeDtypeStruct(qkv.shape, bf16),
        in_specs=[SMEM, SMEM] + [VMEM] * 7,
        out_specs=VMEM,
        scratch_shapes=[
            pltpu.VMEM((heads, seq, dim), bf16),
            pltpu.VMEM((heads, seq, dim), bf16),
            pltpu.VMEM((heads, dim, seq), f32),
            pltpu.VMEM((heads, dim, seq), f32),
        ],
        cost_estimate=pl.CostEstimate(
            flops=20_000_000_000, bytes_accessed=8_000_000, transcendentals=6_000_000
        ),
        name="attend_back",
    )(lo, phys, start, qkv, mixed, dmixed, lse, cosine, sine)


def rotary_tables(length):
    half = ROT // 2
    freq = 10000.0 ** (-(jnp.arange(half, dtype=f32) * 2.0) / ROT)
    angle = freq[:, None] * jnp.arange(length, dtype=f32)[None, :]
    return jnp.cos(angle), jnp.sin(angle)


def standardize(value):
    average = jnp.mean(value, axis=-1, keepdims=True)
    centered = value - average
    var = jnp.mean(centered * centered, axis=-1, keepdims=True)
    inverse = lax.rsqrt(var + 1e-05)
    return centered * inverse, inverse


def body(dp, tp, tokens, segment_ids, cotangent, gain1, bias1, gain2, bias2,
         qkv_weight, qkv_bias, dense_weight, dense_bias, fc_in_weight, fc_in_bias,
         fc_out_weight, fc_out_bias):
    t = lax.axis_index("tensor")
    own = tokens[0]
    own_grad = cotangent[0]
    rows, width = own.shape
    seq = rows * tp
    count = seq // BLK
    heads = qkv_weight.shape[1] // (3 * HEAD_DIM)
    ids = segment_ids[0]
    g1, b1, g2, b2 = [v.astype(f32) for v in (gain1, bias1, gain2, bias2)]

    begins = jnp.sum(ids[None, :] < jnp.arange(SEGS, dtype=jnp.int32)[:, None], axis=1)
    start = jnp.sum(
        jnp.where(ids[None, :] == jnp.arange(SEGS, dtype=jnp.int32)[:, None], begins[:, None], 0),
        axis=0, keepdims=True,
    ).astype(jnp.int32)
    lo = start[0, ::BLK] // BLK
    per = rows // BLK
    block = jnp.arange(count, dtype=jnp.int32)
    phys = ((block // per) ^ t) * per + block % per
    cosine, sine = rotary_tables(seq)
    order = lambda table: jnp.concatenate(
        [lax.dynamic_slice_in_dim(table, (t ^ k) * rows, rows, 1) for k in range(tp)], axis=1
    )
    cos_here, sin_here = order(cosine), order(sine)

    x = jnp.concatenate(gather_relative(own, tp), axis=0).astype(f32)
    dy = jnp.concatenate(gather_relative(own_grad, tp), axis=0)
    xhat, inverse = standardize(x)
    h1 = (xhat * g1 + b1).astype(bf16)
    h2 = (xhat * g2 + b2).astype(bf16)

    pre = dot(h2, fc_in_weight) + fc_in_bias.astype(f32)
    act, pull = jax.vjp(partial(jax.nn.gelu, approximate=False), pre)
    act = act.astype(bf16)
    dpre = pull(dot_nt(dy, fc_out_weight))[0].astype(bf16)
    w2_grad = dot_tn(act, dy)
    w1_grad = dot_tn(h2, dpre)
    c1_grad = jnp.sum(dpre.astype(f32), axis=0)
    dh2 = dot_nt(dpre, fc_in_weight)
    ff_grads = sum_over_rows(jnp.concatenate([w1_grad, w2_grad], axis=0), dp)

    qkv = lax.dot_general(qkv_weight, h1, (((0,), (1,)), ((), ())), preferred_element_type=f32)
    qkv = (qkv + qkv_bias.astype(f32)[:, None]).reshape(heads, 3, HEAD_DIM, seq)
    half = ROT // 2
    one, two, rest = qkv[:, :2, :half], qkv[:, :2, half:ROT], qkv[:, :2, ROT:]
    turned = jnp.concatenate(
        [one * cos_here - two * sin_here, two * cos_here + one * sin_here, rest], axis=2
    )
    qkv = jnp.concatenate(
        [turned[:, :1] * HEAD_DIM ** (-0.5), turned[:, 1:], qkv[:, 2:]], axis=1
    ).astype(bf16)
    mixed, lse = attend(lo, phys, start, qkv)
    flat = mixed.reshape(heads * HEAD_DIM, seq)
    dense_grad = dot(flat, dy)
    partial_out = dot_tn(flat, dense_weight) + dot(act, fc_out_weight)
    summed = scatter_relative(
        {k: partial_out[k * rows : (k + 1) * rows] for k in range(tp)}, tp
    )
    result = (
        own.astype(f32) + summed + dense_bias.astype(f32) + fc_out_bias.astype(f32)
    ).astype(bf16)
    dmixed = dot_nt(dense_weight, dy).astype(bf16).reshape(heads, HEAD_DIM, seq)
    dqkv = attend_back(lo, phys, start, qkv, mixed, dmixed, lse, cosine, sine)
    dflat = dqkv.reshape(3 * heads * HEAD_DIM, seq)
    qkv_grad = dot(dflat, h1)
    qkv_b_grad = jnp.sum(dflat.astype(f32), axis=1)
    dh1 = lax.dot_general(dflat, qkv_weight, (((0,), (1,)), ((), ())), preferred_element_type=f32)

    both = dh1 * g1 + dh2 * g2
    summed_back = scatter_relative({k: both[k * rows : (k + 1) * rows] for k in range(tp)}, tp)

    vectors = jnp.stack(
        [
            jnp.sum(dh1 * xhat, axis=0),
            jnp.sum(dh1, axis=0),
            jnp.sum(dh2 * xhat, axis=0),
            jnp.sum(dh2, axis=0),
            jnp.sum(dy.astype(f32), axis=0),
            c1_grad,
            jnp.pad(qkv_b_grad, (0, width - qkv_b_grad.shape[0])),
            jnp.zeros((width,), f32),
        ]
    )
    high = vectors.astype(bf16)
    low = (vectors - high.astype(f32)).astype(bf16)
    packed = jnp.concatenate([high, low], axis=0)
    for bit in range(int(np.log2(dp))):
        packed2 = swap(packed, "dp", dp, 1 << bit).astype(f32)
        vectors = vectors + packed2[:8] + packed2[8:]
        high = vectors.astype(bf16)
        low = (vectors - high.astype(f32)).astype(bf16)
        packed = jnp.concatenate([high, low], axis=0)
    c1_grad, qkv_b_grad, out_bias_grad = vectors[5], vectors[6, : qkv_b_grad.shape[0]], vectors[4]
    norms = vectors[:4]
    bit = 1
    while bit < tp:
        norms = norms + swap(norms, "tensor", tp, bit)
        bit *= 2

    attn_grads = sum_over_rows(jnp.concatenate([qkv_grad, dense_grad], axis=0), dp)

    mine = xhat[:rows]
    term = inverse[:rows] * (
        summed_back
        - jnp.mean(summed_back, axis=-1, keepdims=True)
        - mine * jnp.mean(summed_back * mine, axis=-1, keepdims=True)
    )
    input_grad = own_grad.astype(f32) + term
    inner = fc_in_weight.shape[0]
    return (
        result[None],
        input_grad[None],
        norms[0],
        norms[1],
        norms[2],
        norms[3],
        attn_grads[: qkv_grad.shape[0]].astype(f32).T,
        qkv_b_grad,
        attn_grads[qkv_grad.shape[0] :].astype(f32),
        out_bias_grad,
        ff_grads[:inner].astype(f32),
        c1_grad,
        ff_grads[inner:].astype(f32),
        out_bias_grad,
    )


def solution(mesh):
    split = P("dp", "tensor", None)
    columns, stacked, vector = P(None, "tensor"), P("tensor", None), P("tensor")
    whole = P()
    return jax.shard_map(
        partial(body, mesh.shape["dp"], mesh.shape["tensor"]),
        mesh=mesh,
        in_specs=(
            split, P("dp", None), split, whole, whole, whole, whole, columns, vector, stacked,
            whole, columns, vector, stacked, whole,
        ),
        out_specs=(
            split, split, whole, whole, whole, whole, columns, vector, stacked, whole, columns,
            vector, stacked, whole,
        ),
        check_vma=False,
    )
```

```python
from functools import partial

import jax
import jax.numpy as jnp
import numpy as np
from jax import lax
from jax.experimental import pallas as pl
from jax.experimental.pallas import tpu as pltpu
from jax.sharding import PartitionSpec as P

HEAD_DIM = 64
ROT = 16
SEGS = 8
BLK = 256
NEG = -1e30
LOG2E = 1.4426950408889634
f32, bf16, i32 = jnp.float32, jnp.bfloat16, jnp.int32
VMEM = pl.BlockSpec(memory_space=pltpu.VMEM)
SMEM = pl.BlockSpec(memory_space=pltpu.SMEM)
MIB = 1 << 20


def dot(a, b):
    return jnp.dot(a, b, preferred_element_type=f32)


def dot_nt(a, b):
    return lax.dot_general(a, b, (((1,), (1,)), ((), ())), preferred_element_type=f32)


def dot_tn(a, b):
    return lax.dot_general(a, b, (((0,), (0,)), ((), ())), preferred_element_type=f32)


def like(shape, dtype):
    return jax.ShapeDtypeStruct(shape, dtype)


def call(kernel, name, inputs, outs, scratch=(), limit=8, flops=0, moved=1_000_000, smem=(), smem_out=()):
    return pl.pallas_call(
        kernel,
        out_shape=tuple(outs),
        in_specs=[SMEM if i in smem else VMEM for i in range(len(inputs))],
        out_specs=tuple(SMEM if i in smem_out else VMEM for i in range(len(outs))),
        scratch_shapes=list(scratch),
        compiler_params=pltpu.CompilerParams(vmem_limit_bytes=limit * MIB),
        cost_estimate=pl.CostEstimate(flops=flops, bytes_accessed=moved, transcendentals=0),
        name=name,
    )(*inputs)


def row_of(ref):
    return ref[...].astype(f32).reshape(1, -1)


def column_of(row):
    return jnp.broadcast_to(row, (128, row.shape[1])).T[:, 0:1]


def pair_rows(rows):
    rows = jnp.concatenate(rows, axis=0)
    high = rows.astype(bf16)
    return jnp.concatenate([high, (rows - high.astype(f32)).astype(bf16)], axis=0)


def segments_kernel(ids_ref, first_ref, start_ref, lo_ref):
    ids = ids_ref[...]
    start = jnp.zeros_like(ids)
    begins = []
    for s in range(SEGS):
        begin = jnp.sum(jnp.where(ids < s, 1.0, 0.0)).astype(i32)
        begins.append(begin)
        start = jnp.where(ids == s, begin, start)
    start_ref[...] = start
    for i in range(lo_ref.shape[0]):
        seg = first_ref[0, i * BLK]
        lo = begins[0]
        for s in range(1, SEGS):
            lo = jnp.where(seg == s, begins[s], lo)
        lo_ref[i] = lax.div(lo, BLK)


def front_kernel(
    place_ref, x0_ref, x1_ref, g1_ref, b1_ref, g2_ref, b2_ref, w1_ref, c1_ref, wq_ref, bq_ref,
    cos_ref, sin_ref, xh_ref, act_ref, slope_ref, qkv_ref, *, first,
):
    heads = qkv_ref.shape[0]
    half = ROT // 2
    rows = x0_ref.shape[0]
    g1, b1, g2, b2, c1 = [row_of(r) for r in (g1_ref, b1_ref, g2_ref, b2_ref, c1_ref)]
    for piece, x_ref in enumerate((x0_ref, x1_ref)):
        out = slice(piece * rows, (piece + 1) * rows)
        at = (place_ref[0] ^ (first + piece)) * rows
        here = pl.ds(pl.multiple_of(at, 128), rows)
        x = x_ref[...].astype(f32)
        c = x - jnp.mean(x, axis=1, keepdims=True)
        xh = c * lax.rsqrt(jnp.mean(c * c, axis=1, keepdims=True) + 1e-05)
        xh_ref[out, :] = xh.astype(bf16)
        h1 = (xh * g1 + b1).astype(bf16)
        h2 = (xh * g2 + b2).astype(bf16)
        pre = dot(h2, w1_ref[...]) + c1
        qkv = dot_nt(wq_ref[...], h1) + bq_ref[...]
        cosine, sine = cos_ref[:, here], sin_ref[:, here]
        for h in range(heads):
            for part in range(3):
                at = (3 * h + part) * HEAD_DIM
                v = qkv[at : at + HEAD_DIM]
                if part < 2:
                    one, two = v[:half], v[half:ROT]
                    v = jnp.concatenate(
                        [one * cosine - two * sine, two * cosine + one * sine, v[ROT:]], axis=0
                    )
                if part == 0:
                    v = v * HEAD_DIM ** (-0.5)
                qkv_ref[h, part, :, out] = v.astype(bf16)
        cdf = 0.5 + 0.5 * lax.erf(pre * 0.5**0.5)
        pdf = jnp.exp(pre * pre * -0.5) * (2.0 * np.pi) ** -0.5
        act_ref[out, :] = (pre * cdf).astype(bf16)
        slope_ref[out, :] = (cdf + pre * pdf).astype(bf16)


def halves(payload_ref, keep_ref, send_ref, side):
    rows = keep_ref.shape[0]
    keep_ref[...] = payload_ref[pl.ds(pl.multiple_of(side * rows, 16), rows), :]
    send_ref[...] = payload_ref[pl.ds(pl.multiple_of((1 - side) * rows, 16), rows), :]


def ff_back_kernel(*refs, last):
    place_ref, refs = refs[0], refs[1:]
    ins = refs[:9]
    dy0_ref, dy1_ref, act_ref, slope_ref, xh_ref, g2_ref, w1_ref, w2_ref, wd_ref = ins
    refs = refs[9:]
    if last:
        b2_ref, w1_in, w2_in, sums_in = refs[:4]
        refs = refs[4:]
        out_ref, back_ref, do_ref, k1_ref, s1_ref, k2_ref, s2_ref, sums_ref = refs[:8]
        w1g_ref, w2g_ref, pay_ref = refs[8:]
    else:
        out_ref, back_ref, do_ref, w1g_ref, w2g_ref, sums_ref = refs
    rows = dy0_ref.shape[0]
    g2 = row_of(g2_ref)
    sums = [sums_in[i : i + 1, :] for i in range(2)] if last else [0.0, 0.0]
    for piece, dy_ref in enumerate((dy0_ref, dy1_ref)):
        r = slice(piece * rows, (piece + 1) * rows)
        dy = dy_ref[...]
        act = act_ref[r, :]
        du = (dot_nt(dy, w2_ref[...]) * slope_ref[r, :].astype(f32)).astype(bf16)
        w2_part = dot_tn(act, dy)
        w1_part = dot_tn(xh_ref[r, :], du)
        if piece == 0:
            w2g_ref[...] = w2_in[...] + w2_part if last else w2_part
            w1g_ref[...] = w1_in[...] + w1_part if last else w1_part
        else:
            w2g_ref[...] += w2_part
            w1g_ref[...] += w1_part
        out_ref[r, :] = dot(act, w2_ref[...]).astype(bf16)
        back_ref[r, :] = (dot_nt(du, w1_ref[...]) * g2).astype(bf16)
        do_ref[:, r] = dot_nt(wd_ref[...], dy).astype(bf16)
        sums[0] = sums[0] + jnp.sum(du.astype(f32), axis=0, keepdims=True)
        sums[1] = sums[1] + jnp.sum(dy.astype(f32), axis=0, keepdims=True)
    sums_ref[0:1, :] = sums[0]
    sums_ref[1:2, :] = sums[1]
    if last:
        side = lax.rem(place_ref[1], 2)
        pay_ref[...] = w2g_ref[...].astype(bf16)
        halves(pay_ref, k2_ref, s2_ref, side)
        du_sum = jnp.broadcast_to(sums[0], (8, sums[0].shape[1]))
        high = du_sum.astype(bf16)
        low = (du_sum - high.astype(f32)).astype(bf16)
        sums_ref[3:4, :] = (dot_nt(high, w1_ref[...]) + dot_nt(low, w1_ref[...]))[0:1]
        raw = w1g_ref[...]
        gain = jnp.sum(raw * w1_ref[...].astype(f32), axis=1, keepdims=True)
        sums_ref[2:3, :] = jnp.broadcast_to(gain, (gain.shape[0], 128)).T[0:1, :]
        pay_ref[...] = (raw * column_of(g2) + column_of(row_of(b2_ref)) * sums[0]).astype(bf16)
        halves(pay_ref, k1_ref, s1_ref, side)


def blocks(place_ref, count, per):
    def phys(j):
        return pl.ds(
            pl.multiple_of(((lax.div(j, per) ^ place_ref[0]) * per + lax.rem(j, per)) * BLK, BLK),
            BLK,
        )

    return phys


def attend_kernel(
    place_ref, lo_ref, start_ref, left_ref, right_ref, outl_ref, outr_ref,
    dy0_ref, dy1_ref, dy2_ref, dy3_ref, wd_ref,
    qkv_ref, o_ref, lse_ref, keep0_ref, keep2_ref, send_ref, wdg_ref, kn_ref,
):
    heads, seq = qkv_ref.shape[0], qkv_ref.shape[3]
    count, rows = seq // BLK, keep0_ref.shape[0]
    phys = blocks(place_ref, count, rows // BLK)
    qkv_ref[:, :, :, : seq // 2] = left_ref[...]
    qkv_ref[:, :, :, seq // 2 :] = right_ref[...]
    for h in range(heads):
        for b in range(count):
            r = slice(b * BLK, (b + 1) * BLK)
            kn_ref[h, r, :] = qkv_ref[h, 1, :, r].T
    ik = lax.broadcasted_iota(i32, (BLK, BLK), 0)
    iq = lax.broadcasted_iota(i32, (BLK, BLK), 1)

    @pl.loop(0, count)
    def _(i):
        qs = phys(i)
        start = start_ref[0:1, pl.ds(pl.multiple_of(i * BLK, BLK), BLK)]

        def step(ks, mask, carry):
            scores = [
                jnp.where(mask, dot(kn_ref[h, ks, :], qkv_ref[h, 0, :, qs]), NEG)
                for h in range(heads)
            ]
            out = []
            for h in range(heads):
                top = jnp.max(scores[h], axis=0, keepdims=True)
                if carry is not None:
                    top = jnp.maximum(top, carry[h][0])
                expo = jnp.exp2(scores[h] * LOG2E - top * LOG2E)
                total = jnp.sum(expo, axis=0, keepdims=True)
                mixed = dot(qkv_ref[h, 2, :, ks], expo.astype(bf16))
                if carry is not None:
                    fade = jnp.exp2((carry[h][0] - top) * LOG2E)
                    total = total + carry[h][1] * fade
                    mixed = mixed + carry[h][2] * fade
                out.append((top, total, mixed))
            return tuple(out)

        carry = step(qs, (ik <= iq) & (ik >= start - i * BLK), None)
        carry = lax.fori_loop(
            lo_ref[i], i, lambda j, c: step(phys(j), ik >= start - j * BLK, c), carry
        )
        for h in range(heads):
            top, total, mixed = carry[h]
            at = slice(h * HEAD_DIM, (h + 1) * HEAD_DIM)
            o_ref[at, qs] = (mixed * (1.0 / total)).astype(bf16)
            lse_ref[h, 0:1, qs] = top * LOG2E + jnp.log2(total)

    dys = (dy0_ref, dy1_ref, dy2_ref, dy3_ref)
    wdg = None
    for k in range(4):
        r = slice(k * rows, (k + 1) * rows)
        o = o_ref[:, r]
        side = outl_ref if k < 2 else outr_ref
        at = slice((k % 2) * rows, (k % 2 + 1) * rows)
        total = side[at, :].astype(f32) + dot_tn(o, wd_ref[...])
        if k == 0:
            keep0_ref[...] = total
        elif k == 2:
            keep2_ref[...] = total
        else:
            send_ref[(k // 2) * rows : (k // 2 + 1) * rows, :] = total.astype(bf16)
        part = dot(o, dys[k][...])
        wdg = part if k == 0 else wdg + part
    wdg_ref[...] = wdg.astype(bf16)


def attend_back_kernel(
    place_ref, lo_ref, start_ref, qkv_ref, o_ref, dol_ref, dor_ref, lse_ref, cos_ref, sin_ref,
    xhl_ref, xhr_ref, wq_ref, g1_ref, b1_ref, wdg_ref, sums_ref,
    dqkv_ref, keep_ref, send_ref, do_ref, kn_ref, vn_ref, dk_ref, dv_ref, pay_ref,
):
    heads, seq = qkv_ref.shape[0], qkv_ref.shape[3]
    count = seq // BLK
    phys = blocks(place_ref, count, count // 4)
    half = ROT // 2
    do_ref[:, : seq // 2] = dol_ref[...]
    do_ref[:, seq // 2 :] = dor_ref[...]
    for h in range(heads):
        for b in range(count):
            r = slice(b * BLK, (b + 1) * BLK)
            kn_ref[h, r, :] = qkv_ref[h, 1, :, r].T
            vn_ref[h, r, :] = qkv_ref[h, 2, :, r].T
    dk_ref[...] = jnp.zeros_like(dk_ref)
    dv_ref[...] = jnp.zeros_like(dv_ref)
    ik = lax.broadcasted_iota(i32, (BLK, BLK), 0)
    iq = lax.broadcasted_iota(i32, (BLK, BLK), 1)

    def unrotate(grad, cosine, sine):
        one, two = grad[:half], grad[half:ROT]
        return jnp.concatenate(
            [one * cosine + two * sine, two * cosine - one * sine, grad[ROT:]], axis=0
        )

    @pl.loop(0, count)
    def _(i):
        qs = phys(i)
        here = pl.ds(pl.multiple_of(i * BLK, BLK), BLK)
        start = start_ref[0:1, here]
        dos = [do_ref[h * HEAD_DIM : (h + 1) * HEAD_DIM, qs] for h in range(heads)]
        delta = [
            jnp.sum(
                dos[h].astype(f32) * o_ref[h * HEAD_DIM : (h + 1) * HEAD_DIM, qs].astype(f32),
                axis=0, keepdims=True,
            )
            for h in range(heads)
        ]
        lse = [lse_ref[h, 0:1, qs] for h in range(heads)]

        def step(ks, mask, carry):
            scores = [
                jnp.where(mask, dot(kn_ref[h, ks, :], qkv_ref[h, 0, :, qs]), NEG)
                for h in range(heads)
            ]
            dprobs = [dot(vn_ref[h, ks, :], dos[h]) for h in range(heads)]
            probs = [jnp.exp2(scores[h] * LOG2E - lse[h]) for h in range(heads)]
            dscores = [(probs[h] * (dprobs[h] - delta[h])).astype(bf16) for h in range(heads)]
            out = []
            for h in range(heads):
                dv_ref[h, :, ks] += dot_nt(dos[h], probs[h].astype(bf16))
                dk_ref[h, :, ks] += dot_nt(qkv_ref[h, 0, :, qs], dscores[h])
                dq = dot(qkv_ref[h, 1, :, ks], dscores[h])
                out.append(dq if carry is None else carry[h] + dq)
            return tuple(out)

        carry = step(qs, (ik <= iq) & (ik >= start - i * BLK), None)
        carry = lax.fori_loop(
            lo_ref[i], i, lambda j, c: step(phys(j), ik >= start - j * BLK, c), carry
        )
        for h in range(heads):
            dq = unrotate(carry[h] * HEAD_DIM ** (-0.5), cos_ref[:, here], sin_ref[:, here])
            dqkv_ref[h, 0, :, qs] = dq.astype(bf16)

    @pl.loop(0, count)
    def _(i):
        qs = phys(i)
        here = pl.ds(pl.multiple_of(i * BLK, BLK), BLK)
        for h in range(heads):
            dk = unrotate(dk_ref[h, :, qs], cos_ref[:, here], sin_ref[:, here])
            dqkv_ref[h, 1, :, qs] = dk.astype(bf16)
            dqkv_ref[h, 2, :, qs] = dv_ref[h, :, qs].astype(bf16)

    g1, b1 = row_of(g1_ref), row_of(b1_ref)
    cols = 3 * HEAD_DIM
    gain, bias, bq = 0.0, 0.0, []
    for h in range(heads):
        grad = dqkv_ref[h].reshape(cols, seq)
        raw = dot(grad[:, : seq // 2], xhl_ref[...]) + dot(grad[:, seq // 2 :], xhr_ref[...])
        total = jnp.sum(grad.astype(f32), axis=1, keepdims=True)
        bq.append(jnp.broadcast_to(total, (cols, 128)).T[0:1, :])
        pay_ref[h * cols : (h + 1) * cols, :] = (raw * g1 + total * b1).astype(bf16)
        weight = wq_ref[h * cols : (h + 1) * cols, :].astype(f32)
        gain = gain + jnp.sum(weight * raw, axis=0, keepdims=True)
        bias = bias + jnp.sum(weight * total, axis=0, keepdims=True)
    pay_ref[heads * cols :, :] = wdg_ref[...]
    width = pay_ref.shape[1]
    zeros = jnp.zeros((1, width - heads * cols), f32)
    vectors = pair_rows(
        [
            gain, bias, sums_ref[2:3, :], sums_ref[3:4, :], sums_ref[1:2, :], sums_ref[0:1, :],
            jnp.concatenate(bq + [zeros], axis=1), jnp.zeros((1, width), f32),
        ]
    )
    side = lax.rem(place_ref[1], 2)
    rows = pay_ref.shape[0] // 2
    halves(pay_ref, keep_ref.at[0:rows], send_ref.at[0:rows], side)
    keep_ref[rows:, :] = vectors
    send_ref[rows:, :] = vectors


def tokens_back_kernel(
    dqkv_ref, backl_ref, backr_ref, wq_ref, g1_ref, keep0_ref, keep2_ref, send_ref
):
    rows = keep0_ref.shape[0]
    g1 = row_of(g1_ref)
    cols, seq = wq_ref.shape[0], dqkv_ref.shape[3]
    for k in range(4):
        grad = dqkv_ref[:, :, :, k * rows : (k + 1) * rows].reshape(cols, rows)
        side = backl_ref if k < 2 else backr_ref
        at = slice((k % 2) * rows, (k % 2 + 1) * rows)
        total = side[at, :].astype(f32) + dot_tn(grad, wq_ref[...]) * g1
        if k == 0:
            keep0_ref[...] = total
        elif k == 2:
            keep2_ref[...] = total
        else:
            send_ref[(k // 2) * rows : (k // 2 + 1) * rows, :] = total.astype(bf16)


def forward_kernel(keep2_ref, got_ref, sent_ref):
    rows = keep2_ref.shape[0]
    sent_ref[...] = (keep2_ref[...] + got_ref[rows:, :].astype(f32)).astype(bf16)


def result_kernel(x_ref, keep0_ref, got_ref, far_ref, bd_ref, c2_ref, out_ref):
    rows = x_ref.shape[0]
    summed = keep0_ref[...] + got_ref[:rows, :].astype(f32) + far_ref[...].astype(f32)
    out_ref[...] = (x_ref[...].astype(f32) + summed + (row_of(bd_ref) + row_of(c2_ref))).astype(bf16)


def tokens_grad_kernel(x_ref, dy_ref, keep0_ref, got_ref, far_ref, out_ref):
    rows = x_ref.shape[0]
    grad = keep0_ref[...] + got_ref[:rows, :].astype(f32) + far_ref[...].astype(f32)
    x = x_ref[...].astype(f32)
    c = x - jnp.mean(x, axis=1, keepdims=True)
    inverse = lax.rsqrt(jnp.mean(c * c, axis=1, keepdims=True) + 1e-05)
    xh = c * inverse
    term = grad - jnp.mean(grad, axis=1, keepdims=True)
    term = term - xh * jnp.mean(grad * xh, axis=1, keepdims=True)
    out_ref[...] = dy_ref[...].astype(f32) + inverse * term


def swap(value, axis, size, distance):
    return lax.ppermute(value, axis, [(i, i ^ distance) for i in range(size)])


def shifted(value, size, stride, factor, shift):
    pairs = []
    for i in range(size):
        digit = (i // stride) % factor
        pairs.append((i, i + ((digit + shift) % factor - digit) * stride))
    return lax.ppermute(value, "dp", pairs)


def unpair(rows):
    return rows[0:8, :].astype(f32) + rows[8:16, :].astype(f32)


def split_kernel(place_ref, keep_ref, got_ref, *out_refs, stride, tail):
    factor = len(out_refs)
    digit = lax.rem(lax.div(place_ref[1], stride), factor)
    rows = (keep_ref.shape[0] - tail) // factor
    for s in range(factor):
        at = pl.ds(pl.multiple_of(lax.rem(digit + s, factor) * rows, 8), rows)
        out_refs[s][0:rows, :] = (keep_ref[at, :].astype(f32) + got_ref[at, :].astype(f32)).astype(bf16)
        if tail:
            total = unpair(keep_ref[factor * rows :, :]) + unpair(got_ref[factor * rows :, :])
            out_refs[s][rows:, :] = pair_rows([total])


def total_kernel(*refs, tail):
    ins = refs[:-2] if tail else refs[:-1]
    out_ref = refs[len(ins)]
    rows = out_ref.shape[0]
    total = ins[0][0:rows, :].astype(f32)
    for r in ins[1:]:
        total = total + r[0:rows, :].astype(f32)
    out_ref[...] = total.astype(bf16)
    if tail:
        vectors = unpair(ins[0][rows:, :])
        for r in ins[1:]:
            vectors = vectors + unpair(r[rows:, :])
        refs[-1][...] = vectors


def place_kernel(place_ref, mine_ref, got_ref, *out_refs, stride, factor):
    digit = lax.rem(lax.div(place_ref[1], stride), factor)
    side = lax.rem(place_ref[1], 2)
    rows = mine_ref.shape[0] // factor
    out_ref = out_refs[-1]
    for s in range(factor):
        chunk = lax.rem(digit + factor - s, factor)
        for part, ref in ((side, mine_ref), (1 - side, got_ref)):
            at = pl.ds(pl.multiple_of((part * factor + chunk) * rows, 8), rows)
            out_ref[at, :] = ref[s * rows : (s + 1) * rows, :].astype(f32)
    if len(out_refs) > 1:
        split = out_refs[0].shape[0]
        out_refs[0][...] = out_ref[:split, :]
        out_refs[1][...] = out_ref[split:, :]


def reduce_pieces(place, keep, got, dp, tail):
    stride, factor = 2, 4
    rows = (keep.shape[0] - tail) // factor
    width = keep.shape[1]
    pieces = call(
        partial(split_kernel, stride=stride, tail=tail), "split", [place, keep, got],
        [like((rows + tail, width), bf16)] * factor, smem=(0,),
    )
    parts = [pieces[0]] + [
        shifted(pieces[s], dp, stride, factor, s) for s in range(1, factor)
    ]
    outs = [like((rows, width), bf16)] + ([like((8, width), f32)] if tail else [])
    return call(partial(total_kernel, tail=tail), "total", parts, outs)


def spread_pieces(total, dp):
    stride, factor = 2, 4
    pieces = [total] + [shifted(total, dp, stride, factor, s) for s in range(1, factor)]
    return jnp.concatenate(pieces, axis=0)


def settle(place, mine, got, outs, limit=8):
    scratch = [pltpu.VMEM((2 * mine.shape[0], mine.shape[1]), f32)] if len(outs) > 1 else []
    return call(
        partial(place_kernel, stride=2, factor=4), "place", [place, mine, got], outs, scratch,
        smem=(0,), limit=limit,
    )


def rest_sum(value, dp):
    if dp == 8:
        return value
    groups = [[i + 8 * j for j in range(dp // 8)] for i in range(8)]
    return lax.psum(value, "dp", axis_index_groups=groups)


def rotary_tables(length):
    half = ROT // 2
    freq = np.float32(10000.0) ** (-(np.arange(half, dtype=np.float32) * 2.0) / ROT)
    angle = freq.astype(np.float32)[:, None] * np.arange(length, dtype=np.float32)[None, :]
    return np.cos(angle).astype(np.float32), np.sin(angle).astype(np.float32)


def body(dp, tp, tokens, segment_ids, cotangent, gain1, bias1, gain2, bias2,
         qkv_weight, qkv_bias, dense_weight, dense_bias, fc_in_weight, fc_in_bias,
         fc_out_weight, fc_out_bias):
    assert tp == 4 and dp % 8 == 0
    x0, dy0 = tokens[0], cotangent[0]
    rows, width = x0.shape
    seq = rows * tp
    count = seq // BLK
    wq = qkv_weight.T
    heads = wq.shape[0] // (3 * HEAD_DIM)
    cosine, sine = rotary_tables(seq)
    place = jnp.stack([lax.axis_index("tensor"), lax.axis_index("dp")]).astype(i32)

    x1 = swap(x0, "tensor", tp, 1)
    x2 = swap(x0, "tensor", tp, 2)
    dy1 = swap(dy0, "tensor", tp, 1)
    dy2 = swap(dy0, "tensor", tp, 2)
    x3 = swap(x2, "tensor", tp, 1)
    dy3 = swap(dy2, "tensor", tp, 1)

    start, lo = call(
        segments_kernel, "segments", [segment_ids, segment_ids],
        [like((1, seq), i32), like((count,), i32)], smem=(1,), smem_out=(1,),
    )
    bq_column = qkv_bias.astype(f32)[:, None]
    pair = 2 * rows
    hidden = fc_in_weight.shape[1]

    def front(xa, xb, first):
        return call(
            partial(front_kernel, first=first), "front",
            [place, xa, xb, gain1, bias1, gain2, bias2, fc_in_weight, fc_in_bias, wq, bq_column,
             cosine, sine],
            [like((pair, width), bf16), like((pair, hidden), bf16), like((pair, hidden), bf16),
             like((heads, 3, HEAD_DIM, pair), bf16)],
            smem=(0,), limit=16, flops=2 * pair * width * (hidden + wq.shape[0]),
        )

    def ff_back(da, db, act, slope, xh, carry):
        inner = dense_weight.shape[0]
        outs = [like((pair, width), bf16), like((pair, width), bf16), like((inner, pair), bf16)]
        full = [like((width, hidden), f32), like((hidden, width), f32)]
        sums = like((8, width), f32)
        half = [like((width // 2, hidden), bf16)] * 2 + [like((hidden // 2, width), bf16)] * 2
        inputs = [place, da, db, act, slope, xh, gain2, fc_in_weight, fc_out_weight, dense_weight]
        scratch = []
        if carry is None:
            outs = outs + full + [sums]
        else:
            inputs = inputs + [bias2] + list(carry)
            outs = outs + half + [sums]
            scratch = [
                pltpu.VMEM((width, hidden), f32), pltpu.VMEM((hidden, width), f32),
                pltpu.VMEM((width, hidden), bf16),
            ]
        return call(
            partial(ff_back_kernel, last=carry is not None), "ff_back", inputs, outs, scratch,
            smem=(0,), limit=22, flops=2 * pair * width * (5 * hidden + inner),
        )

    xh_l, act_l, slope_l, qkv_l = front(x0, x1, 0)
    out_l, back_l, do_l, w1_part, w2_part, sums_l = ff_back(dy0, dy1, act_l, slope_l, xh_l, None)
    xh_r, act_r, slope_r, qkv_r = front(x2, x3, 2)
    out_r, back_r, do_r, k1, s1, k2, s2, sums = ff_back(
        dy2, dy3, act_r, slope_r, xh_r, (w1_part, w2_part, sums_l)
    )
    inner = heads * HEAD_DIM
    qkv, mixed, lse, keep0, keep2, send, dense_grad = call(
        attend_kernel, "attend",
        [place, lo, start, qkv_l, qkv_r, out_l, out_r, dy0, dy1, dy2, dy3, dense_weight],
        [like((heads, 3, HEAD_DIM, seq), bf16), like((inner, seq), bf16), like((heads, 1, seq), f32),
         like((rows, width), f32), like((rows, width), f32), like((pair, width), bf16),
         like((inner, width), bf16)],
        [pltpu.VMEM((heads, seq, HEAD_DIM), bf16)],
        smem=(0, 1), limit=12, flops=15_000_000_000,
    )
    got = swap(send, "tensor", tp, 1)
    far = swap(call(forward_kernel, "forward", [keep2, got], [like((rows, width), bf16)])[0],
               "tensor", tp, 2)
    result = call(
        result_kernel, "result", [x0, keep0, got, far, dense_bias, fc_out_bias],
        [like((rows, width), bf16)],
    )[0]

    vectors_rows = 16
    dqkv, keep_c, send_c = call(
        attend_back_kernel, "attend_back",
        [place, lo, start, qkv, mixed, do_l, do_r, lse, cosine, sine, xh_l, xh_r, wq, gain1, bias1,
         dense_grad, sums],
        [like((heads, 3, HEAD_DIM, seq), bf16)]
        + [like((width // 2 + vectors_rows, width), bf16)] * 2,
        [
            pltpu.VMEM((inner, seq), bf16),
            pltpu.VMEM((heads, seq, HEAD_DIM), bf16), pltpu.VMEM((heads, seq, HEAD_DIM), bf16),
            pltpu.VMEM((heads, HEAD_DIM, seq), f32), pltpu.VMEM((heads, HEAD_DIM, seq), f32),
            pltpu.VMEM((wq.shape[0] + inner, width), bf16),
        ],
        smem=(0, 1), limit=20, flops=22_000_000_000,
    )
    keep0b, keep2b, sendb = call(
        tokens_back_kernel, "tokens_back", [dqkv, back_l, back_r, wq, gain1],
        [like((rows, width), f32), like((rows, width), f32), like((pair, width), bf16)],
        limit=8, flops=2 * seq * width * wq.shape[0],
    )
    gotb = swap(sendb, "tensor", tp, 1)
    farb = swap(call(forward_kernel, "forward", [keep2b, gotb], [like((rows, width), bf16)])[0],
                "tensor", tp, 2)
    input_grad = call(
        tokens_grad_kernel, "tokens_grad", [x0, dy0, keep0b, gotb, farb],
        [like((rows, width), f32)],
    )[0]

    def all_sum(keep, send, tail=0):
        got = swap(send, "dp", dp, 1)
        total = reduce_pieces(place, keep, got, dp, tail)
        vectors = rest_sum(total[1], dp) if tail else None
        mine = spread_pieces(rest_sum(total[0].astype(f32), dp).astype(bf16) if dp > 8 else total[0], dp)
        return mine, swap(mine, "dp", dp, 1), vectors

    mine2, other2, _ = all_sum(k2, s2)
    mine1, other1, _ = all_sum(k1, s1)
    mine_c, other_c, vectors = all_sum(keep_c, send_c, vectors_rows)
    w2_grad = settle(place, mine2, other2, [like((hidden, width), f32)])[0]
    w1_grad = settle(place, mine1, other1, [like((width, hidden), f32)])[0]
    wq_grad, wd_grad = settle(
        place, mine_c, other_c, [like((wq.shape[0], width), f32), like((inner, width), f32)]
    )
    near = vectors + swap(vectors, "tensor", tp, 1)
    near = near + swap(near, "tensor", tp, 2)
    return (
        result[None], input_grad[None], near[0], near[1], near[2], near[3],
        wq_grad.T, vectors[6, : wq.shape[0]], wd_grad, vectors[4],
        w1_grad, vectors[5], w2_grad, vectors[4],
    )


def solution(mesh):
    split = P("dp", "tensor", None)
    columns, stacked, vector = P(None, "tensor"), P("tensor", None), P("tensor")
    whole = P()
    return jax.shard_map(
        partial(body, mesh.shape["dp"], mesh.shape["tensor"]),
        mesh=mesh,
        in_specs=(
            split, P("dp", None), split, whole, whole, whole, whole, columns, vector, stacked,
            whole, columns, vector, stacked, whole,
        ),
        out_specs=(
            split, split, whole, whole, whole, whole, columns, vector, stacked, whole, columns,
            vector, stacked, whole,
        ),
        check_vma=False,
    )
```

```python
from functools import partial

import jax
import jax.numpy as jnp
import numpy as np
from jax import lax
from jax.experimental import pallas as pl
from jax.experimental.pallas import tpu as pltpu
from jax.sharding import PartitionSpec as P

HEAD_DIM = 64
ROT = 16
SEGS = 8
BLK = 256
NEG = -1e30
LOG2E = 1.4426950408889634
f32, bf16, i32 = jnp.float32, jnp.bfloat16, jnp.int32
VMEM = pl.BlockSpec(memory_space=pltpu.VMEM)
SMEM = pl.BlockSpec(memory_space=pltpu.SMEM)
MIB = 1 << 20
UNIT = 500_000_000
ORDER_A, ORDER_B = (0, 1, 2), (1, 0, 2)


def dot(a, b):
    return jnp.dot(a, b, preferred_element_type=f32)


def dot_nt(a, b):
    return lax.dot_general(a, b, (((1,), (1,)), ((), ())), preferred_element_type=f32)


def dot_tn(a, b):
    return lax.dot_general(a, b, (((0,), (0,)), ((), ())), preferred_element_type=f32)


def like(shape, dtype):
    return jax.ShapeDtypeStruct(shape, dtype)


def call(kernel, name, inputs, outs, scratch=(), limit=8, smem=(), smem_out=(), flops=1000):
    return pl.pallas_call(
        kernel,
        out_shape=tuple(outs),
        in_specs=[SMEM if i in smem else VMEM for i in range(len(inputs))],
        out_specs=tuple(SMEM if i in smem_out else VMEM for i in range(len(outs))),
        scratch_shapes=list(scratch),
        compiler_params=pltpu.CompilerParams(vmem_limit_bytes=limit * MIB),
        cost_estimate=pl.CostEstimate(flops=flops, bytes_accessed=1000, transcendentals=0),
        name=name,
    )(*inputs)


def after(token, *values):
    return lax.optimization_barrier((token, *values))[1:]


def row_of(ref):
    return ref[...].astype(f32).reshape(1, -1)


def column_of(row):
    return jnp.broadcast_to(row, (128, row.shape[1])).T[:, 0:1]


def pair_rows(rows):
    rows = jnp.concatenate(rows, axis=0)
    high = rows.astype(bf16)
    return jnp.concatenate([high, (rows - high.astype(f32)).astype(bf16)], axis=0)


def segments_kernel(ids_ref, first_ref, start_ref, lo_ref):
    ids = ids_ref[...]
    start = jnp.zeros_like(ids)
    begins = []
    for s in range(SEGS):
        begin = jnp.sum(jnp.where(ids < s, 1.0, 0.0)).astype(i32)
        begins.append(begin)
        start = jnp.where(ids == s, begin, start)
    start_ref[...] = start
    for i in range(lo_ref.shape[0]):
        seg = first_ref[0, i * BLK]
        lo = begins[0]
        for s in range(1, SEGS):
            lo = jnp.where(seg == s, begins[s], lo)
        lo_ref[i] = lax.div(lo, BLK)


def front_kernel(place_ref, *refs, first, pieces):
    x_refs, refs = refs[:pieces], refs[pieces:]
    g1_ref, b1_ref, g2_ref, b2_ref, w1_ref, c1_ref, wq_ref, bq_ref, cos_ref, sin_ref = refs[:10]
    xh_ref, act_ref, slope_ref, qkv_ref = refs[10:]
    heads = qkv_ref.shape[0]
    half = ROT // 2
    rows = x_refs[0].shape[0]
    g1, b1, g2, b2, c1 = [row_of(r) for r in (g1_ref, b1_ref, g2_ref, b2_ref, c1_ref)]
    for piece, x_ref in enumerate(x_refs):
        out = slice(piece * rows, (piece + 1) * rows)
        at = (place_ref[0] ^ (first + piece)) * rows
        here = pl.ds(pl.multiple_of(at, 128), rows)
        x = x_ref[...].astype(f32)
        c = x - jnp.mean(x, axis=1, keepdims=True)
        xh = c * lax.rsqrt(jnp.mean(c * c, axis=1, keepdims=True) + 1e-05)
        xh_ref[out, :] = xh.astype(bf16)
        h1 = (xh * g1 + b1).astype(bf16)
        h2 = (xh * g2 + b2).astype(bf16)
        pre = dot(h2, w1_ref[...]) + c1
        qkv = dot_nt(wq_ref[...], h1) + bq_ref[...]
        cosine, sine = cos_ref[:, here], sin_ref[:, here]
        for h in range(heads):
            for part in range(3):
                at = (3 * h + part) * HEAD_DIM
                v = qkv[at : at + HEAD_DIM]
                if part < 2:
                    one, two = v[:half], v[half:ROT]
                    v = jnp.concatenate(
                        [one * cosine - two * sine, two * cosine + one * sine, v[ROT:]], axis=0
                    )
                if part == 0:
                    v = v * HEAD_DIM ** (-0.5)
                qkv_ref[h, part, :, out] = v.astype(bf16)
        cdf = 0.5 + 0.5 * lax.erf(pre * 0.5**0.5)
        pdf = jnp.exp(pre * pre * -0.5) * (2.0 * np.pi) ** -0.5
        act_ref[out, :] = (pre * cdf).astype(bf16)
        slope_ref[out, :] = (cdf + pre * pdf).astype(bf16)


def halves(payload_ref, keep_ref, send_ref, side):
    rows = keep_ref.shape[0]
    keep_ref[...] = payload_ref[pl.ds(pl.multiple_of(side * rows, 16), rows), :]
    send_ref[...] = payload_ref[pl.ds(pl.multiple_of((1 - side) * rows, 16), rows), :]


def bit_of(place_ref, bit):
    return lax.rem(lax.div(place_ref[1], 1 << bit), 2)


def ff_back_kernel(place_ref, *refs, pieces, carried, last):
    dy_refs, refs = refs[:pieces], refs[pieces:]
    act_ref, slope_ref, xh_ref, g2_ref, b2_ref, w1_ref, w2_ref, wd_ref = refs[:8]
    refs = refs[8:]
    if carried:
        w1_in, w2_in, sums_in = refs[:3]
        refs = refs[3:]
    if last:
        out_ref, back_ref, do_ref, k1_ref, s1_ref, k2_ref, s2_ref, sums_ref = refs[:8]
        w1g_ref, w2g_ref, pay_ref = refs[8:]
    else:
        out_ref, back_ref, do_ref, w1g_ref, w2g_ref, sums_ref = refs
    rows = dy_refs[0].shape[0]
    g2 = row_of(g2_ref)
    sums = [sums_in[i : i + 1, :] for i in range(2)] if carried else [0.0, 0.0]
    for piece, dy_ref in enumerate(dy_refs):
        r = slice(piece * rows, (piece + 1) * rows)
        dy = dy_ref[...]
        act = act_ref[r, :]
        du = (dot_nt(dy, w2_ref[...]) * slope_ref[r, :].astype(f32)).astype(bf16)
        w2_part = dot_tn(act, dy)
        w1_part = dot_tn(xh_ref[r, :], du)
        if piece == 0:
            w2g_ref[...] = w2_in[...] + w2_part if carried else w2_part
            w1g_ref[...] = w1_in[...] + w1_part if carried else w1_part
        else:
            w2g_ref[...] += w2_part
            w1g_ref[...] += w1_part
        out_ref[r, :] = dot(act, w2_ref[...]).astype(bf16)
        back_ref[r, :] = (dot_nt(du, w1_ref[...]) * g2).astype(bf16)
        do_ref[:, r] = dot_nt(wd_ref[...], dy).astype(bf16)
        sums[0] = sums[0] + jnp.sum(du.astype(f32), axis=0, keepdims=True)
        sums[1] = sums[1] + jnp.sum(dy.astype(f32), axis=0, keepdims=True)
    sums_ref[0:1, :] = sums[0]
    sums_ref[1:2, :] = sums[1]
    if last:
        pay_ref[...] = w2g_ref[...].astype(bf16)
        halves(pay_ref, k2_ref, s2_ref, bit_of(place_ref, ORDER_A[0]))
        du_sum = jnp.broadcast_to(sums[0], (8, sums[0].shape[1]))
        high = du_sum.astype(bf16)
        low = (du_sum - high.astype(f32)).astype(bf16)
        sums_ref[3:4, :] = (dot_nt(high, w1_ref[...]) + dot_nt(low, w1_ref[...]))[0:1]
        raw = w1g_ref[...]
        gain = jnp.sum(raw * w1_ref[...].astype(f32), axis=1, keepdims=True)
        sums_ref[2:3, :] = jnp.broadcast_to(gain, (gain.shape[0], 128)).T[0:1, :]
        pay_ref[...] = (raw * column_of(g2) + column_of(row_of(b2_ref)) * sums[0]).astype(bf16)
        halves(pay_ref, k1_ref, s1_ref, bit_of(place_ref, ORDER_B[0]))


def blocks(place_ref, count, per):
    def phys(j):
        return pl.ds(
            pl.multiple_of(((lax.div(j, per) ^ place_ref[0]) * per + lax.rem(j, per)) * BLK, BLK),
            BLK,
        )

    return phys


def spans(refs, axis):
    at = 0
    for ref in refs:
        size = ref.shape[axis]
        yield slice(at, at + size), ref
        at += size


def attend_kernel(
    place_ref, lo_ref, start_ref, part0_ref, part1_ref, part2_ref,
    qkv_ref, o_ref, lse_ref, kn_ref,
):
    heads, seq = qkv_ref.shape[0], qkv_ref.shape[3]
    count = seq // BLK
    phys = blocks(place_ref, count, count // 4)
    for at, ref in spans((part0_ref, part1_ref, part2_ref), 3):
        qkv_ref[:, :, :, at] = ref[...]
    for h in range(heads):
        for b in range(count):
            r = slice(b * BLK, (b + 1) * BLK)
            kn_ref[h, r, :] = qkv_ref[h, 1, :, r].T
    ik = lax.broadcasted_iota(i32, (BLK, BLK), 0)
    iq = lax.broadcasted_iota(i32, (BLK, BLK), 1)

    @pl.loop(0, count)
    def _(i):
        qs = phys(i)
        start = start_ref[0:1, pl.ds(pl.multiple_of(i * BLK, BLK), BLK)]

        def step(ks, mask, carry):
            scores = [
                jnp.where(mask, dot(kn_ref[h, ks, :], qkv_ref[h, 0, :, qs]), NEG)
                for h in range(heads)
            ]
            out = []
            for h in range(heads):
                top = jnp.max(scores[h], axis=0, keepdims=True)
                if carry is not None:
                    top = jnp.maximum(top, carry[h][0])
                expo = jnp.exp2(scores[h] * LOG2E - top * LOG2E)
                total = jnp.sum(expo, axis=0, keepdims=True)
                mixed = dot(qkv_ref[h, 2, :, ks], expo.astype(bf16))
                if carry is not None:
                    fade = jnp.exp2((carry[h][0] - top) * LOG2E)
                    total = total + carry[h][1] * fade
                    mixed = mixed + carry[h][2] * fade
                out.append((top, total, mixed))
            return tuple(out)

        carry = step(qs, (ik <= iq) & (ik >= start - i * BLK), None)
        carry = lax.fori_loop(
            lo_ref[i], i, lambda j, c: step(phys(j), ik >= start - j * BLK, c), carry
        )
        for h in range(heads):
            top, total, mixed = carry[h]
            at = slice(h * HEAD_DIM, (h + 1) * HEAD_DIM)
            o_ref[at, qs] = (mixed * (1.0 / total)).astype(bf16)
            lse_ref[h, 0:1, qs] = top * LOG2E + jnp.log2(total)


def chunk(refs, k, rows):
    for at, ref in spans(refs, 0):
        if at.start <= k * rows < at.stop:
            return ref[k * rows - at.start : (k + 1) * rows - at.start, :]


def deal(k, total, keep0_ref, keep2_ref, send_ref):
    rows = keep0_ref.shape[0]
    if k == 0:
        keep0_ref[...] = total
    elif k == 2:
        keep2_ref[...] = total
    else:
        send_ref[(k // 2) * rows : (k // 2 + 1) * rows, :] = total.astype(bf16)


def attend_end_kernel(
    o_ref, dy0_ref, dy1_ref, dy2_ref, dy3_ref, wd_ref, out0_ref, out1_ref, out2_ref,
    keep0_ref, keep2_ref, send_ref, wdg_ref,
):
    rows = keep0_ref.shape[0]
    wdg = None
    for k, dy_ref in enumerate((dy0_ref, dy1_ref, dy2_ref, dy3_ref)):
        o = o_ref[:, k * rows : (k + 1) * rows]
        out = chunk((out0_ref, out1_ref, out2_ref), k, rows).astype(f32)
        deal(k, out + dot_tn(o, wd_ref[...]), keep0_ref, keep2_ref, send_ref)
        part = dot(o, dy_ref[...])
        wdg = part if k == 0 else wdg + part
    wdg_ref[...] = wdg.astype(bf16)


def attend_back_kernel(
    place_ref, lo_ref, start_ref, qkv_ref, o_ref, do0_ref, do1_ref, do2_ref, lse_ref, cos_ref,
    sin_ref, dqkv_ref, do_ref, kn_ref, vn_ref, dk_ref, dv_ref,
):
    heads, seq = qkv_ref.shape[0], qkv_ref.shape[3]
    count = seq // BLK
    phys = blocks(place_ref, count, count // 4)
    half = ROT // 2
    for at, ref in spans((do0_ref, do1_ref, do2_ref), 1):
        do_ref[:, at] = ref[...]
    for h in range(heads):
        for b in range(count):
            r = slice(b * BLK, (b + 1) * BLK)
            kn_ref[h, r, :] = qkv_ref[h, 1, :, r].T
            vn_ref[h, r, :] = qkv_ref[h, 2, :, r].T
    dk_ref[...] = jnp.zeros_like(dk_ref)
    dv_ref[...] = jnp.zeros_like(dv_ref)
    ik = lax.broadcasted_iota(i32, (BLK, BLK), 0)
    iq = lax.broadcasted_iota(i32, (BLK, BLK), 1)

    def unrotate(grad, cosine, sine):
        one, two = grad[:half], grad[half:ROT]
        return jnp.concatenate(
            [one * cosine + two * sine, two * cosine - one * sine, grad[ROT:]], axis=0
        )

    @pl.loop(0, count)
    def _(i):
        qs = phys(i)
        here = pl.ds(pl.multiple_of(i * BLK, BLK), BLK)
        start = start_ref[0:1, here]
        dos = [do_ref[h * HEAD_DIM : (h + 1) * HEAD_DIM, qs] for h in range(heads)]
        delta = [
            jnp.sum(
                dos[h].astype(f32) * o_ref[h * HEAD_DIM : (h + 1) * HEAD_DIM, qs].astype(f32),
                axis=0, keepdims=True,
            )
            for h in range(heads)
        ]
        lse = [lse_ref[h, 0:1, qs] for h in range(heads)]

        def step(ks, mask, carry):
            scores = [
                jnp.where(mask, dot(kn_ref[h, ks, :], qkv_ref[h, 0, :, qs]), NEG)
                for h in range(heads)
            ]
            dprobs = [dot(vn_ref[h, ks, :], dos[h]) for h in range(heads)]
            probs = [jnp.exp2(scores[h] * LOG2E - lse[h]) for h in range(heads)]
            dscores = [(probs[h] * (dprobs[h] - delta[h])).astype(bf16) for h in range(heads)]
            out = []
            for h in range(heads):
                dv_ref[h, :, ks] += dot_nt(dos[h], probs[h].astype(bf16))
                dk_ref[h, :, ks] += dot_nt(qkv_ref[h, 0, :, qs], dscores[h])
                dq = dot(qkv_ref[h, 1, :, ks], dscores[h])
                out.append(dq if carry is None else carry[h] + dq)
            return tuple(out)

        carry = step(qs, (ik <= iq) & (ik >= start - i * BLK), None)
        carry = lax.fori_loop(
            lo_ref[i], i, lambda j, c: step(phys(j), ik >= start - j * BLK, c), carry
        )
        for h in range(heads):
            dq = unrotate(carry[h] * HEAD_DIM ** (-0.5), cos_ref[:, here], sin_ref[:, here])
            dqkv_ref[h, 0, :, qs] = dq.astype(bf16)

    @pl.loop(0, count)
    def _(i):
        qs = phys(i)
        here = pl.ds(pl.multiple_of(i * BLK, BLK), BLK)
        for h in range(heads):
            dk = unrotate(dk_ref[h, :, qs], cos_ref[:, here], sin_ref[:, here])
            dqkv_ref[h, 1, :, qs] = dk.astype(bf16)
            dqkv_ref[h, 2, :, qs] = dv_ref[h, :, qs].astype(bf16)


def qkv_end_kernel(
    place_ref, dqkv_ref, xh0_ref, xh1_ref, xh2_ref, wq_ref, g1_ref, b1_ref, wdg_ref, sums_ref,
    keep_ref, send_ref, pay_ref,
):
    heads, seq = dqkv_ref.shape[0], dqkv_ref.shape[3]
    g1, b1 = row_of(g1_ref), row_of(b1_ref)
    cols = 3 * HEAD_DIM
    gain, bias, bq = 0.0, 0.0, []
    for h in range(heads):
        grad = dqkv_ref[h].reshape(cols, seq)
        raw = None
        for at, ref in spans((xh0_ref, xh1_ref, xh2_ref), 0):
            part = dot(grad[:, at], ref[...])
            raw = part if raw is None else raw + part
        total = jnp.sum(grad.astype(f32), axis=1, keepdims=True)
        bq.append(jnp.broadcast_to(total, (cols, 128)).T[0:1, :])
        pay_ref[h * cols : (h + 1) * cols, :] = (raw * g1 + total * b1).astype(bf16)
        weight = wq_ref[h * cols : (h + 1) * cols, :].astype(f32)
        gain = gain + jnp.sum(weight * raw, axis=0, keepdims=True)
        bias = bias + jnp.sum(weight * total, axis=0, keepdims=True)
    pay_ref[heads * cols :, :] = wdg_ref[...]
    width = pay_ref.shape[1]
    zeros = jnp.zeros((1, width - heads * cols), f32)
    vectors = pair_rows(
        [
            gain, bias, sums_ref[2:3, :], sums_ref[3:4, :], sums_ref[1:2, :], sums_ref[0:1, :],
            jnp.concatenate(bq + [zeros], axis=1), jnp.zeros((1, width), f32),
        ]
    )
    side = bit_of(place_ref, ORDER_A[0])
    rows = pay_ref.shape[0] // 2
    halves(pay_ref, keep_ref.at[0:rows], send_ref.at[0:rows], side)
    keep_ref[rows:, :] = vectors
    send_ref[rows:, :] = vectors


def tokens_back_kernel(
    dqkv_ref, back0_ref, back1_ref, back2_ref, wq_ref, g1_ref, keep0_ref, keep2_ref, send_ref
):
    rows = keep0_ref.shape[0]
    g1 = row_of(g1_ref)
    cols = wq_ref.shape[0]
    for k in range(4):
        grad = dqkv_ref[:, :, :, k * rows : (k + 1) * rows].reshape(cols, rows)
        back = chunk((back0_ref, back1_ref, back2_ref), k, rows).astype(f32)
        deal(k, back + dot_tn(grad, wq_ref[...]) * g1, keep0_ref, keep2_ref, send_ref)


def forward_kernel(keep2_ref, got_ref, sent_ref):
    rows = keep2_ref.shape[0]
    sent_ref[...] = (keep2_ref[...] + got_ref[rows:, :].astype(f32)).astype(bf16)


def result_kernel(x_ref, keep0_ref, got_ref, far_ref, bd_ref, c2_ref, out_ref):
    rows = x_ref.shape[0]
    summed = keep0_ref[...] + got_ref[:rows, :].astype(f32) + far_ref[...].astype(f32)
    out_ref[...] = (x_ref[...].astype(f32) + summed + (row_of(bd_ref) + row_of(c2_ref))).astype(bf16)


def tokens_grad_kernel(x_ref, dy_ref, keep0_ref, got_ref, far_ref, out_ref):
    rows = x_ref.shape[0]
    grad = keep0_ref[...] + got_ref[:rows, :].astype(f32) + far_ref[...].astype(f32)
    x = x_ref[...].astype(f32)
    c = x - jnp.mean(x, axis=1, keepdims=True)
    inverse = lax.rsqrt(jnp.mean(c * c, axis=1, keepdims=True) + 1e-05)
    xh = c * inverse
    term = grad - jnp.mean(grad, axis=1, keepdims=True)
    term = term - xh * jnp.mean(grad * xh, axis=1, keepdims=True)
    out_ref[...] = dy_ref[...].astype(f32) + inverse * term


def swap(value, axis, size, distance):
    return lax.ppermute(value, axis, [(i, i ^ distance) for i in range(size)])


def unpair(rows):
    return rows[0:8, :].astype(f32) + rows[8:16, :].astype(f32)


def fold_kernel(place_ref, keep_ref, got_ref, next_ref, send_ref, *, bit, tail):
    rows = (keep_ref.shape[0] - tail) // 2
    side = bit_of(place_ref, bit)
    for half, out_ref in ((side, next_ref), (1 - side, send_ref)):
        at = pl.ds(pl.multiple_of(half * rows, 16), rows)
        out_ref[0:rows, :] = (keep_ref[at, :].astype(f32) + got_ref[at, :].astype(f32)).astype(bf16)
    if tail:
        vectors = pair_rows([unpair(keep_ref[2 * rows :, :]) + unpair(got_ref[2 * rows :, :])])
        next_ref[rows:, :] = vectors
        send_ref[rows:, :] = vectors


def total_kernel(keep_ref, got_ref, out_ref, *vector_ref):
    rows = out_ref.shape[0]
    total = keep_ref[0:rows, :].astype(f32) + got_ref[0:rows, :].astype(f32)
    out_ref[...] = total.astype(bf16)
    if vector_ref:
        vector_ref[0][...] = unpair(keep_ref[rows:, :]) + unpair(got_ref[rows:, :])


def join_kernel(place_ref, mine_ref, got_ref, *out_refs, bit):
    side = bit_of(place_ref, bit)
    rows = mine_ref.shape[0]
    out_ref = out_refs[-1]
    for part, ref in ((side, mine_ref), (1 - side, got_ref)):
        at = pl.ds(pl.multiple_of(part * rows, 16), rows)
        out_ref[at, :] = ref[...].astype(out_ref.dtype)
    if len(out_refs) > 1:
        split = out_refs[0].shape[0]
        out_refs[0][...] = out_ref[:split, :]
        out_refs[1][...] = out_ref[split:, :]


def dp_swap(value, dp, bit):
    return swap(value, "dp", dp, 1 << bit)


def fold(place, keep, got, bit, tail=0):
    rows = (keep.shape[0] - tail) // 2 + tail
    return call(
        partial(fold_kernel, bit=bit, tail=tail), "fold", [place, keep, got],
        [like((rows, keep.shape[1]), bf16)] * 2, smem=(0,),
    )


def join(place, mine, got, bit, outs=None):
    width = mine.shape[1]
    if outs is None:
        outs = [like((2 * mine.shape[0], width), bf16)]
    scratch = [pltpu.VMEM((2 * mine.shape[0], width), f32)] if len(outs) > 1 else []
    return call(
        partial(join_kernel, bit=bit), "join", [place, mine, got], outs, scratch, smem=(0,),
    )


def rest_sum(value, dp):
    if dp == 8:
        return value
    groups = [[i + 8 * j for j in range(dp // 8)] for i in range(8)]
    return lax.psum(value, "dp", axis_index_groups=groups)


def rotary_tables(length):
    half = ROT // 2
    freq = np.float32(10000.0) ** (-(np.arange(half, dtype=np.float32) * 2.0) / ROT)
    angle = freq.astype(np.float32)[:, None] * np.arange(length, dtype=np.float32)[None, :]
    return np.cos(angle).astype(np.float32), np.sin(angle).astype(np.float32)


def body(dp, tp, tokens, segment_ids, cotangent, gain1, bias1, gain2, bias2,
         qkv_weight, qkv_bias, dense_weight, dense_bias, fc_in_weight, fc_in_bias,
         fc_out_weight, fc_out_bias):
    assert tp == 4 and dp % 8 == 0
    x0, dy0 = tokens[0], cotangent[0]
    rows, width = x0.shape
    seq = rows * tp
    count = seq // BLK
    wq = qkv_weight.T
    heads = wq.shape[0] // (3 * HEAD_DIM)
    cosine, sine = rotary_tables(seq)
    place = jnp.stack([lax.axis_index("tensor"), lax.axis_index("dp")]).astype(i32)

    x1 = swap(x0, "tensor", tp, 1)
    x2 = swap(x0, "tensor", tp, 2)
    dy1 = swap(dy0, "tensor", tp, 1)
    dy2 = swap(dy0, "tensor", tp, 2)

    bq_column = qkv_bias.astype(f32)[:, None]
    start, lo = call(
        segments_kernel, "segments", [segment_ids, segment_ids],
        [like((1, seq), i32), like((count,), i32)], smem=(1,), smem_out=(1,), flops=8 * UNIT,
    )
    (x1,) = after(start, x1)
    hidden, inner = fc_in_weight.shape[1], dense_weight.shape[0]

    def front(xs, first):
        size = rows * len(xs)
        return call(
            partial(front_kernel, first=first, pieces=len(xs)), "front",
            [place, *xs, gain1, bias1, gain2, bias2, fc_in_weight, fc_in_bias, wq, bq_column,
             cosine, sine],
            [like((size, width), bf16), like((size, hidden), bf16), like((size, hidden), bf16),
             like((heads, 3, HEAD_DIM, size), bf16)],
            smem=(0,), limit=16, flops=len(xs) * 2 * UNIT,
        )

    def ff_back(dys, act, slope, xh, carry=(), last=False):
        size = rows * len(dys)
        outs = [like((size, width), bf16), like((size, width), bf16), like((inner, size), bf16)]
        full = [like((width, hidden), f32), like((hidden, width), f32)]
        sums = [like((8, width), f32)]
        half = [like((width // 2, hidden), bf16)] * 2 + [like((hidden // 2, width), bf16)] * 2
        scratch = [
            pltpu.VMEM((width, hidden), f32), pltpu.VMEM((hidden, width), f32),
            pltpu.VMEM((width, hidden), bf16),
        ]
        return call(
            partial(ff_back_kernel, pieces=len(dys), carried=bool(carry), last=last), "ff_back",
            [place, *dys, act, slope, xh, gain2, bias2, fc_in_weight, fc_out_weight, dense_weight,
             *carry],
            outs + (half if last else full) + sums, scratch if last else [],
            smem=(0,), limit=22 if last else 16, flops=len(dys) * 4 * UNIT,
        )

    xh0, act0, slope0, qkv0 = front((x0, x1), 0)
    (act0,) = after(qkv0, act0)
    out0, back0, do0, *carry = ff_back((dy0, dy1), act0, slope0, xh0)
    x3 = swap(*after(carry[2], x2), "tensor", tp, 1)
    (x2,) = after(carry[2], x2)
    xh1, act1, slope1, qkv1 = front((x2,), 2)
    (x3,) = after(qkv1, x3)
    xh2, act2, slope2, qkv2 = front((x3,), 3)
    qkv, mixed, lse = call(
        attend_kernel, "attend", [place, lo, start, qkv0, qkv1, qkv2],
        [like((heads, 3, HEAD_DIM, seq), bf16), like((inner, seq), bf16), like((heads, 1, seq), f32)],
        [pltpu.VMEM((heads, seq, HEAD_DIM), bf16)],
        smem=(0, 1), limit=12, flops=10 * UNIT,
    )
    dy3 = swap(*after(lse, dy2), "tensor", tp, 1)
    (dy2,) = after(lse, dy2)
    out1, back1, do1, *carry = ff_back((dy2,), act1, slope1, xh1, carry)
    (dy3,) = after(carry[2], dy3)
    out2, back2, do2, k1, s1, k2, s2, sums = ff_back((dy3,), act2, slope2, xh2, carry, last=True)

    got2 = dp_swap(s2, dp, ORDER_A[0])
    got1 = dp_swap(s1, dp, ORDER_B[0])
    (mixed_late,) = after(sums, mixed)
    pair = 2 * rows
    keep0, keep2, send, dense_grad = call(
        attend_end_kernel, "attend_end",
        [mixed_late, dy0, dy1, dy2, dy3, dense_weight, out0, out1, out2],
        [like((rows, width), f32), like((rows, width), f32), like((pair, width), bf16),
         like((inner, width), bf16)],
        limit=12, flops=3 * UNIT,
    )
    got = swap(send, "tensor", tp, 1)
    (mixed_late,) = after(dense_grad, mixed)
    (dqkv,) = call(
        attend_back_kernel, "attend_back",
        [place, lo, start, qkv, mixed_late, do0, do1, do2, lse, cosine, sine],
        [like((heads, 3, HEAD_DIM, seq), bf16)],
        [
            pltpu.VMEM((inner, seq), bf16),
            pltpu.VMEM((heads, seq, HEAD_DIM), bf16), pltpu.VMEM((heads, seq, HEAD_DIM), bf16),
            pltpu.VMEM((heads, HEAD_DIM, seq), f32), pltpu.VMEM((heads, HEAD_DIM, seq), f32),
        ],
        smem=(0, 1), limit=20, flops=14 * UNIT,
    )
    keep2, got, got1, got2 = after(dqkv, keep2, got, got1, got2)
    far = swap(call(forward_kernel, "forward", [keep2, got], [like((rows, width), bf16)])[0],
               "tensor", tp, 2)
    k2, s2 = fold(place, k2, got2, ORDER_A[1])
    got2 = dp_swap(s2, dp, ORDER_A[1])
    k1, s1 = fold(place, k1, got1, ORDER_B[1])
    got1 = dp_swap(s1, dp, ORDER_B[1])

    tail = 16
    (dqkv,) = after((k1, k2), dqkv)
    keep_c, send_c = call(
        qkv_end_kernel, "qkv_end",
        [place, dqkv, xh0, xh1, xh2, wq, gain1, bias1, dense_grad, sums],
        [like((width // 2 + tail, width), bf16)] * 2,
        [pltpu.VMEM((wq.shape[0] + inner, width), bf16)],
        smem=(0,), limit=12, flops=3 * UNIT,
    )
    got_c = dp_swap(send_c, dp, ORDER_A[0])
    (dqkv,) = after(keep_c, dqkv)
    keep0b, keep2b, sendb = call(
        tokens_back_kernel, "tokens_back", [dqkv, back0, back1, back2, wq, gain1],
        [like((rows, width), f32), like((rows, width), f32), like((pair, width), bf16)],
        limit=8, flops=3 * UNIT,
    )
    gotb = swap(sendb, "tensor", tp, 1)

    def finish_sum(keep, got, vector=0):
        size = keep.shape[0] - vector
        outs = [like((size, width), bf16)] + ([like((8, width), f32)] if vector else [])
        total = call(total_kernel, "total", [keep, got], outs)
        if dp == 8:
            return total
        return [rest_sum(total[0].astype(f32), dp).astype(bf16)] + [
            rest_sum(t, dp) for t in total[1:]
        ]

    k2, s2 = fold(place, k2, got2, ORDER_A[2])
    got2 = dp_swap(s2, dp, ORDER_A[2])
    k1, s1 = fold(place, k1, got1, ORDER_B[2])
    got1 = dp_swap(s1, dp, ORDER_B[2])
    farb = swap(call(forward_kernel, "forward", [keep2b, gotb], [like((rows, width), bf16)])[0],
                "tensor", tp, 2)
    keep_c, send_c = fold(place, keep_c, got_c, ORDER_A[1], tail)
    got_c = dp_swap(send_c, dp, ORDER_A[1])

    (mine2,) = finish_sum(k2, got2)
    (mine1,) = finish_sum(k1, got1)
    for step in (2, 1):
        mine2 = join(place, mine2, dp_swap(mine2, dp, ORDER_A[step]), ORDER_A[step])[0]
        mine1 = join(place, mine1, dp_swap(mine1, dp, ORDER_B[step]), ORDER_B[step])[0]
    w2_grad = join(place, mine2, dp_swap(mine2, dp, ORDER_A[0]), ORDER_A[0],
                   [like((hidden, width), f32)])[0]
    w1_grad = join(place, mine1, dp_swap(mine1, dp, ORDER_B[0]), ORDER_B[0],
                   [like((width, hidden), f32)])[0]

    keep_c, send_c = fold(place, keep_c, got_c, ORDER_A[2], tail)
    got_c = dp_swap(send_c, dp, ORDER_A[2])
    mine_c, vectors = finish_sum(keep_c, got_c, tail)
    for step in (2, 1):
        mine_c = join(place, mine_c, dp_swap(mine_c, dp, ORDER_A[step]), ORDER_A[step])[0]
    wq_grad, wd_grad = join(
        place, mine_c, dp_swap(mine_c, dp, ORDER_A[0]), ORDER_A[0],
        [like((wq.shape[0], width), f32), like((inner, width), f32)],
    )
    near = vectors + swap(vectors, "tensor", tp, 1)
    near = near + swap(near, "tensor", tp, 2)
    result = call(
        result_kernel, "result", [x0, keep0, got, far, dense_bias, fc_out_bias],
        [like((rows, width), bf16)],
    )[0]
    input_grad = call(
        tokens_grad_kernel, "tokens_grad", [x0, dy0, keep0b, gotb, farb],
        [like((rows, width), f32)],
    )[0]
    return (
        result[None], input_grad[None], near[0], near[1], near[2], near[3],
        wq_grad.T, vectors[6, : wq.shape[0]], wd_grad, vectors[4],
        w1_grad, vectors[5], w2_grad, vectors[4],
    )


def solution(mesh):
    split = P("dp", "tensor", None)
    columns, stacked, vector = P(None, "tensor"), P("tensor", None), P("tensor")
    whole = P()
    return jax.shard_map(
        partial(body, mesh.shape["dp"], mesh.shape["tensor"]),
        mesh=mesh,
        in_specs=(
            split, P("dp", None), split, whole, whole, whole, whole, columns, vector, stacked,
            whole, columns, vector, stacked, whole,
        ),
        out_specs=(
            split, split, whole, whole, whole, whole, columns, vector, stacked, whole, columns,
            vector, stacked, whole,
        ),
        check_vma=False,
    )
```

```python
from functools import partial

import jax
import jax.numpy as jnp
import numpy as np
from jax import lax
from jax.experimental import pallas as pl
from jax.experimental.pallas import tpu as pltpu
from jax.sharding import PartitionSpec as P

HEAD_DIM = 64
ROT = 16
SEGS = 8
BLK = 256
NEG = -1e30
LOG2E = 1.4426950408889634
f32, bf16, i32 = jnp.float32, jnp.bfloat16, jnp.int32
VMEM = pl.BlockSpec(memory_space=pltpu.VMEM)
SMEM = pl.BlockSpec(memory_space=pltpu.SMEM)
MIB = 1 << 20
UNIT = 500_000_000
SEQUENCE = (
    "attend_back", "p1", "qkv_end", "p2", "q1", "sides", "q2", "p3",
    "forward", "p4", "q3", "p5", "q4", "vectors", "q5", "result",
    "tokens_grad", "p6", "q6",
)
COSTS = {
    "attend": 10, "attend_back": 14, "ff_back": 4, "front": 2, "p3": 150, "p4": 60,
    "segments": 8,
}
ORDER_A, ORDER_B = (0, 1, 2), (1, 0, 2)


def dot(a, b):
    return jnp.dot(a, b, preferred_element_type=f32)


def dot_nt(a, b):
    return lax.dot_general(a, b, (((1,), (1,)), ((), ())), preferred_element_type=f32)


def dot_tn(a, b):
    return lax.dot_general(a, b, (((0,), (0,)), ((), ())), preferred_element_type=f32)


def like(shape, dtype):
    return jax.ShapeDtypeStruct(shape, dtype)


def call(kernel, name, inputs, outs, scratch=(), limit=8, smem=(), smem_out=(), flops=1000):
    return pl.pallas_call(
        kernel,
        out_shape=tuple(outs),
        in_specs=[SMEM if i in smem else VMEM for i in range(len(inputs))],
        out_specs=tuple(SMEM if i in smem_out else VMEM for i in range(len(outs))),
        scratch_shapes=list(scratch),
        compiler_params=pltpu.CompilerParams(vmem_limit_bytes=limit * MIB),
        cost_estimate=pl.CostEstimate(flops=flops, bytes_accessed=1000, transcendentals=0),
        name=name,
    )(*inputs)


def cost(name, times=1):
    return int(COSTS.get(name, 0.002) * times * UNIT)


def after(token, *values):
    return lax.optimization_barrier((token, *values))[1:]


class Chain:
    def __init__(self, token):
        self.token = token

    def __call__(self, kernel, name, inputs, outs, hold, **options):
        inputs = list(inputs)
        (inputs[hold],) = after(self.token, inputs[hold])
        outs = call(kernel, name, inputs, outs, **options)
        self.token = outs[0]
        return outs


def row_of(ref):
    return ref[...].astype(f32).reshape(1, -1)


def column_of(row):
    return jnp.broadcast_to(row, (128, row.shape[1])).T[:, 0:1]


def pair_rows(rows):
    rows = jnp.concatenate(rows, axis=0)
    high = rows.astype(bf16)
    return jnp.concatenate([high, (rows - high.astype(f32)).astype(bf16)], axis=0)


def segments_kernel(ids_ref, first_ref, start_ref, lo_ref):
    ids = ids_ref[...]
    start = jnp.zeros_like(ids)
    begins = []
    for s in range(SEGS):
        begin = jnp.sum(jnp.where(ids < s, 1.0, 0.0)).astype(i32)
        begins.append(begin)
        start = jnp.where(ids == s, begin, start)
    start_ref[...] = start
    for i in range(lo_ref.shape[0]):
        seg = first_ref[0, i * BLK]
        lo = begins[0]
        for s in range(1, SEGS):
            lo = jnp.where(seg == s, begins[s], lo)
        lo_ref[i] = lax.div(lo, BLK)


def front_kernel(place_ref, *refs, first, pieces):
    x_refs, refs = refs[:pieces], refs[pieces:]
    g1_ref, b1_ref, g2_ref, b2_ref, w1_ref, c1_ref, wq_ref, bq_ref, cos_ref, sin_ref = refs[:10]
    xh_ref, act_ref, slope_ref, qkv_ref = refs[10:]
    heads = qkv_ref.shape[0]
    half = ROT // 2
    rows = x_refs[0].shape[0]
    g1, b1, g2, b2, c1 = [row_of(r) for r in (g1_ref, b1_ref, g2_ref, b2_ref, c1_ref)]
    for piece, x_ref in enumerate(x_refs):
        out = slice(piece * rows, (piece + 1) * rows)
        at = (place_ref[0] ^ (first + piece)) * rows
        here = pl.ds(pl.multiple_of(at, 128), rows)
        x = x_ref[...].astype(f32)
        c = x - jnp.mean(x, axis=1, keepdims=True)
        xh = c * lax.rsqrt(jnp.mean(c * c, axis=1, keepdims=True) + 1e-05)
        xh_ref[out, :] = xh.astype(bf16)
        h1 = (xh * g1 + b1).astype(bf16)
        h2 = (xh * g2 + b2).astype(bf16)
        pre = dot(h2, w1_ref[...]) + c1
        qkv = dot_nt(wq_ref[...], h1) + bq_ref[...]
        cosine, sine = cos_ref[:, here], sin_ref[:, here]
        for h in range(heads):
            for part in range(3):
                at = (3 * h + part) * HEAD_DIM
                v = qkv[at : at + HEAD_DIM]
                if part < 2:
                    one, two = v[:half], v[half:ROT]
                    v = jnp.concatenate(
                        [one * cosine - two * sine, two * cosine + one * sine, v[ROT:]], axis=0
                    )
                if part == 0:
                    v = v * HEAD_DIM ** (-0.5)
                qkv_ref[h, part, :, out] = v.astype(bf16)
        cdf = 0.5 + 0.5 * lax.erf(pre * 0.5**0.5)
        pdf = jnp.exp(pre * pre * -0.5) * (2.0 * np.pi) ** -0.5
        act_ref[out, :] = (pre * cdf).astype(bf16)
        slope_ref[out, :] = (cdf + pre * pdf).astype(bf16)


def halves(payload_ref, keep_ref, send_ref, side):
    rows = keep_ref.shape[0]
    keep_ref[...] = payload_ref[pl.ds(pl.multiple_of(side * rows, 16), rows), :]
    send_ref[...] = payload_ref[pl.ds(pl.multiple_of((1 - side) * rows, 16), rows), :]


def bit_of(place_ref, bit):
    return lax.rem(lax.div(place_ref[1], 1 << bit), 2)


def ff_back_kernel(place_ref, *refs, pieces, carried, last):
    dy_refs, refs = refs[:pieces], refs[pieces:]
    act_ref, slope_ref, xh_ref, g2_ref, b2_ref, w1_ref, w2_ref, wd_ref = refs[:8]
    refs = refs[8:]
    if carried:
        w1_in, w2_in, sums_in = refs[:3]
        refs = refs[3:]
    if last:
        out_ref, back_ref, do_ref, k1_ref, s1_ref, k2_ref, s2_ref = refs[:7]
        w1g_ref, w2g_ref, pay_ref = refs[7:]
    else:
        out_ref, back_ref, do_ref, w1g_ref, w2g_ref, sums_ref = refs
    rows = dy_refs[0].shape[0]
    g2 = row_of(g2_ref)
    sums = [sums_in[i : i + 1, :] for i in range(2)] if carried else [0.0, 0.0]
    for piece, dy_ref in enumerate(dy_refs):
        r = slice(piece * rows, (piece + 1) * rows)
        dy = dy_ref[...]
        act = act_ref[r, :]
        du = (dot_nt(dy, w2_ref[...]) * slope_ref[r, :].astype(f32)).astype(bf16)
        w2_part = dot_tn(act, dy)
        w1_part = dot_tn(xh_ref[r, :], du)
        if piece == 0:
            w2g_ref[...] = w2_in[...] + w2_part if carried else w2_part
            w1g_ref[...] = w1_in[...] + w1_part if carried else w1_part
        else:
            w2g_ref[...] += w2_part
            w1g_ref[...] += w1_part
        out_ref[r, :] = dot(act, w2_ref[...]).astype(bf16)
        back_ref[r, :] = (dot_nt(du, w1_ref[...]) * g2).astype(bf16)
        do_ref[:, r] = dot_nt(wd_ref[...], dy).astype(bf16)
        sums[0] = sums[0] + jnp.sum(du.astype(f32), axis=0, keepdims=True)
        sums[1] = sums[1] + jnp.sum(dy.astype(f32), axis=0, keepdims=True)
    if not last:
        sums_ref[0:1, :] = sums[0]
        sums_ref[1:2, :] = sums[1]
    else:
        pay_ref[...] = w2g_ref[...].astype(bf16)
        half = pay_ref.shape[0] // 2
        halves(pay_ref, k2_ref.at[0:half], s2_ref.at[0:half], bit_of(place_ref, ORDER_A[0]))
        du_sum = jnp.broadcast_to(sums[0], (8, sums[0].shape[1]))
        high = du_sum.astype(bf16)
        low = (du_sum - high.astype(f32)).astype(bf16)
        bias = (dot_nt(high, w1_ref[...]) + dot_nt(low, w1_ref[...]))[0:1]
        raw = w1g_ref[...]
        gain = jnp.sum(raw * w1_ref[...].astype(f32), axis=1, keepdims=True)
        gain = jnp.broadcast_to(gain, (gain.shape[0], 128)).T[0:1, :]
        vectors = pair_rows([gain, bias, sums[1], sums[0]])
        k2_ref[half:, :] = vectors
        s2_ref[half:, :] = vectors
        pay_ref[...] = (raw * column_of(g2) + column_of(row_of(b2_ref)) * sums[0]).astype(bf16)
        halves(pay_ref, k1_ref, s1_ref, bit_of(place_ref, ORDER_B[0]))


def blocks(place_ref, count, per):
    def phys(j):
        return pl.ds(
            pl.multiple_of(((lax.div(j, per) ^ place_ref[0]) * per + lax.rem(j, per)) * BLK, BLK),
            BLK,
        )

    return phys


def spans(refs, axis):
    at = 0
    for ref in refs:
        size = ref.shape[axis]
        yield slice(at, at + size), ref
        at += size


def attend_kernel(
    place_ref, lo_ref, start_ref, part0_ref, part1_ref, part2_ref,
    qkv_ref, o_ref, lse_ref, kn_ref,
):
    heads, seq = qkv_ref.shape[0], qkv_ref.shape[3]
    count = seq // BLK
    phys = blocks(place_ref, count, count // 4)
    for at, ref in spans((part0_ref, part1_ref, part2_ref), 3):
        qkv_ref[:, :, :, at] = ref[...]
    for h in range(heads):
        for b in range(count):
            r = slice(b * BLK, (b + 1) * BLK)
            kn_ref[h, r, :] = qkv_ref[h, 1, :, r].T
    ik = lax.broadcasted_iota(i32, (BLK, BLK), 0)
    iq = lax.broadcasted_iota(i32, (BLK, BLK), 1)

    @pl.loop(0, count)
    def _(i):
        qs = phys(i)
        start = start_ref[0:1, pl.ds(pl.multiple_of(i * BLK, BLK), BLK)]

        def step(ks, mask, carry):
            scores = [
                jnp.where(mask, dot(kn_ref[h, ks, :], qkv_ref[h, 0, :, qs]), NEG)
                for h in range(heads)
            ]
            out = []
            for h in range(heads):
                top = jnp.max(scores[h], axis=0, keepdims=True)
                if carry is not None:
                    top = jnp.maximum(top, carry[h][0])
                expo = jnp.exp2(scores[h] * LOG2E - top * LOG2E)
                total = jnp.sum(expo, axis=0, keepdims=True)
                mixed = dot(qkv_ref[h, 2, :, ks], expo.astype(bf16))
                if carry is not None:
                    fade = jnp.exp2((carry[h][0] - top) * LOG2E)
                    total = total + carry[h][1] * fade
                    mixed = mixed + carry[h][2] * fade
                out.append((top, total, mixed))
            return tuple(out)

        carry = step(qs, (ik <= iq) & (ik >= start - i * BLK), None)
        carry = lax.fori_loop(
            lo_ref[i], i, lambda j, c: step(phys(j), ik >= start - j * BLK, c), carry
        )
        for h in range(heads):
            top, total, mixed = carry[h]
            at = slice(h * HEAD_DIM, (h + 1) * HEAD_DIM)
            o_ref[at, qs] = (mixed * (1.0 / total)).astype(bf16)
            lse_ref[h, 0:1, qs] = top * LOG2E + jnp.log2(total)


def chunk(refs, k, rows):
    for at, ref in spans(refs, 0):
        if at.start <= k * rows < at.stop:
            return ref[k * rows - at.start : (k + 1) * rows - at.start, :]


def attend_back_kernel(
    place_ref, lo_ref, start_ref, qkv_ref, o_ref, do0_ref, do1_ref, do2_ref, lse_ref, cos_ref,
    sin_ref, dqkv_ref, do_ref, kn_ref, vn_ref, dk_ref, dv_ref,
):
    heads, seq = qkv_ref.shape[0], qkv_ref.shape[3]
    count = seq // BLK
    phys = blocks(place_ref, count, count // 4)
    half = ROT // 2
    for at, ref in spans((do0_ref, do1_ref, do2_ref), 1):
        do_ref[:, at] = ref[...]
    for h in range(heads):
        for b in range(count):
            r = slice(b * BLK, (b + 1) * BLK)
            kn_ref[h, r, :] = qkv_ref[h, 1, :, r].T
            vn_ref[h, r, :] = qkv_ref[h, 2, :, r].T
    dk_ref[...] = jnp.zeros_like(dk_ref)
    dv_ref[...] = jnp.zeros_like(dv_ref)
    ik = lax.broadcasted_iota(i32, (BLK, BLK), 0)
    iq = lax.broadcasted_iota(i32, (BLK, BLK), 1)

    def unrotate(grad, cosine, sine):
        one, two = grad[:half], grad[half:ROT]
        return jnp.concatenate(
            [one * cosine + two * sine, two * cosine - one * sine, grad[ROT:]], axis=0
        )

    @pl.loop(0, count)
    def _(i):
        qs = phys(i)
        here = pl.ds(pl.multiple_of(i * BLK, BLK), BLK)
        start = start_ref[0:1, here]
        dos = [do_ref[h * HEAD_DIM : (h + 1) * HEAD_DIM, qs] for h in range(heads)]
        delta = [
            jnp.sum(
                dos[h].astype(f32) * o_ref[h * HEAD_DIM : (h + 1) * HEAD_DIM, qs].astype(f32),
                axis=0, keepdims=True,
            )
            for h in range(heads)
        ]
        lse = [lse_ref[h, 0:1, qs] for h in range(heads)]

        def step(ks, mask, carry):
            scores = [
                jnp.where(mask, dot(kn_ref[h, ks, :], qkv_ref[h, 0, :, qs]), NEG)
                for h in range(heads)
            ]
            dprobs = [dot(vn_ref[h, ks, :], dos[h]) for h in range(heads)]
            probs = [jnp.exp2(scores[h] * LOG2E - lse[h]) for h in range(heads)]
            dscores = [(probs[h] * (dprobs[h] - delta[h])).astype(bf16) for h in range(heads)]
            out = []
            for h in range(heads):
                dv_ref[h, :, ks] += dot_nt(dos[h], probs[h].astype(bf16))
                dk_ref[h, :, ks] += dot_nt(qkv_ref[h, 0, :, qs], dscores[h])
                dq = dot(qkv_ref[h, 1, :, ks], dscores[h])
                out.append(dq if carry is None else carry[h] + dq)
            return tuple(out)

        carry = step(qs, (ik <= iq) & (ik >= start - i * BLK), None)
        carry = lax.fori_loop(
            lo_ref[i], i, lambda j, c: step(phys(j), ik >= start - j * BLK, c), carry
        )
        for h in range(heads):
            dq = unrotate(carry[h] * HEAD_DIM ** (-0.5), cos_ref[:, here], sin_ref[:, here])
            dqkv_ref[h, 0, :, qs] = dq.astype(bf16)

    @pl.loop(0, count)
    def _(i):
        qs = phys(i)
        here = pl.ds(pl.multiple_of(i * BLK, BLK), BLK)
        for h in range(heads):
            dk = unrotate(dk_ref[h, :, qs], cos_ref[:, here], sin_ref[:, here])
            dqkv_ref[h, 1, :, qs] = dk.astype(bf16)
            dqkv_ref[h, 2, :, qs] = dv_ref[h, :, qs].astype(bf16)


def qkv_end_kernel(
    place_ref, dqkv_ref, xh0_ref, xh1_ref, xh2_ref, wq_ref, g1_ref, b1_ref,
    o_ref, dy0_ref, dy1_ref, dy2_ref, dy3_ref, ka_ref, sa_ref, kb_ref, sb_ref, pay_ref,
):
    heads, seq = dqkv_ref.shape[0], dqkv_ref.shape[3]
    g1, b1 = row_of(g1_ref), row_of(b1_ref)
    cols = 3 * HEAD_DIM
    gain, bias, bq = 0.0, 0.0, []
    for h in range(heads):
        grad = dqkv_ref[h].reshape(cols, seq)
        raw = None
        for at, ref in spans((xh0_ref, xh1_ref, xh2_ref), 0):
            part = dot(grad[:, at], ref[...])
            raw = part if raw is None else raw + part
        total = jnp.sum(grad.astype(f32), axis=1, keepdims=True)
        bq.append(jnp.broadcast_to(total, (cols, 128)).T[0:1, :])
        pay_ref[h * cols : (h + 1) * cols, :] = (raw * g1 + total * b1).astype(bf16)
        weight = wq_ref[h * cols : (h + 1) * cols, :].astype(f32)
        gain = gain + jnp.sum(weight * raw, axis=0, keepdims=True)
        bias = bias + jnp.sum(weight * total, axis=0, keepdims=True)
    dense = None
    for at, ref in spans((dy0_ref, dy1_ref, dy2_ref, dy3_ref), 0):
        part = dot(o_ref[:, at], ref[...])
        dense = part if dense is None else dense + part
    pay_ref[heads * cols :, :] = dense.astype(bf16)
    width = pay_ref.shape[1]
    zeros = jnp.zeros((1, width - heads * cols), f32)
    vectors = pair_rows([gain, bias, jnp.concatenate(bq + [zeros], axis=1), jnp.zeros((1, width), f32)])
    rows = kb_ref.shape[0]
    top, bottom = pay_ref.at[0 : 2 * rows], pay_ref.at[2 * rows : 4 * rows]
    halves(top, ka_ref.at[0:rows], sa_ref.at[0:rows], bit_of(place_ref, ORDER_A[0]))
    halves(bottom, kb_ref, sb_ref, bit_of(place_ref, ORDER_B[0]))
    ka_ref[rows:, :] = vectors
    sa_ref[rows:, :] = vectors


def sides_kernel(
    dqkv_ref, back0_ref, back1_ref, back2_ref, wq_ref, g1_ref,
    o_ref, out0_ref, out1_ref, out2_ref, wd_ref,
    outn_ref, outf_ref, backn_ref, backf_ref, send_ref,
):
    rows = outn_ref.shape[0]
    g1 = row_of(g1_ref)
    cols = wq_ref.shape[0]
    for k in range(4):
        r = slice(k * rows, (k + 1) * rows)
        back = chunk((back0_ref, back1_ref, back2_ref), k, rows).astype(f32)
        back = back + dot_tn(dqkv_ref[:, :, :, r].reshape(cols, rows), wq_ref[...]) * g1
        out = chunk((out0_ref, out1_ref, out2_ref), k, rows).astype(f32)
        out = out + dot_tn(o_ref[:, r], wd_ref[...])
        for value, keep, place in ((out, (outn_ref, outf_ref), 0), (back, (backn_ref, backf_ref), 2)):
            if k % 2:
                at = (place + k // 2) * rows
                send_ref[at : at + rows, :] = value.astype(bf16)
            else:
                keep[k // 2][...] = value


def forward_kernel(outf_ref, backf_ref, got_ref, sent_ref):
    rows = outf_ref.shape[0]
    for i, ref in enumerate((outf_ref, backf_ref)):
        got = got_ref[(2 * i + 1) * rows : (2 * i + 2) * rows, :].astype(f32)
        sent_ref[i * rows : (i + 1) * rows, :] = (ref[...] + got).astype(bf16)


def result_kernel(x_ref, keep_ref, got_ref, far_ref, bd_ref, c2_ref, out_ref):
    rows = x_ref.shape[0]
    summed = keep_ref[...] + got_ref[:rows, :].astype(f32) + far_ref[:rows, :].astype(f32)
    out_ref[...] = (x_ref[...].astype(f32) + summed + (row_of(bd_ref) + row_of(c2_ref))).astype(bf16)


def tokens_grad_kernel(x_ref, dy_ref, keep_ref, got_ref, far_ref, out_ref):
    rows = x_ref.shape[0]
    grad = keep_ref[...] + got_ref[2 * rows : 3 * rows, :].astype(f32) + far_ref[rows:, :].astype(f32)
    x = x_ref[...].astype(f32)
    c = x - jnp.mean(x, axis=1, keepdims=True)
    inverse = lax.rsqrt(jnp.mean(c * c, axis=1, keepdims=True) + 1e-05)
    xh = c * inverse
    term = grad - jnp.mean(grad, axis=1, keepdims=True)
    term = term - xh * jnp.mean(grad * xh, axis=1, keepdims=True)
    out_ref[...] = dy_ref[...].astype(f32) + inverse * term


def swap(value, axis, size, distance):
    return lax.ppermute(value, axis, [(i, i ^ distance) for i in range(size)])


def unpair(rows):
    rows = rows.astype(f32)
    return rows[0:4, :] + rows[4:8, :]


def half_sum(keep_ref, got_ref, half, rows):
    at = pl.ds(pl.multiple_of(half * rows, 16), rows)
    return (keep_ref[at, :].astype(f32) + got_ref[at, :].astype(f32)).astype(bf16)


def vector_sum(keep_ref, got_ref):
    return unpair(keep_ref[-8:, :]) + unpair(got_ref[-8:, :])


def fold_kernel(place_ref, ka_ref, ga_ref, kb_ref, gb_ref, *outs):
    for keep_ref, got_ref, next_ref, send_ref, order in (
        (ka_ref, ga_ref, outs[0], outs[1], ORDER_A), (kb_ref, gb_ref, outs[2], outs[3], ORDER_B),
    ):
        rows = keep_ref.shape[0] // 16 * 8
        side = bit_of(place_ref, order[1])
        for half, out_ref in ((side, next_ref), (1 - side, send_ref)):
            out_ref[0:rows, :] = half_sum(keep_ref, got_ref, half, rows)
    vectors = pair_rows([vector_sum(ka_ref, ga_ref)])
    outs[0][-8:, :] = vectors
    outs[1][-8:, :] = vectors


def far_fold_kernel(place_ref, ka_ref, ga_ref, kb_ref, gb_ref, next_ref, send_ref):
    side = bit_of(place_ref, ORDER_A[2])
    first = 0
    for keep_ref, got_ref in ((ka_ref, ga_ref), (kb_ref, gb_ref)):
        rows = keep_ref.shape[0] // 16 * 8
        for half, out_ref in ((side, next_ref), (1 - side, send_ref)):
            out_ref[first : first + rows, :] = half_sum(keep_ref, got_ref, half, rows)
        first += rows
    vectors = pair_rows([vector_sum(ka_ref, ga_ref)])
    next_ref[first:, :] = vectors
    send_ref[first:, :] = vectors


def total_kernel(keep_ref, got_ref, out_ref, vector_ref):
    rows = out_ref.shape[0]
    total = keep_ref[0:rows, :].astype(f32) + got_ref[0:rows, :].astype(f32)
    out_ref[...] = total.astype(bf16)
    vector_ref[...] = vector_sum(keep_ref, got_ref)


def put_halves(out_ref, mine, got, side):
    rows = mine.shape[0]
    for half, value in ((side, mine), (1 - side, got)):
        out_ref[pl.ds(pl.multiple_of(half * rows, 16), rows), :] = value.astype(out_ref.dtype)


def far_join_kernel(place_ref, mine_ref, got_ref, a_ref, b_ref):
    side = bit_of(place_ref, ORDER_A[2])
    first = 0
    for out_ref in (a_ref, b_ref):
        r = slice(first, first + out_ref.shape[0] // 2)
        put_halves(out_ref, mine_ref[r, :], got_ref[r, :], side)
        first = r.stop


def join_kernel(place_ref, ma_ref, ga_ref, mb_ref, gb_ref, a_ref, b_ref, *, step):
    put_halves(a_ref, ma_ref[...], ga_ref[...], bit_of(place_ref, ORDER_A[step]))
    put_halves(b_ref, mb_ref[...], gb_ref[...], bit_of(place_ref, ORDER_B[step]))


def spread_kernel(place_ref, ma_ref, ga_ref, mb_ref, gb_ref, wq_ref, wd_ref):
    rows = ma_ref.shape[0]
    put_halves(wq_ref.at[0 : 2 * rows], ma_ref[...], ga_ref[...], bit_of(place_ref, ORDER_A[0]))
    side = bit_of(place_ref, ORDER_B[0])
    mine, got = mb_ref[...].astype(f32), gb_ref[...].astype(f32)
    wq_ref[2 * rows :, :] = jnp.where(side == 0, mine, got)
    wd_ref[...] = jnp.where(side == 0, got, mine)


def vectors_kernel(near_ref, a_ref, c_ref, *out_refs):
    for i in range(4):
        out_refs[i][...] = near_ref[i : i + 1, :].reshape(-1)
    out_refs[4][...] = a_ref[2:3, :].reshape(-1)
    out_refs[5][...] = a_ref[2:3, :].reshape(-1)
    out_refs[6][...] = a_ref[3:4, :].reshape(-1)
    out_refs[7][...] = c_ref[2:3, : out_refs[7].shape[0]].reshape(-1)


def dp_swap(value, dp, bit):
    return swap(value, "dp", dp, 1 << bit)


def rest_sum(value, dp):
    if dp == 8:
        return value
    groups = [[i + 8 * j for j in range(dp // 8)] for i in range(8)]
    return lax.psum(value.astype(f32), "dp", axis_index_groups=groups).astype(value.dtype)


def rotary_tables(length):
    half = ROT // 2
    freq = np.float32(10000.0) ** (-(np.arange(half, dtype=np.float32) * 2.0) / ROT)
    angle = freq.astype(np.float32)[:, None] * np.arange(length, dtype=np.float32)[None, :]
    return np.cos(angle).astype(np.float32), np.sin(angle).astype(np.float32)


def body(dp, tp, tokens, segment_ids, cotangent, gain1, bias1, gain2, bias2,
         qkv_weight, qkv_bias, dense_weight, dense_bias, fc_in_weight, fc_in_bias,
         fc_out_weight, fc_out_bias):
    assert tp == 4 and dp % 8 == 0
    x0, dy0 = tokens[0], cotangent[0]
    rows, width = x0.shape
    seq = rows * tp
    count = seq // BLK
    wq = qkv_weight.T
    heads = wq.shape[0] // (3 * HEAD_DIM)
    cosine, sine = rotary_tables(seq)
    place = jnp.stack([lax.axis_index("tensor"), lax.axis_index("dp")]).astype(i32)

    x1 = swap(x0, "tensor", tp, 1)
    x2 = swap(x0, "tensor", tp, 2)
    dy1 = swap(dy0, "tensor", tp, 1)
    dy2 = swap(dy0, "tensor", tp, 2)

    bq_column = qkv_bias.astype(f32)[:, None]
    start, lo = call(
        segments_kernel, "segments", [segment_ids, segment_ids],
        [like((1, seq), i32), like((count,), i32)], smem=(1,), smem_out=(1,), flops=cost("segments"),
    )
    (x1,) = after(start, x1)
    hidden, inner = fc_in_weight.shape[1], dense_weight.shape[0]

    def front(xs, first):
        size = rows * len(xs)
        return call(
            partial(front_kernel, first=first, pieces=len(xs)), "front",
            [place, *xs, gain1, bias1, gain2, bias2, fc_in_weight, fc_in_bias, wq, bq_column,
             cosine, sine],
            [like((size, width), bf16), like((size, hidden), bf16), like((size, hidden), bf16),
             like((heads, 3, HEAD_DIM, size), bf16)],
            smem=(0,), limit=16, flops=cost("front", len(xs)),
        )

    def ff_back(dys, act, slope, xh, carry=(), last=False):
        size = rows * len(dys)
        outs = [like((size, width), bf16), like((size, width), bf16), like((inner, size), bf16)]
        full = [like((width, hidden), f32), like((hidden, width), f32)]
        sums = [like((8, width), f32)]
        half = [like((width // 2, hidden), bf16)] * 2 + [like((hidden // 2 + 8, width), bf16)] * 2
        scratch = [
            pltpu.VMEM((width, hidden), f32), pltpu.VMEM((hidden, width), f32),
            pltpu.VMEM((width, hidden), bf16),
        ]
        return call(
            partial(ff_back_kernel, pieces=len(dys), carried=bool(carry), last=last), "ff_back",
            [place, *dys, act, slope, xh, gain2, bias2, fc_in_weight, fc_out_weight, dense_weight,
             *carry],
            outs + (half if last else full + sums), scratch if last else [],
            smem=(0,), limit=22 if last else 16, flops=cost("ff_back", len(dys)),
        )

    xh0, act0, slope0, qkv0 = front((x0, x1), 0)
    (act0,) = after(qkv0, act0)
    out0, back0, do0, *carry = ff_back((dy0, dy1), act0, slope0, xh0)
    x3 = swap(*after(carry[2], x2), "tensor", tp, 1)
    (x2,) = after(carry[2], x2)
    xh1, act1, slope1, qkv1 = front((x2,), 2)
    (x3,) = after(qkv1, x3)
    xh2, act2, slope2, qkv2 = front((x3,), 3)
    qkv, mixed, lse = call(
        attend_kernel, "attend", [place, lo, start, qkv0, qkv1, qkv2],
        [like((heads, 3, HEAD_DIM, seq), bf16), like((inner, seq), bf16), like((heads, 1, seq), f32)],
        [pltpu.VMEM((heads, seq, HEAD_DIM), bf16)],
        smem=(0, 1), limit=12, flops=cost("attend"),
    )
    dy3 = swap(*after(lse, dy2), "tensor", tp, 1)
    (dy2,) = after(lse, dy2)
    out1, back1, do1, *carry = ff_back((dy2,), act1, slope1, xh1, carry)
    (dy3,) = after(carry[2], dy3)
    out2, back2, do2, k1, s1, k2, s2 = ff_back((dy3,), act2, slope2, xh2, carry, last=True)

    run = Chain(do2)
    tail = 8
    keep, got, vectors, made = {}, {}, {}, {}

    def part(count):
        return like((count, width), bf16)

    def send(name, a, b, step):
        got[name] = [dp_swap(a, dp, ORDER_A[step]), dp_swap(b, dp, ORDER_B[step])]

    def parts(name):
        (ka, kb), (ga, gb) = keep[name], got[name]
        return [place, ka, ga, kb, gb]

    def fold(name):
        na, nb = keep[name][0].shape[0] // 16 * 8, keep[name][1].shape[0] // 2
        ka, sa, kb, sb = run(
            fold_kernel, "fold", parts(name), [part(na + tail)] * 2 + [part(nb)] * 2,
            hold=2, smem=(0,), flops=cost(f"{name}1"),
        )
        keep[name] = ka, kb
        send(name, sa, sb, 1)

    def far_fold(name):
        count = sum(k.shape[0] // 16 * 8 for k in keep[name]) + tail
        keep[name], sent = run(
            far_fold_kernel, "far_fold", parts(name), [part(count)] * 2, hold=2, smem=(0,),
            flops=cost(f"{name}2"),
        )
        got[name] = dp_swap(sent, dp, ORDER_A[2])

    def complete(name):
        total, vector = run(
            total_kernel, "total", [keep[name], got[name]],
            [part(keep[name].shape[0] - tail), like((4, width), f32)], hold=1,
            flops=cost(f"{name}3"),
        )
        keep[name], vectors[name] = rest_sum(total, dp), rest_sum(vector, dp)
        got[name] = dp_swap(keep[name], dp, ORDER_A[2])
        if len(vectors) == 2:
            near = jnp.concatenate([vectors["q"][:2], vectors["p"][:2]], axis=0)
            near = near + swap(near, "tensor", tp, 1)
            made["near"] = near + swap(near, "tensor", tp, 2)

    def far_join(name):
        keep[name] = run(
            far_join_kernel, "far_join", [place, keep[name], got[name]],
            [part(keep[name].shape[0])] * 2, hold=2, smem=(0,), flops=cost(f"{name}4"),
        )
        send(name, *keep[name], 1)

    def join(name):
        keep[name] = run(
            partial(join_kernel, step=1), "join", parts(name),
            [part(2 * k.shape[0]) for k in keep[name]], hold=2, smem=(0,), flops=cost(f"{name}5"),
        )
        send(name, *keep[name], 0)

    def finish_p():
        made["p"] = run(
            partial(join_kernel, step=0), "grads", parts("p"),
            [like((hidden, width), f32), like((width, hidden), f32)], hold=2, smem=(0,),
            flops=cost("p6"),
        )

    def finish_q():
        made["q"] = run(
            spread_kernel, "spread", parts("q"),
            [like((wq.shape[0], width), f32), like((inner, width), f32)], hold=2, smem=(0,),
            flops=cost("q6"),
        )

    def attend_back():
        (made["dqkv"],) = run(
            attend_back_kernel, "attend_back",
            [place, lo, start, qkv, mixed, do0, do1, do2, lse, cosine, sine],
            [like((heads, 3, HEAD_DIM, seq), bf16)], hold=4,
            scratch=[
                pltpu.VMEM((inner, seq), bf16),
                pltpu.VMEM((heads, seq, HEAD_DIM), bf16), pltpu.VMEM((heads, seq, HEAD_DIM), bf16),
                pltpu.VMEM((heads, HEAD_DIM, seq), f32), pltpu.VMEM((heads, HEAD_DIM, seq), f32),
            ],
            smem=(0, 1), limit=20, flops=cost("attend_back"),
        )

    def qkv_end():
        count = (wq.shape[0] + inner) // 4
        ka, sa, kb, sb = run(
            qkv_end_kernel, "qkv_end",
            [place, made["dqkv"], xh0, xh1, xh2, wq, gain1, bias1, mixed, dy0, dy1, dy2, dy3],
            [part(count + tail)] * 2 + [part(count)] * 2, hold=1,
            scratch=[pltpu.VMEM((4 * count, width), bf16)], smem=(0,), limit=12,
            flops=cost("qkv_end"),
        )
        keep["q"] = ka, kb
        send("q", sa, sb, 0)

    def sides():
        *made["sides"], sent = run(
            sides_kernel, "sides",
            [made["dqkv"], back0, back1, back2, wq, gain1, mixed, out0, out1, out2, dense_weight],
            [like((rows, width), f32)] * 4 + [like((4 * rows, width), bf16)],
            hold=0, limit=12, flops=cost("sides"),
        )
        made["crossed"] = swap(sent, "tensor", tp, 1)

    def forward():
        _, far_out, _, far_back = made["sides"]
        (sent,) = run(
            forward_kernel, "forward", [far_out, far_back, made["crossed"]],
            [like((2 * rows, width), bf16)], hold=2, flops=cost("forward"),
        )
        made["far"] = swap(sent, "tensor", tp, 2)

    def result():
        (made["result"],) = run(
            result_kernel, "result",
            [x0, made["sides"][0], made["crossed"], made["far"], dense_bias, fc_out_bias],
            [like((rows, width), bf16)], hold=3, flops=cost("result"),
        )

    def tokens_grad():
        (made["tokens_grad"],) = run(
            tokens_grad_kernel, "tokens_grad",
            [x0, dy0, made["sides"][2], made["crossed"], made["far"]],
            [like((rows, width), f32)], hold=4, flops=cost("tokens_grad"),
        )

    def finish_vectors():
        flat = like((width,), f32)
        made["vectors"] = run(
            vectors_kernel, "vectors", [made["near"], vectors["p"], vectors["q"]],
            [flat] * 7 + [like((wq.shape[0],), f32)], hold=0, flops=cost("vectors"),
        )

    steps = {
        "attend_back": attend_back, "qkv_end": qkv_end, "sides": sides, "forward": forward,
        "result": result, "tokens_grad": tokens_grad, "vectors": finish_vectors,
        "p6": finish_p, "q6": finish_q,
    }
    for name in "pq":
        for step, act in enumerate((fold, far_fold, complete, far_join, join)):
            steps[f"{name}{step + 1}"] = partial(act, name)
    keep["p"] = k2, k1
    send("p", s2, s1, 0)
    for step in SEQUENCE:
        steps[step]()
    *vectors, bq_grad = made["vectors"]
    (w2_grad, w1_grad), (wq_grad, wd_grad) = made["p"], made["q"]
    result, input_grad = made["result"], made["tokens_grad"]
    gain1_grad, bias1_grad, gain2_grad, bias2_grad, dense_sum, out_sum, du_sum = vectors
    return (
        result[None], input_grad[None], gain1_grad, bias1_grad, gain2_grad, bias2_grad,
        wq_grad.T, bq_grad, wd_grad, dense_sum, w1_grad, du_sum, w2_grad, out_sum,
    )


def solution(mesh):
    split = P("dp", "tensor", None)
    columns, stacked, vector = P(None, "tensor"), P("tensor", None), P("tensor")
    whole = P()
    return jax.shard_map(
        partial(body, mesh.shape["dp"], mesh.shape["tensor"]),
        mesh=mesh,
        in_specs=(
            split, P("dp", None), split, whole, whole, whole, whole, columns, vector, stacked,
            whole, columns, vector, stacked, whole,
        ),
        out_specs=(
            split, split, whole, whole, whole, whole, columns, vector, stacked, whole, columns,
            vector, stacked, whole,
        ),
        check_vma=False,
    )
```

```python
from functools import partial

import jax
import jax.numpy as jnp
import numpy as np
from jax import lax
from jax.experimental import pallas as pl
from jax.experimental.pallas import tpu as pltpu
from jax.sharding import PartitionSpec as P

HEAD_DIM = 64
ROT = 16
SEGS = 8
BLK = 256
NEG = -1e30
LOG2E = 1.4426950408889634
f32, bf16, i32 = jnp.float32, jnp.bfloat16, jnp.int32
VMEM = pl.BlockSpec(memory_space=pltpu.VMEM)
SMEM = pl.BlockSpec(memory_space=pltpu.SMEM)
MIB = 1 << 20
UNIT = 500_000_000
SEQUENCE = (
    "attend_back", "p1", "qkv_end", "p2", "q1", "sides", "q2", "p3",
    "forward", "p4", "q3", "p5", "q4", "result", "tokens_grad", "q5",
    "p6", "vectors", "q6",
)
COSTS = {
    "attend": 10, "attend_back": 14, "ff_back": 4, "front": 2, "p3": 150, "p4": 60,
    "segments": 8, "tokens_grad": 20,
}
ORDER_A, ORDER_B = (0, 1, 2), (1, 0, 2)


def dot(a, b):
    return jnp.dot(a, b, preferred_element_type=f32)


def dot_nt(a, b):
    return lax.dot_general(a, b, (((1,), (1,)), ((), ())), preferred_element_type=f32)


def dot_tn(a, b):
    return lax.dot_general(a, b, (((0,), (0,)), ((), ())), preferred_element_type=f32)


def like(shape, dtype):
    return jax.ShapeDtypeStruct(shape, dtype)


def call(kernel, name, inputs, outs, scratch=(), limit=8, smem=(), smem_out=(), flops=1000):
    return pl.pallas_call(
        kernel,
        out_shape=tuple(outs),
        in_specs=[SMEM if i in smem else VMEM for i in range(len(inputs))],
        out_specs=tuple(SMEM if i in smem_out else VMEM for i in range(len(outs))),
        scratch_shapes=list(scratch),
        compiler_params=pltpu.CompilerParams(vmem_limit_bytes=limit * MIB),
        cost_estimate=pl.CostEstimate(flops=flops, bytes_accessed=1000, transcendentals=0),
        name=name,
    )(*inputs)


def cost(name, times=1):
    return int(COSTS.get(name, 0.002) * times * UNIT)


def after(token, *values):
    return lax.optimization_barrier((token, *values))[1:]


class Chain:
    def __init__(self, token):
        self.token = token

    def __call__(self, kernel, name, inputs, outs, hold, **options):
        inputs = list(inputs)
        (inputs[hold],) = after(self.token, inputs[hold])
        outs = call(kernel, name, inputs, outs, **options)
        self.token = outs[0]
        return outs


def row_of(ref):
    return ref[...].astype(f32).reshape(1, -1)


def column_of(row):
    return jnp.broadcast_to(row, (128, row.shape[1])).T[:, 0:1]


def pair_rows(rows):
    rows = jnp.concatenate(rows, axis=0)
    high = rows.astype(bf16)
    return jnp.concatenate([high, (rows - high.astype(f32)).astype(bf16)], axis=0)


def segments_kernel(ids_ref, first_ref, start_ref, lo_ref):
    ids = ids_ref[...]
    start = jnp.zeros_like(ids)
    begins = []
    for s in range(SEGS):
        begin = jnp.sum(jnp.where(ids < s, 1.0, 0.0)).astype(i32)
        begins.append(begin)
        start = jnp.where(ids == s, begin, start)
    start_ref[...] = start
    for i in range(lo_ref.shape[0]):
        seg = first_ref[0, i * BLK]
        lo = begins[0]
        for s in range(1, SEGS):
            lo = jnp.where(seg == s, begins[s], lo)
        lo_ref[i] = lax.div(lo, BLK)


def front_kernel(place_ref, *refs, first, pieces):
    x_refs, refs = refs[:pieces], refs[pieces:]
    g1_ref, b1_ref, g2_ref, b2_ref, w1_ref, c1_ref, wq_ref, bq_ref, cos_ref, sin_ref = refs[:10]
    xh_ref, act_ref, slope_ref, qkv_ref = refs[10:]
    heads = qkv_ref.shape[0]
    half = ROT // 2
    rows = x_refs[0].shape[0]
    g1, b1, g2, b2, c1 = [row_of(r) for r in (g1_ref, b1_ref, g2_ref, b2_ref, c1_ref)]
    for piece, x_ref in enumerate(x_refs):
        out = slice(piece * rows, (piece + 1) * rows)
        at = (place_ref[0] ^ (first + piece)) * rows
        here = pl.ds(pl.multiple_of(at, 128), rows)
        x = x_ref[...].astype(f32)
        c = x - jnp.mean(x, axis=1, keepdims=True)
        xh = c * lax.rsqrt(jnp.mean(c * c, axis=1, keepdims=True) + 1e-05)
        xh_ref[out, :] = xh.astype(bf16)
        h1 = (xh * g1 + b1).astype(bf16)
        h2 = (xh * g2 + b2).astype(bf16)
        pre = dot(h2, w1_ref[...]) + c1
        qkv = dot_nt(wq_ref[...], h1) + bq_ref[...]
        cosine, sine = cos_ref[:, here], sin_ref[:, here]
        for h in range(heads):
            for part in range(3):
                at = (3 * h + part) * HEAD_DIM
                v = qkv[at : at + HEAD_DIM]
                if part < 2:
                    one, two = v[:half], v[half:ROT]
                    v = jnp.concatenate(
                        [one * cosine - two * sine, two * cosine + one * sine, v[ROT:]], axis=0
                    )
                if part == 0:
                    v = v * HEAD_DIM ** (-0.5)
                qkv_ref[h, part, :, out] = v.astype(bf16)
        cdf = 0.5 + 0.5 * lax.erf(pre * 0.5**0.5)
        pdf = jnp.exp(pre * pre * -0.5) * (2.0 * np.pi) ** -0.5
        act_ref[out, :] = (pre * cdf).astype(bf16)
        slope_ref[out, :] = (cdf + pre * pdf).astype(bf16)


def halves(payload_ref, keep_ref, send_ref, side):
    rows = keep_ref.shape[0]
    keep_ref[...] = payload_ref[pl.ds(pl.multiple_of(side * rows, 16), rows), :]
    send_ref[...] = payload_ref[pl.ds(pl.multiple_of((1 - side) * rows, 16), rows), :]


def bit_of(place_ref, bit):
    return lax.rem(lax.div(place_ref[1], 1 << bit), 2)


def ff_back_kernel(place_ref, *refs, pieces, carried, last):
    dy_refs, refs = refs[:pieces], refs[pieces:]
    act_ref, slope_ref, xh_ref, g2_ref, b2_ref, w1_ref, w2_ref, wd_ref = refs[:8]
    refs = refs[8:]
    if carried:
        w1_in, w2_in, sums_in = refs[:3]
        refs = refs[3:]
    if last:
        out_ref, back_ref, do_ref, k1_ref, s1_ref, k2_ref, s2_ref = refs[:7]
        w1g_ref, w2g_ref, pay_ref = refs[7:]
    else:
        out_ref, back_ref, do_ref, w1g_ref, w2g_ref, sums_ref = refs
    rows = dy_refs[0].shape[0]
    g2 = row_of(g2_ref)
    sums = [sums_in[i : i + 1, :] for i in range(2)] if carried else [0.0, 0.0]
    for piece, dy_ref in enumerate(dy_refs):
        r = slice(piece * rows, (piece + 1) * rows)
        dy = dy_ref[...]
        act = act_ref[r, :]
        du = (dot_nt(dy, w2_ref[...]) * slope_ref[r, :].astype(f32)).astype(bf16)
        w2_part = dot_tn(act, dy)
        w1_part = dot_tn(xh_ref[r, :], du)
        if piece == 0:
            w2g_ref[...] = w2_in[...] + w2_part if carried else w2_part
            w1g_ref[...] = w1_in[...] + w1_part if carried else w1_part
        else:
            w2g_ref[...] += w2_part
            w1g_ref[...] += w1_part
        out_ref[r, :] = dot(act, w2_ref[...]).astype(bf16)
        back_ref[r, :] = (dot_nt(du, w1_ref[...]) * g2).astype(bf16)
        do_ref[:, r] = dot_nt(wd_ref[...], dy).astype(bf16)
        sums[0] = sums[0] + jnp.sum(du.astype(f32), axis=0, keepdims=True)
        sums[1] = sums[1] + jnp.sum(dy.astype(f32), axis=0, keepdims=True)
    if not last:
        sums_ref[0:1, :] = sums[0]
        sums_ref[1:2, :] = sums[1]
    else:
        pay_ref[...] = w2g_ref[...].astype(bf16)
        half = pay_ref.shape[0] // 2
        halves(pay_ref, k2_ref.at[0:half], s2_ref.at[0:half], bit_of(place_ref, ORDER_A[0]))
        du_sum = jnp.broadcast_to(sums[0], (8, sums[0].shape[1]))
        high = du_sum.astype(bf16)
        low = (du_sum - high.astype(f32)).astype(bf16)
        bias = (dot_nt(high, w1_ref[...]) + dot_nt(low, w1_ref[...]))[0:1]
        raw = w1g_ref[...]
        gain = jnp.sum(raw * w1_ref[...].astype(f32), axis=1, keepdims=True)
        gain = jnp.broadcast_to(gain, (gain.shape[0], 128)).T[0:1, :]
        vectors = pair_rows([gain, bias, sums[1], sums[0]])
        k2_ref[half:, :] = vectors
        s2_ref[half:, :] = vectors
        pay_ref[...] = (raw * column_of(g2) + column_of(row_of(b2_ref)) * sums[0]).astype(bf16)
        halves(pay_ref, k1_ref, s1_ref, bit_of(place_ref, ORDER_B[0]))


def blocks(place_ref, count, per):
    def phys(j):
        return pl.ds(
            pl.multiple_of(((lax.div(j, per) ^ place_ref[0]) * per + lax.rem(j, per)) * BLK, BLK),
            BLK,
        )

    return phys


def spans(refs, axis):
    at = 0
    for ref in refs:
        size = ref.shape[axis]
        yield slice(at, at + size), ref
        at += size


def attend_kernel(
    place_ref, lo_ref, start_ref, part0_ref, part1_ref, part2_ref,
    qkv_ref, o_ref, lse_ref, kn_ref,
):
    heads, seq = qkv_ref.shape[0], qkv_ref.shape[3]
    count = seq // BLK
    phys = blocks(place_ref, count, count // 4)
    for at, ref in spans((part0_ref, part1_ref, part2_ref), 3):
        qkv_ref[:, :, :, at] = ref[...]
    for h in range(heads):
        for b in range(count):
            r = slice(b * BLK, (b + 1) * BLK)
            kn_ref[h, r, :] = qkv_ref[h, 1, :, r].T
    ik = lax.broadcasted_iota(i32, (BLK, BLK), 0)
    iq = lax.broadcasted_iota(i32, (BLK, BLK), 1)

    @pl.loop(0, count)
    def _(i):
        qs = phys(i)
        start = start_ref[0:1, pl.ds(pl.multiple_of(i * BLK, BLK), BLK)]

        def step(ks, mask, carry):
            scores = [
                jnp.where(mask, dot(kn_ref[h, ks, :], qkv_ref[h, 0, :, qs]), NEG)
                for h in range(heads)
            ]
            out = []
            for h in range(heads):
                top = jnp.max(scores[h], axis=0, keepdims=True)
                if carry is not None:
                    top = jnp.maximum(top, carry[h][0])
                expo = jnp.exp2(scores[h] * LOG2E - top * LOG2E)
                total = jnp.sum(expo, axis=0, keepdims=True)
                mixed = dot(qkv_ref[h, 2, :, ks], expo.astype(bf16))
                if carry is not None:
                    fade = jnp.exp2((carry[h][0] - top) * LOG2E)
                    total = total + carry[h][1] * fade
                    mixed = mixed + carry[h][2] * fade
                out.append((top, total, mixed))
            return tuple(out)

        carry = step(qs, (ik <= iq) & (ik >= start - i * BLK), None)
        carry = lax.fori_loop(
            lo_ref[i], i, lambda j, c: step(phys(j), ik >= start - j * BLK, c), carry
        )
        for h in range(heads):
            top, total, mixed = carry[h]
            at = slice(h * HEAD_DIM, (h + 1) * HEAD_DIM)
            o_ref[at, qs] = (mixed * (1.0 / total)).astype(bf16)
            lse_ref[h, 0:1, qs] = top * LOG2E + jnp.log2(total)


def chunk(refs, k, rows):
    for at, ref in spans(refs, 0):
        if at.start <= k * rows < at.stop:
            return ref[k * rows - at.start : (k + 1) * rows - at.start, :]


def attend_back_kernel(
    place_ref, lo_ref, start_ref, qkv_ref, o_ref, do0_ref, do1_ref, do2_ref, lse_ref, cos_ref,
    sin_ref, dqkv_ref, do_ref, kn_ref, vn_ref, dk_ref, dv_ref,
):
    heads, seq = qkv_ref.shape[0], qkv_ref.shape[3]
    count = seq // BLK
    phys = blocks(place_ref, count, count // 4)
    half = ROT // 2
    for at, ref in spans((do0_ref, do1_ref, do2_ref), 1):
        do_ref[:, at] = ref[...]
    for h in range(heads):
        for b in range(count):
            r = slice(b * BLK, (b + 1) * BLK)
            kn_ref[h, r, :] = qkv_ref[h, 1, :, r].T
            vn_ref[h, r, :] = qkv_ref[h, 2, :, r].T
    dk_ref[...] = jnp.zeros_like(dk_ref)
    dv_ref[...] = jnp.zeros_like(dv_ref)
    ik = lax.broadcasted_iota(i32, (BLK, BLK), 0)
    iq = lax.broadcasted_iota(i32, (BLK, BLK), 1)

    def unrotate(grad, cosine, sine):
        one, two = grad[:half], grad[half:ROT]
        return jnp.concatenate(
            [one * cosine + two * sine, two * cosine - one * sine, grad[ROT:]], axis=0
        )

    @pl.loop(0, count)
    def _(i):
        qs = phys(i)
        here = pl.ds(pl.multiple_of(i * BLK, BLK), BLK)
        start = start_ref[0:1, here]
        dos = [do_ref[h * HEAD_DIM : (h + 1) * HEAD_DIM, qs] for h in range(heads)]
        delta = [
            jnp.sum(
                dos[h].astype(f32) * o_ref[h * HEAD_DIM : (h + 1) * HEAD_DIM, qs].astype(f32),
                axis=0, keepdims=True,
            )
            for h in range(heads)
        ]
        lse = [lse_ref[h, 0:1, qs] for h in range(heads)]

        def step(ks, mask, carry):
            scores = [
                jnp.where(mask, dot(kn_ref[h, ks, :], qkv_ref[h, 0, :, qs]), NEG)
                for h in range(heads)
            ]
            dprobs = [dot(vn_ref[h, ks, :], dos[h]) for h in range(heads)]
            probs = [jnp.exp2(scores[h] * LOG2E - lse[h]) for h in range(heads)]
            dscores = [(probs[h] * (dprobs[h] - delta[h])).astype(bf16) for h in range(heads)]
            out = []
            for h in range(heads):
                dv_ref[h, :, ks] += dot_nt(dos[h], probs[h].astype(bf16))
                dk_ref[h, :, ks] += dot_nt(qkv_ref[h, 0, :, qs], dscores[h])
                dq = dot(qkv_ref[h, 1, :, ks], dscores[h])
                out.append(dq if carry is None else carry[h] + dq)
            return tuple(out)

        carry = step(qs, (ik <= iq) & (ik >= start - i * BLK), None)
        carry = lax.fori_loop(
            lo_ref[i], i, lambda j, c: step(phys(j), ik >= start - j * BLK, c), carry
        )
        for h in range(heads):
            dq = unrotate(carry[h] * HEAD_DIM ** (-0.5), cos_ref[:, here], sin_ref[:, here])
            dqkv_ref[h, 0, :, qs] = dq.astype(bf16)

    @pl.loop(0, count)
    def _(i):
        qs = phys(i)
        here = pl.ds(pl.multiple_of(i * BLK, BLK), BLK)
        for h in range(heads):
            dk = unrotate(dk_ref[h, :, qs], cos_ref[:, here], sin_ref[:, here])
            dqkv_ref[h, 1, :, qs] = dk.astype(bf16)
            dqkv_ref[h, 2, :, qs] = dv_ref[h, :, qs].astype(bf16)


def qkv_end_kernel(
    place_ref, dqkv_ref, xh0_ref, xh1_ref, xh2_ref, wq_ref, g1_ref, b1_ref,
    o_ref, dy0_ref, dy1_ref, dy2_ref, dy3_ref, ka_ref, sa_ref, kb_ref, sb_ref, pay_ref,
):
    heads, seq = dqkv_ref.shape[0], dqkv_ref.shape[3]
    g1, b1 = row_of(g1_ref), row_of(b1_ref)
    cols = 3 * HEAD_DIM
    gain, bias, bq = 0.0, 0.0, []
    for h in range(heads):
        grad = dqkv_ref[h].reshape(cols, seq)
        raw = None
        for at, ref in spans((xh0_ref, xh1_ref, xh2_ref), 0):
            part = dot(grad[:, at], ref[...])
            raw = part if raw is None else raw + part
        total = jnp.sum(grad.astype(f32), axis=1, keepdims=True)
        bq.append(jnp.broadcast_to(total, (cols, 128)).T[0:1, :])
        pay_ref[h * cols : (h + 1) * cols, :] = (raw * g1 + total * b1).astype(bf16)
        weight = wq_ref[h * cols : (h + 1) * cols, :].astype(f32)
        gain = gain + jnp.sum(weight * raw, axis=0, keepdims=True)
        bias = bias + jnp.sum(weight * total, axis=0, keepdims=True)
    dense = None
    for at, ref in spans((dy0_ref, dy1_ref, dy2_ref, dy3_ref), 0):
        part = dot(o_ref[:, at], ref[...])
        dense = part if dense is None else dense + part
    pay_ref[heads * cols :, :] = dense.astype(bf16)
    width = pay_ref.shape[1]
    zeros = jnp.zeros((1, width - heads * cols), f32)
    vectors = pair_rows([gain, bias, jnp.concatenate(bq + [zeros], axis=1), jnp.zeros((1, width), f32)])
    rows = kb_ref.shape[0]
    top, bottom = pay_ref.at[0 : 2 * rows], pay_ref.at[2 * rows : 4 * rows]
    halves(top, ka_ref.at[0:rows], sa_ref.at[0:rows], bit_of(place_ref, ORDER_A[0]))
    halves(bottom, kb_ref, sb_ref, bit_of(place_ref, ORDER_B[0]))
    ka_ref[rows:, :] = vectors
    sa_ref[rows:, :] = vectors


def sides_kernel(
    dqkv_ref, back0_ref, back1_ref, back2_ref, wq_ref, g1_ref,
    o_ref, out0_ref, out1_ref, out2_ref, wd_ref,
    outn_ref, outf_ref, backn_ref, backf_ref, send_ref,
):
    rows = outn_ref.shape[0]
    g1 = row_of(g1_ref)
    cols = wq_ref.shape[0]
    for k in range(4):
        r = slice(k * rows, (k + 1) * rows)
        back = chunk((back0_ref, back1_ref, back2_ref), k, rows).astype(f32)
        back = back + dot_tn(dqkv_ref[:, :, :, r].reshape(cols, rows), wq_ref[...]) * g1
        out = chunk((out0_ref, out1_ref, out2_ref), k, rows).astype(f32)
        out = out + dot_tn(o_ref[:, r], wd_ref[...])
        for value, keep, place in ((out, (outn_ref, outf_ref), 0), (back, (backn_ref, backf_ref), 2)):
            if k % 2:
                at = (place + k // 2) * rows
                send_ref[at : at + rows, :] = value.astype(bf16)
            else:
                keep[k // 2][...] = value


def forward_kernel(outf_ref, backf_ref, got_ref, sent_ref):
    rows = outf_ref.shape[0]
    for i, ref in enumerate((outf_ref, backf_ref)):
        got = got_ref[(2 * i + 1) * rows : (2 * i + 2) * rows, :].astype(f32)
        sent_ref[i * rows : (i + 1) * rows, :] = (ref[...] + got).astype(bf16)


def result_kernel(x_ref, keep_ref, got_ref, far_ref, bd_ref, c2_ref, out_ref):
    rows = x_ref.shape[0]
    summed = keep_ref[...] + got_ref[:rows, :].astype(f32) + far_ref[:rows, :].astype(f32)
    out_ref[...] = (x_ref[...].astype(f32) + summed + (row_of(bd_ref) + row_of(c2_ref))).astype(bf16)


def tokens_grad_kernel(x_ref, dy_ref, keep_ref, got_ref, far_ref, out_ref):
    rows = x_ref.shape[0]
    grad = keep_ref[...] + got_ref[2 * rows : 3 * rows, :].astype(f32) + far_ref[rows:, :].astype(f32)
    x = x_ref[...].astype(f32)
    c = x - jnp.mean(x, axis=1, keepdims=True)
    inverse = lax.rsqrt(jnp.mean(c * c, axis=1, keepdims=True) + 1e-05)
    xh = c * inverse
    term = grad - jnp.mean(grad, axis=1, keepdims=True)
    term = term - xh * jnp.mean(grad * xh, axis=1, keepdims=True)
    out_ref[...] = dy_ref[...].astype(f32) + inverse * term


def swap(value, axis, size, distance):
    return lax.ppermute(value, axis, [(i, i ^ distance) for i in range(size)])


def unpair(rows):
    rows = rows.astype(f32)
    return rows[0:4, :] + rows[4:8, :]


def half_sum(keep_ref, got_ref, half, rows):
    at = pl.ds(pl.multiple_of(half * rows, 16), rows)
    return (keep_ref[at, :].astype(f32) + got_ref[at, :].astype(f32)).astype(bf16)


def vector_sum(keep_ref, got_ref):
    return unpair(keep_ref[-8:, :]) + unpair(got_ref[-8:, :])


def fold_kernel(place_ref, ka_ref, ga_ref, kb_ref, gb_ref, *outs):
    for keep_ref, got_ref, next_ref, send_ref, order in (
        (ka_ref, ga_ref, outs[0], outs[1], ORDER_A), (kb_ref, gb_ref, outs[2], outs[3], ORDER_B),
    ):
        rows = keep_ref.shape[0] // 16 * 8
        side = bit_of(place_ref, order[1])
        for half, out_ref in ((side, next_ref), (1 - side, send_ref)):
            out_ref[0:rows, :] = half_sum(keep_ref, got_ref, half, rows)
    vectors = pair_rows([vector_sum(ka_ref, ga_ref)])
    outs[0][-8:, :] = vectors
    outs[1][-8:, :] = vectors


def far_fold_kernel(place_ref, ka_ref, ga_ref, kb_ref, gb_ref, next_ref, send_ref):
    side = bit_of(place_ref, ORDER_A[2])
    first = 0
    for keep_ref, got_ref in ((ka_ref, ga_ref), (kb_ref, gb_ref)):
        rows = keep_ref.shape[0] // 16 * 8
        for half, out_ref in ((side, next_ref), (1 - side, send_ref)):
            out_ref[first : first + rows, :] = half_sum(keep_ref, got_ref, half, rows)
        first += rows
    vectors = pair_rows([vector_sum(ka_ref, ga_ref)])
    next_ref[first:, :] = vectors
    send_ref[first:, :] = vectors


def total_kernel(keep_ref, got_ref, out_ref, vector_ref):
    rows = out_ref.shape[0]
    total = keep_ref[0:rows, :].astype(f32) + got_ref[0:rows, :].astype(f32)
    out_ref[...] = total.astype(bf16)
    vector_ref[...] = vector_sum(keep_ref, got_ref)


def put_halves(out_ref, mine, got, side):
    rows = mine.shape[0]
    for half, value in ((side, mine), (1 - side, got)):
        out_ref[pl.ds(pl.multiple_of(half * rows, 16), rows), :] = value.astype(out_ref.dtype)


def far_join_kernel(place_ref, mine_ref, got_ref, a_ref, b_ref):
    side = bit_of(place_ref, ORDER_A[2])
    first = 0
    for out_ref in (a_ref, b_ref):
        r = slice(first, first + out_ref.shape[0] // 2)
        put_halves(out_ref, mine_ref[r, :], got_ref[r, :], side)
        first = r.stop


def join_kernel(place_ref, ma_ref, ga_ref, mb_ref, gb_ref, a_ref, b_ref, *, step):
    put_halves(a_ref, ma_ref[...], ga_ref[...], bit_of(place_ref, ORDER_A[step]))
    put_halves(b_ref, mb_ref[...], gb_ref[...], bit_of(place_ref, ORDER_B[step]))


def spread_kernel(place_ref, ma_ref, ga_ref, mb_ref, gb_ref, wq_ref, wd_ref):
    rows = ma_ref.shape[0]
    put_halves(wq_ref.at[0 : 2 * rows], ma_ref[...], ga_ref[...], bit_of(place_ref, ORDER_A[0]))
    side = bit_of(place_ref, ORDER_B[0])
    mine, got = mb_ref[...].astype(f32), gb_ref[...].astype(f32)
    wq_ref[2 * rows :, :] = jnp.where(side == 0, mine, got)
    wd_ref[...] = jnp.where(side == 0, got, mine)


def vectors_kernel(n0_ref, n1_ref, n2_ref, n3_ref, a_ref, c_ref, *out_refs):
    near = (n0_ref[...] + n1_ref[...]) + (n2_ref[...] + n3_ref[...])
    for i in range(4):
        out_refs[i][...] = near[i : i + 1, :].reshape(-1)
    out_refs[4][...] = a_ref[2:3, :].reshape(-1)
    out_refs[5][...] = a_ref[2:3, :].reshape(-1)
    out_refs[6][...] = a_ref[3:4, :].reshape(-1)
    out_refs[7][...] = c_ref[2:3, : out_refs[7].shape[0]].reshape(-1)


def dp_swap(value, dp, bit):
    return swap(value, "dp", dp, 1 << bit)


def rest_sum(value, dp):
    if dp == 8:
        return value
    groups = [[i + 8 * j for j in range(dp // 8)] for i in range(8)]
    return lax.psum(value.astype(f32), "dp", axis_index_groups=groups).astype(value.dtype)


def rotary_tables(length):
    half = ROT // 2
    freq = np.float32(10000.0) ** (-(np.arange(half, dtype=np.float32) * 2.0) / ROT)
    angle = freq.astype(np.float32)[:, None] * np.arange(length, dtype=np.float32)[None, :]
    return np.cos(angle).astype(np.float32), np.sin(angle).astype(np.float32)


def body(dp, tp, tokens, segment_ids, cotangent, gain1, bias1, gain2, bias2,
         qkv_weight, qkv_bias, dense_weight, dense_bias, fc_in_weight, fc_in_bias,
         fc_out_weight, fc_out_bias):
    assert tp == 4 and dp % 8 == 0
    x0, dy0 = tokens[0], cotangent[0]
    rows, width = x0.shape
    seq = rows * tp
    count = seq // BLK
    wq = qkv_weight.T
    heads = wq.shape[0] // (3 * HEAD_DIM)
    cosine, sine = rotary_tables(seq)
    place = jnp.stack([lax.axis_index("tensor"), lax.axis_index("dp")]).astype(i32)

    x1 = swap(x0, "tensor", tp, 1)
    x2 = swap(x0, "tensor", tp, 2)
    dy1 = swap(dy0, "tensor", tp, 1)
    dy2 = swap(dy0, "tensor", tp, 2)

    bq_column = qkv_bias.astype(f32)[:, None]
    start, lo = call(
        segments_kernel, "segments", [segment_ids, segment_ids],
        [like((1, seq), i32), like((count,), i32)], smem=(1,), smem_out=(1,), flops=cost("segments"),
    )
    (x1,) = after(start, x1)
    hidden, inner = fc_in_weight.shape[1], dense_weight.shape[0]

    def front(xs, first):
        size = rows * len(xs)
        return call(
            partial(front_kernel, first=first, pieces=len(xs)), "front",
            [place, *xs, gain1, bias1, gain2, bias2, fc_in_weight, fc_in_bias, wq, bq_column,
             cosine, sine],
            [like((size, width), bf16), like((size, hidden), bf16), like((size, hidden), bf16),
             like((heads, 3, HEAD_DIM, size), bf16)],
            smem=(0,), limit=16, flops=cost("front", len(xs)),
        )

    def ff_back(dys, act, slope, xh, carry=(), last=False):
        size = rows * len(dys)
        outs = [like((size, width), bf16), like((size, width), bf16), like((inner, size), bf16)]
        full = [like((width, hidden), f32), like((hidden, width), f32)]
        sums = [like((8, width), f32)]
        half = [like((width // 2, hidden), bf16)] * 2 + [like((hidden // 2 + 8, width), bf16)] * 2
        scratch = [
            pltpu.VMEM((width, hidden), f32), pltpu.VMEM((hidden, width), f32),
            pltpu.VMEM((width, hidden), bf16),
        ]
        return call(
            partial(ff_back_kernel, pieces=len(dys), carried=bool(carry), last=last), "ff_back",
            [place, *dys, act, slope, xh, gain2, bias2, fc_in_weight, fc_out_weight, dense_weight,
             *carry],
            outs + (half if last else full + sums), scratch if last else [],
            smem=(0,), limit=22 if last else 16, flops=cost("ff_back", len(dys)),
        )

    xh0, act0, slope0, qkv0 = front((x0, x1), 0)
    (act0,) = after(qkv0, act0)
    out0, back0, do0, *carry = ff_back((dy0, dy1), act0, slope0, xh0)
    x3 = swap(*after(carry[2], x2), "tensor", tp, 1)
    (x2,) = after(carry[2], x2)
    xh1, act1, slope1, qkv1 = front((x2,), 2)
    (x3,) = after(qkv1, x3)
    xh2, act2, slope2, qkv2 = front((x3,), 3)
    qkv, mixed, lse = call(
        attend_kernel, "attend", [place, lo, start, qkv0, qkv1, qkv2],
        [like((heads, 3, HEAD_DIM, seq), bf16), like((inner, seq), bf16), like((heads, 1, seq), f32)],
        [pltpu.VMEM((heads, seq, HEAD_DIM), bf16)],
        smem=(0, 1), limit=12, flops=cost("attend"),
    )
    dy3 = swap(*after(lse, dy2), "tensor", tp, 1)
    (dy2,) = after(lse, dy2)
    out1, back1, do1, *carry = ff_back((dy2,), act1, slope1, xh1, carry)
    (dy3,) = after(carry[2], dy3)
    out2, back2, do2, k1, s1, k2, s2 = ff_back((dy3,), act2, slope2, xh2, carry, last=True)

    run = Chain(do2)
    tail = 8
    keep, got, vectors, made = {}, {}, {}, {}

    def part(count):
        return like((count, width), bf16)

    def send(name, a, b, step):
        got[name] = [dp_swap(a, dp, ORDER_A[step]), dp_swap(b, dp, ORDER_B[step])]

    def parts(name):
        (ka, kb), (ga, gb) = keep[name], got[name]
        return [place, ka, ga, kb, gb]

    def fold(name):
        na, nb = keep[name][0].shape[0] // 16 * 8, keep[name][1].shape[0] // 2
        ka, sa, kb, sb = run(
            fold_kernel, "fold", parts(name), [part(na + tail)] * 2 + [part(nb)] * 2,
            hold=2, smem=(0,), flops=cost(f"{name}1"),
        )
        keep[name] = ka, kb
        send(name, sa, sb, 1)

    def far_fold(name):
        count = sum(k.shape[0] // 16 * 8 for k in keep[name]) + tail
        keep[name], sent = run(
            far_fold_kernel, "far_fold", parts(name), [part(count)] * 2, hold=2, smem=(0,),
            flops=cost(f"{name}2"),
        )
        got[name] = dp_swap(sent, dp, ORDER_A[2])

    def complete(name):
        total, vector = run(
            total_kernel, "total", [keep[name], got[name]],
            [part(keep[name].shape[0] - tail), like((4, width), f32)], hold=1,
            flops=cost(f"{name}3"),
        )
        keep[name], vectors[name] = rest_sum(total, dp), rest_sum(vector, dp)
        got[name] = dp_swap(keep[name], dp, ORDER_A[2])
        if len(vectors) == 2:
            near = jnp.concatenate([vectors["q"][:2], vectors["p"][:2]], axis=0)
            made["near"] = [near] + [swap(near, "tensor", tp, k) for k in range(1, tp)]

    def far_join(name):
        keep[name] = run(
            far_join_kernel, "far_join", [place, keep[name], got[name]],
            [part(keep[name].shape[0])] * 2, hold=2, smem=(0,), flops=cost(f"{name}4"),
        )
        send(name, *keep[name], 1)

    def join(name):
        keep[name] = run(
            partial(join_kernel, step=1), "join", parts(name),
            [part(2 * k.shape[0]) for k in keep[name]], hold=2, smem=(0,), flops=cost(f"{name}5"),
        )
        send(name, *keep[name], 0)

    def finish_p():
        made["p"] = run(
            partial(join_kernel, step=0), "grads", parts("p"),
            [like((hidden, width), f32), like((width, hidden), f32)], hold=2, smem=(0,),
            flops=cost("p6"),
        )

    def finish_q():
        made["q"] = run(
            spread_kernel, "spread", parts("q"),
            [like((wq.shape[0], width), f32), like((inner, width), f32)], hold=2, smem=(0,),
            flops=cost("q6"),
        )

    def attend_back():
        (made["dqkv"],) = run(
            attend_back_kernel, "attend_back",
            [place, lo, start, qkv, mixed, do0, do1, do2, lse, cosine, sine],
            [like((heads, 3, HEAD_DIM, seq), bf16)], hold=4,
            scratch=[
                pltpu.VMEM((inner, seq), bf16),
                pltpu.VMEM((heads, seq, HEAD_DIM), bf16), pltpu.VMEM((heads, seq, HEAD_DIM), bf16),
                pltpu.VMEM((heads, HEAD_DIM, seq), f32), pltpu.VMEM((heads, HEAD_DIM, seq), f32),
            ],
            smem=(0, 1), limit=20, flops=cost("attend_back"),
        )

    def qkv_end():
        count = (wq.shape[0] + inner) // 4
        ka, sa, kb, sb = run(
            qkv_end_kernel, "qkv_end",
            [place, made["dqkv"], xh0, xh1, xh2, wq, gain1, bias1, mixed, dy0, dy1, dy2, dy3],
            [part(count + tail)] * 2 + [part(count)] * 2, hold=1,
            scratch=[pltpu.VMEM((4 * count, width), bf16)], smem=(0,), limit=12,
            flops=cost("qkv_end"),
        )
        keep["q"] = ka, kb
        send("q", sa, sb, 0)

    def sides():
        *made["sides"], sent = run(
            sides_kernel, "sides",
            [made["dqkv"], back0, back1, back2, wq, gain1, mixed, out0, out1, out2, dense_weight],
            [like((rows, width), f32)] * 4 + [like((4 * rows, width), bf16)],
            hold=0, limit=12, flops=cost("sides"),
        )
        made["crossed"] = swap(sent, "tensor", tp, 1)

    def forward():
        _, far_out, _, far_back = made["sides"]
        (sent,) = run(
            forward_kernel, "forward", [far_out, far_back, made["crossed"]],
            [like((2 * rows, width), bf16)], hold=2, flops=cost("forward"),
        )
        made["far"] = swap(sent, "tensor", tp, 2)

    def result():
        (made["result"],) = run(
            result_kernel, "result",
            [x0, made["sides"][0], made["crossed"], made["far"], dense_bias, fc_out_bias],
            [like((rows, width), bf16)], hold=3, flops=cost("result"),
        )

    def tokens_grad():
        (made["tokens_grad"],) = run(
            tokens_grad_kernel, "tokens_grad",
            [x0, dy0, made["sides"][2], made["crossed"], made["far"]],
            [like((rows, width), f32)], hold=4, flops=cost("tokens_grad"),
        )

    def finish_vectors():
        flat = like((width,), f32)
        made["vectors"] = run(
            vectors_kernel, "vectors", [*made["near"], vectors["p"], vectors["q"]],
            [flat] * 7 + [like((wq.shape[0],), f32)], hold=0, flops=cost("vectors"),
        )

    steps = {
        "attend_back": attend_back, "qkv_end": qkv_end, "sides": sides, "forward": forward,
        "result": result, "tokens_grad": tokens_grad, "vectors": finish_vectors,
        "p6": finish_p, "q6": finish_q,
    }
    for name in "pq":
        for step, act in enumerate((fold, far_fold, complete, far_join, join)):
            steps[f"{name}{step + 1}"] = partial(act, name)
    keep["p"] = k2, k1
    send("p", s2, s1, 0)
    for step in SEQUENCE:
        steps[step]()
    *vectors, bq_grad = made["vectors"]
    (w2_grad, w1_grad), (wq_grad, wd_grad) = made["p"], made["q"]
    result, input_grad = made["result"], made["tokens_grad"]
    gain1_grad, bias1_grad, gain2_grad, bias2_grad, dense_sum, out_sum, du_sum = vectors
    return (
        result[None], input_grad[None], gain1_grad, bias1_grad, gain2_grad, bias2_grad,
        wq_grad.T, bq_grad, wd_grad, dense_sum, w1_grad, du_sum, w2_grad, out_sum,
    )


def solution(mesh):
    split = P("dp", "tensor", None)
    columns, stacked, vector = P(None, "tensor"), P("tensor", None), P("tensor")
    whole = P()
    return jax.shard_map(
        partial(body, mesh.shape["dp"], mesh.shape["tensor"]),
        mesh=mesh,
        in_specs=(
            split, P("dp", None), split, whole, whole, whole, whole, columns, vector, stacked,
            whole, columns, vector, stacked, whole,
        ),
        out_specs=(
            split, split, whole, whole, whole, whole, columns, vector, stacked, whole, columns,
            vector, stacked, whole,
        ),
        check_vma=False,
    )
```

```python
from functools import partial

import jax
import jax.numpy as jnp
import numpy as np
from jax import lax
from jax.experimental import pallas as pl
from jax.experimental.pallas import tpu as pltpu
from jax.sharding import PartitionSpec as P

HEAD_DIM = 64
ROT = 16
SEGS = 8
BLK = 256
NEG = -1e30
LOG2E = 1.4426950408889634
f32, bf16, i32 = jnp.float32, jnp.bfloat16, jnp.int32
VMEM = pl.BlockSpec(memory_space=pltpu.VMEM)
SMEM = pl.BlockSpec(memory_space=pltpu.SMEM)
MIB = 1 << 20
UNIT = 500_000_000
SEQUENCE = (
    "attend_back", "p1", "qkv_end", "p2", "q1", "sides", "q2", "p3",
    "forward", "p4", "q3", "p5", "q4", "result", "tokens_grad", "vectors",
    "q5", "p6", "q6",
)
COSTS = {
    "attend": 10, "attend_back": 14, "ff_back": 4, "front": 2, "p3": 150, "p4": 60,
    "segments": 8, "tokens_grad": 20,
}
ORDER_A, ORDER_B = (0, 1, 2), (1, 0, 2)


def dot(a, b):
    return jnp.dot(a, b, preferred_element_type=f32)


def dot_nt(a, b):
    return lax.dot_general(a, b, (((1,), (1,)), ((), ())), preferred_element_type=f32)


def dot_tn(a, b):
    return lax.dot_general(a, b, (((0,), (0,)), ((), ())), preferred_element_type=f32)


def like(shape, dtype):
    return jax.ShapeDtypeStruct(shape, dtype)


def call(kernel, name, inputs, outs, scratch=(), limit=8, smem=(), smem_out=(), flops=1000):
    return pl.pallas_call(
        kernel,
        out_shape=tuple(outs),
        in_specs=[SMEM if i in smem else VMEM for i in range(len(inputs))],
        out_specs=tuple(SMEM if i in smem_out else VMEM for i in range(len(outs))),
        scratch_shapes=list(scratch),
        compiler_params=pltpu.CompilerParams(vmem_limit_bytes=limit * MIB),
        cost_estimate=pl.CostEstimate(flops=flops, bytes_accessed=1000, transcendentals=0),
        name=name,
    )(*inputs)


def cost(name, times=1):
    return int(COSTS.get(name, 0.002) * times * UNIT)


def after(token, *values):
    return lax.optimization_barrier((token, *values))[1:]


class Chain:
    def __init__(self, token):
        self.token = token

    def __call__(self, kernel, name, inputs, outs, hold, **options):
        inputs = list(inputs)
        (inputs[hold],) = after(self.token, inputs[hold])
        outs = call(kernel, name, inputs, outs, **options)
        self.token = outs[0]
        return outs


def row_of(ref):
    return ref[...].astype(f32).reshape(1, -1)


def column_of(row):
    return jnp.broadcast_to(row, (128, row.shape[1])).T[:, 0:1]


def pair_rows(rows):
    rows = jnp.concatenate(rows, axis=0)
    high = rows.astype(bf16)
    return jnp.concatenate([high, (rows - high.astype(f32)).astype(bf16)], axis=0)


def segments_kernel(ids_ref, first_ref, start_ref, lo_ref):
    ids = ids_ref[...]
    start = jnp.zeros_like(ids)
    begins = []
    for s in range(SEGS):
        begin = jnp.sum(jnp.where(ids < s, 1.0, 0.0)).astype(i32)
        begins.append(begin)
        start = jnp.where(ids == s, begin, start)
    start_ref[...] = start
    for i in range(lo_ref.shape[0]):
        seg = first_ref[0, i * BLK]
        lo = begins[0]
        for s in range(1, SEGS):
            lo = jnp.where(seg == s, begins[s], lo)
        lo_ref[i] = lax.div(lo, BLK)


def front_kernel(place_ref, *refs, first, pieces):
    x_refs, refs = refs[:pieces], refs[pieces:]
    g1_ref, b1_ref, g2_ref, b2_ref, w1_ref, c1_ref, wq_ref, bq_ref, cos_ref, sin_ref = refs[:10]
    xh_ref, act_ref, slope_ref, qkv_ref = refs[10:]
    heads = qkv_ref.shape[0]
    half = ROT // 2
    rows = x_refs[0].shape[0]
    g1, b1, g2, b2, c1 = [row_of(r) for r in (g1_ref, b1_ref, g2_ref, b2_ref, c1_ref)]
    for piece, x_ref in enumerate(x_refs):
        out = slice(piece * rows, (piece + 1) * rows)
        at = (place_ref[0] ^ (first + piece)) * rows
        here = pl.ds(pl.multiple_of(at, 128), rows)
        x = x_ref[...].astype(f32)
        c = x - jnp.mean(x, axis=1, keepdims=True)
        xh = c * lax.rsqrt(jnp.mean(c * c, axis=1, keepdims=True) + 1e-05)
        xh_ref[out, :] = xh.astype(bf16)
        h1 = (xh * g1 + b1).astype(bf16)
        h2 = (xh * g2 + b2).astype(bf16)
        pre = dot(h2, w1_ref[...]) + c1
        qkv = dot_nt(wq_ref[...], h1) + bq_ref[...]
        cosine, sine = cos_ref[:, here], sin_ref[:, here]
        for h in range(heads):
            for part in range(3):
                at = (3 * h + part) * HEAD_DIM
                v = qkv[at : at + HEAD_DIM]
                if part < 2:
                    one, two = v[:half], v[half:ROT]
                    v = jnp.concatenate(
                        [one * cosine - two * sine, two * cosine + one * sine, v[ROT:]], axis=0
                    )
                if part == 0:
                    v = v * HEAD_DIM ** (-0.5)
                qkv_ref[h, part, :, out] = v.astype(bf16)
        cdf = 0.5 + 0.5 * lax.erf(pre * 0.5**0.5)
        pdf = jnp.exp(pre * pre * -0.5) * (2.0 * np.pi) ** -0.5
        act_ref[out, :] = (pre * cdf).astype(bf16)
        slope_ref[out, :] = (cdf + pre * pdf).astype(bf16)


def halves(payload_ref, keep_ref, send_ref, side):
    rows = keep_ref.shape[0]
    keep_ref[...] = payload_ref[pl.ds(pl.multiple_of(side * rows, 16), rows), :]
    send_ref[...] = payload_ref[pl.ds(pl.multiple_of((1 - side) * rows, 16), rows), :]


def bit_of(place_ref, bit):
    return lax.rem(lax.div(place_ref[1], 1 << bit), 2)


def ff_back_kernel(place_ref, *refs, pieces, carried, last):
    dy_refs, refs = refs[:pieces], refs[pieces:]
    act_ref, slope_ref, xh_ref, g2_ref, b2_ref, w1_ref, w2_ref, wd_ref = refs[:8]
    refs = refs[8:]
    if carried:
        w1_in, w2_in, sums_in = refs[:3]
        refs = refs[3:]
    if last:
        out_ref, back_ref, do_ref, k1_ref, s1_ref, k2_ref, s2_ref = refs[:7]
        w1g_ref, w2g_ref, pay_ref = refs[7:]
    else:
        out_ref, back_ref, do_ref, w1g_ref, w2g_ref, sums_ref = refs
    rows = dy_refs[0].shape[0]
    g2 = row_of(g2_ref)
    sums = [sums_in[i : i + 1, :] for i in range(2)] if carried else [0.0, 0.0]
    for piece, dy_ref in enumerate(dy_refs):
        r = slice(piece * rows, (piece + 1) * rows)
        dy = dy_ref[...]
        act = act_ref[r, :]
        du = (dot_nt(dy, w2_ref[...]) * slope_ref[r, :].astype(f32)).astype(bf16)
        w2_part = dot_tn(act, dy)
        w1_part = dot_tn(xh_ref[r, :], du)
        if piece == 0:
            w2g_ref[...] = w2_in[...] + w2_part if carried else w2_part
            w1g_ref[...] = w1_in[...] + w1_part if carried else w1_part
        else:
            w2g_ref[...] += w2_part
            w1g_ref[...] += w1_part
        out_ref[r, :] = dot(act, w2_ref[...]).astype(bf16)
        back_ref[r, :] = (dot_nt(du, w1_ref[...]) * g2).astype(bf16)
        do_ref[:, r] = dot_nt(wd_ref[...], dy).astype(bf16)
        sums[0] = sums[0] + jnp.sum(du.astype(f32), axis=0, keepdims=True)
        sums[1] = sums[1] + jnp.sum(dy.astype(f32), axis=0, keepdims=True)
    if not last:
        sums_ref[0:1, :] = sums[0]
        sums_ref[1:2, :] = sums[1]
    else:
        pay_ref[...] = w2g_ref[...].astype(bf16)
        half = pay_ref.shape[0] // 2
        halves(pay_ref, k2_ref.at[0:half], s2_ref.at[0:half], bit_of(place_ref, ORDER_A[0]))
        du_sum = jnp.broadcast_to(sums[0], (8, sums[0].shape[1]))
        high = du_sum.astype(bf16)
        low = (du_sum - high.astype(f32)).astype(bf16)
        bias = (dot_nt(high, w1_ref[...]) + dot_nt(low, w1_ref[...]))[0:1]
        raw = w1g_ref[...]
        gain = jnp.sum(raw * w1_ref[...].astype(f32), axis=1, keepdims=True)
        gain = jnp.broadcast_to(gain, (gain.shape[0], 128)).T[0:1, :]
        vectors = pair_rows([gain, bias, sums[1], sums[0]])
        k2_ref[half:, :] = vectors
        s2_ref[half:, :] = vectors
        pay_ref[...] = (raw * column_of(g2) + column_of(row_of(b2_ref)) * sums[0]).astype(bf16)
        halves(pay_ref, k1_ref, s1_ref, bit_of(place_ref, ORDER_B[0]))


def blocks(place_ref, count, per):
    def phys(j):
        return pl.ds(
            pl.multiple_of(((lax.div(j, per) ^ place_ref[0]) * per + lax.rem(j, per)) * BLK, BLK),
            BLK,
        )

    return phys


def spans(refs, axis):
    at = 0
    for ref in refs:
        size = ref.shape[axis]
        yield slice(at, at + size), ref
        at += size


def attend_kernel(
    place_ref, lo_ref, start_ref, part0_ref, part1_ref, part2_ref,
    qkv_ref, o_ref, lse_ref, kn_ref,
):
    heads, seq = qkv_ref.shape[0], qkv_ref.shape[3]
    count = seq // BLK
    phys = blocks(place_ref, count, count // 4)
    for at, ref in spans((part0_ref, part1_ref, part2_ref), 3):
        qkv_ref[:, :, :, at] = ref[...]
    for h in range(heads):
        for b in range(count):
            r = slice(b * BLK, (b + 1) * BLK)
            kn_ref[h, r, :] = qkv_ref[h, 1, :, r].T
    ik = lax.broadcasted_iota(i32, (BLK, BLK), 0)
    iq = lax.broadcasted_iota(i32, (BLK, BLK), 1)

    @pl.loop(0, count)
    def _(i):
        qs = phys(i)
        start = start_ref[0:1, pl.ds(pl.multiple_of(i * BLK, BLK), BLK)]

        def step(ks, mask, carry):
            scores = [
                jnp.where(mask, dot(kn_ref[h, ks, :], qkv_ref[h, 0, :, qs]), NEG)
                for h in range(heads)
            ]
            out = []
            for h in range(heads):
                top = jnp.max(scores[h], axis=0, keepdims=True)
                if carry is not None:
                    top = jnp.maximum(top, carry[h][0])
                expo = jnp.exp2(scores[h] * LOG2E - top * LOG2E)
                total = jnp.sum(expo, axis=0, keepdims=True)
                mixed = dot(qkv_ref[h, 2, :, ks], expo.astype(bf16))
                if carry is not None:
                    fade = jnp.exp2((carry[h][0] - top) * LOG2E)
                    total = total + carry[h][1] * fade
                    mixed = mixed + carry[h][2] * fade
                out.append((top, total, mixed))
            return tuple(out)

        carry = step(qs, (ik <= iq) & (ik >= start - i * BLK), None)
        carry = lax.fori_loop(
            lo_ref[i], i, lambda j, c: step(phys(j), ik >= start - j * BLK, c), carry
        )
        for h in range(heads):
            top, total, mixed = carry[h]
            at = slice(h * HEAD_DIM, (h + 1) * HEAD_DIM)
            o_ref[at, qs] = (mixed * (1.0 / total)).astype(bf16)
            lse_ref[h, 0:1, qs] = top * LOG2E + jnp.log2(total)


def chunk(refs, k, rows):
    for at, ref in spans(refs, 0):
        if at.start <= k * rows < at.stop:
            return ref[k * rows - at.start : (k + 1) * rows - at.start, :]


def attend_back_kernel(
    place_ref, lo_ref, start_ref, qkv_ref, o_ref, do0_ref, do1_ref, do2_ref, lse_ref, cos_ref,
    sin_ref, dqkv_ref, do_ref, kn_ref, vn_ref, dk_ref, dv_ref,
):
    heads, seq = qkv_ref.shape[0], qkv_ref.shape[3]
    count = seq // BLK
    phys = blocks(place_ref, count, count // 4)
    half = ROT // 2
    for at, ref in spans((do0_ref, do1_ref, do2_ref), 1):
        do_ref[:, at] = ref[...]
    for h in range(heads):
        for b in range(count):
            r = slice(b * BLK, (b + 1) * BLK)
            kn_ref[h, r, :] = qkv_ref[h, 1, :, r].T
            vn_ref[h, r, :] = qkv_ref[h, 2, :, r].T
    dk_ref[...] = jnp.zeros_like(dk_ref)
    dv_ref[...] = jnp.zeros_like(dv_ref)
    ik = lax.broadcasted_iota(i32, (BLK, BLK), 0)
    iq = lax.broadcasted_iota(i32, (BLK, BLK), 1)

    def unrotate(grad, cosine, sine):
        one, two = grad[:half], grad[half:ROT]
        return jnp.concatenate(
            [one * cosine + two * sine, two * cosine - one * sine, grad[ROT:]], axis=0
        )

    @pl.loop(0, count)
    def _(i):
        qs = phys(i)
        here = pl.ds(pl.multiple_of(i * BLK, BLK), BLK)
        start = start_ref[0:1, here]
        dos = [do_ref[h * HEAD_DIM : (h + 1) * HEAD_DIM, qs] for h in range(heads)]
        delta = [
            jnp.sum(
                dos[h].astype(f32) * o_ref[h * HEAD_DIM : (h + 1) * HEAD_DIM, qs].astype(f32),
                axis=0, keepdims=True,
            )
            for h in range(heads)
        ]
        lse = [lse_ref[h, 0:1, qs] for h in range(heads)]

        def step(ks, mask, carry):
            scores = [
                jnp.where(mask, dot(kn_ref[h, ks, :], qkv_ref[h, 0, :, qs]), NEG)
                for h in range(heads)
            ]
            dprobs = [dot(vn_ref[h, ks, :], dos[h]) for h in range(heads)]
            probs = [jnp.exp2(scores[h] * LOG2E - lse[h]) for h in range(heads)]
            dscores = [(probs[h] * (dprobs[h] - delta[h])).astype(bf16) for h in range(heads)]
            out = []
            for h in range(heads):
                dv_ref[h, :, ks] += dot_nt(dos[h], probs[h].astype(bf16))
                dk_ref[h, :, ks] += dot_nt(qkv_ref[h, 0, :, qs], dscores[h])
                dq = dot(qkv_ref[h, 1, :, ks], dscores[h])
                out.append(dq if carry is None else carry[h] + dq)
            return tuple(out)

        carry = step(qs, (ik <= iq) & (ik >= start - i * BLK), None)
        carry = lax.fori_loop(
            lo_ref[i], i, lambda j, c: step(phys(j), ik >= start - j * BLK, c), carry
        )
        for h in range(heads):
            dq = unrotate(carry[h] * HEAD_DIM ** (-0.5), cos_ref[:, here], sin_ref[:, here])
            dqkv_ref[h, 0, :, qs] = dq.astype(bf16)

    @pl.loop(0, count)
    def _(i):
        qs = phys(i)
        here = pl.ds(pl.multiple_of(i * BLK, BLK), BLK)
        for h in range(heads):
            dk = unrotate(dk_ref[h, :, qs], cos_ref[:, here], sin_ref[:, here])
            dqkv_ref[h, 1, :, qs] = dk.astype(bf16)
            dqkv_ref[h, 2, :, qs] = dv_ref[h, :, qs].astype(bf16)


def qkv_end_kernel(
    place_ref, dqkv_ref, xh0_ref, xh1_ref, xh2_ref, wq_ref, g1_ref, b1_ref,
    o_ref, dy0_ref, dy1_ref, dy2_ref, dy3_ref, ka_ref, sa_ref, kb_ref, sb_ref, pay_ref,
):
    heads, seq = dqkv_ref.shape[0], dqkv_ref.shape[3]
    g1, b1 = row_of(g1_ref), row_of(b1_ref)
    cols = 3 * HEAD_DIM
    gain, bias, bq = 0.0, 0.0, []
    for h in range(heads):
        grad = dqkv_ref[h].reshape(cols, seq)
        raw = None
        for at, ref in spans((xh0_ref, xh1_ref, xh2_ref), 0):
            part = dot(grad[:, at], ref[...])
            raw = part if raw is None else raw + part
        total = jnp.sum(grad.astype(f32), axis=1, keepdims=True)
        bq.append(jnp.broadcast_to(total, (cols, 128)).T[0:1, :])
        pay_ref[h * cols : (h + 1) * cols, :] = (raw * g1 + total * b1).astype(bf16)
        weight = wq_ref[h * cols : (h + 1) * cols, :].astype(f32)
        gain = gain + jnp.sum(weight * raw, axis=0, keepdims=True)
        bias = bias + jnp.sum(weight * total, axis=0, keepdims=True)
    dense = None
    for at, ref in spans((dy0_ref, dy1_ref, dy2_ref, dy3_ref), 0):
        part = dot(o_ref[:, at], ref[...])
        dense = part if dense is None else dense + part
    pay_ref[heads * cols :, :] = dense.astype(bf16)
    width = pay_ref.shape[1]
    zeros = jnp.zeros((1, width - heads * cols), f32)
    vectors = pair_rows([gain, bias, jnp.concatenate(bq + [zeros], axis=1), jnp.zeros((1, width), f32)])
    rows = kb_ref.shape[0]
    top, bottom = pay_ref.at[0 : 2 * rows], pay_ref.at[2 * rows : 4 * rows]
    halves(top, ka_ref.at[0:rows], sa_ref.at[0:rows], bit_of(place_ref, ORDER_A[0]))
    halves(bottom, kb_ref, sb_ref, bit_of(place_ref, ORDER_B[0]))
    ka_ref[rows:, :] = vectors
    sa_ref[rows:, :] = vectors


def sides_kernel(
    dqkv_ref, back0_ref, back1_ref, back2_ref, wq_ref, g1_ref,
    o_ref, out0_ref, out1_ref, out2_ref, wd_ref,
    outn_ref, outf_ref, backn_ref, backf_ref, send_ref,
):
    rows = outn_ref.shape[0]
    g1 = row_of(g1_ref)
    cols = wq_ref.shape[0]
    for k in range(4):
        r = slice(k * rows, (k + 1) * rows)
        back = chunk((back0_ref, back1_ref, back2_ref), k, rows).astype(f32)
        back = back + dot_tn(dqkv_ref[:, :, :, r].reshape(cols, rows), wq_ref[...]) * g1
        out = chunk((out0_ref, out1_ref, out2_ref), k, rows).astype(f32)
        out = out + dot_tn(o_ref[:, r], wd_ref[...])
        for value, keep, place in ((out, (outn_ref, outf_ref), 0), (back, (backn_ref, backf_ref), 2)):
            if k % 2:
                at = (place + k // 2) * rows
                send_ref[at : at + rows, :] = value.astype(bf16)
            else:
                keep[k // 2][...] = value


def forward_kernel(outf_ref, backf_ref, got_ref, sent_ref):
    rows = outf_ref.shape[0]
    for i, ref in enumerate((outf_ref, backf_ref)):
        got = got_ref[(2 * i + 1) * rows : (2 * i + 2) * rows, :].astype(f32)
        sent_ref[i * rows : (i + 1) * rows, :] = (ref[...] + got).astype(bf16)


def result_kernel(x_ref, keep_ref, got_ref, far_ref, bd_ref, c2_ref, out_ref):
    rows = x_ref.shape[0]
    summed = keep_ref[...] + got_ref[:rows, :].astype(f32) + far_ref[:rows, :].astype(f32)
    out_ref[...] = (x_ref[...].astype(f32) + summed + (row_of(bd_ref) + row_of(c2_ref))).astype(bf16)


def tokens_grad_kernel(x_ref, dy_ref, keep_ref, got_ref, far_ref, out_ref):
    rows = x_ref.shape[0]
    grad = keep_ref[...] + got_ref[2 * rows : 3 * rows, :].astype(f32) + far_ref[rows:, :].astype(f32)
    x = x_ref[...].astype(f32)
    c = x - jnp.mean(x, axis=1, keepdims=True)
    inverse = lax.rsqrt(jnp.mean(c * c, axis=1, keepdims=True) + 1e-05)
    xh = c * inverse
    term = grad - jnp.mean(grad, axis=1, keepdims=True)
    term = term - xh * jnp.mean(grad * xh, axis=1, keepdims=True)
    out_ref[...] = dy_ref[...].astype(f32) + inverse * term


def swap(value, axis, size, distance):
    return lax.ppermute(value, axis, [(i, i ^ distance) for i in range(size)])


def unpair(rows):
    rows = rows.astype(f32)
    return rows[0:4, :] + rows[4:8, :]


def half_sum(keep_ref, got_ref, half, rows):
    at = pl.ds(pl.multiple_of(half * rows, 16), rows)
    return (keep_ref[at, :].astype(f32) + got_ref[at, :].astype(f32)).astype(bf16)


def vector_sum(keep_ref, got_ref):
    return unpair(keep_ref[-8:, :]) + unpair(got_ref[-8:, :])


def fold_kernel(place_ref, ka_ref, ga_ref, kb_ref, gb_ref, *outs):
    for keep_ref, got_ref, next_ref, send_ref, order in (
        (ka_ref, ga_ref, outs[0], outs[1], ORDER_A), (kb_ref, gb_ref, outs[2], outs[3], ORDER_B),
    ):
        rows = keep_ref.shape[0] // 16 * 8
        side = bit_of(place_ref, order[1])
        for half, out_ref in ((side, next_ref), (1 - side, send_ref)):
            out_ref[0:rows, :] = half_sum(keep_ref, got_ref, half, rows)
    vectors = pair_rows([vector_sum(ka_ref, ga_ref)])
    outs[0][-8:, :] = vectors
    outs[1][-8:, :] = vectors


def far_fold_kernel(place_ref, ka_ref, ga_ref, kb_ref, gb_ref, next_ref, send_ref):
    side = bit_of(place_ref, ORDER_A[2])
    first = 0
    for keep_ref, got_ref in ((ka_ref, ga_ref), (kb_ref, gb_ref)):
        rows = keep_ref.shape[0] // 16 * 8
        for half, out_ref in ((side, next_ref), (1 - side, send_ref)):
            out_ref[first : first + rows, :] = half_sum(keep_ref, got_ref, half, rows)
        first += rows
    vectors = pair_rows([vector_sum(ka_ref, ga_ref)])
    next_ref[first:, :] = vectors
    send_ref[first:, :] = vectors


def total_kernel(keep_ref, got_ref, out_ref, vector_ref):
    rows = out_ref.shape[0]
    total = keep_ref[0:rows, :].astype(f32) + got_ref[0:rows, :].astype(f32)
    out_ref[...] = total.astype(bf16)
    vector_ref[...] = vector_sum(keep_ref, got_ref)


def put_halves(out_ref, mine, got, side):
    rows = mine.shape[0]
    for half, value in ((side, mine), (1 - side, got)):
        out_ref[pl.ds(pl.multiple_of(half * rows, 16), rows), :] = value.astype(out_ref.dtype)


def far_join_kernel(place_ref, mine_ref, got_ref, a_ref, b_ref):
    side = bit_of(place_ref, ORDER_A[2])
    first = 0
    for out_ref in (a_ref, b_ref):
        r = slice(first, first + out_ref.shape[0] // 2)
        put_halves(out_ref, mine_ref[r, :], got_ref[r, :], side)
        first = r.stop


def join_kernel(place_ref, ma_ref, ga_ref, mb_ref, gb_ref, a_ref, b_ref, *, step):
    put_halves(a_ref, ma_ref[...], ga_ref[...], bit_of(place_ref, ORDER_A[step]))
    put_halves(b_ref, mb_ref[...], gb_ref[...], bit_of(place_ref, ORDER_B[step]))


def spread_kernel(place_ref, ma_ref, ga_ref, mb_ref, gb_ref, wq_ref, wd_ref):
    rows = ma_ref.shape[0]
    put_halves(wq_ref.at[0 : 2 * rows], ma_ref[...], ga_ref[...], bit_of(place_ref, ORDER_A[0]))
    side = bit_of(place_ref, ORDER_B[0])
    mine, got = mb_ref[...].astype(f32), gb_ref[...].astype(f32)
    wq_ref[2 * rows :, :] = jnp.where(side == 0, mine, got)
    wd_ref[...] = jnp.where(side == 0, got, mine)


def vectors_kernel(near_ref, a_ref, c_ref, *out_refs):
    near = (near_ref[0] + near_ref[1]) + (near_ref[2] + near_ref[3])
    for i in range(4):
        out_refs[i][...] = near[i : i + 1, :].reshape(-1)
    out_refs[4][...] = a_ref[2:3, :].reshape(-1)
    out_refs[5][...] = a_ref[2:3, :].reshape(-1)
    out_refs[6][...] = a_ref[3:4, :].reshape(-1)
    out_refs[7][...] = c_ref[2:3, : out_refs[7].shape[0]].reshape(-1)


def dp_swap(value, dp, bit):
    return swap(value, "dp", dp, 1 << bit)


def rest_sum(value, dp):
    if dp == 8:
        return value
    groups = [[i + 8 * j for j in range(dp // 8)] for i in range(8)]
    return lax.psum(value.astype(f32), "dp", axis_index_groups=groups).astype(value.dtype)


def rotary_tables(length):
    half = ROT // 2
    freq = np.float32(10000.0) ** (-(np.arange(half, dtype=np.float32) * 2.0) / ROT)
    angle = freq.astype(np.float32)[:, None] * np.arange(length, dtype=np.float32)[None, :]
    return np.cos(angle).astype(np.float32), np.sin(angle).astype(np.float32)


def body(dp, tp, tokens, segment_ids, cotangent, gain1, bias1, gain2, bias2,
         qkv_weight, qkv_bias, dense_weight, dense_bias, fc_in_weight, fc_in_bias,
         fc_out_weight, fc_out_bias):
    assert tp == 4 and dp % 8 == 0
    x0, dy0 = tokens[0], cotangent[0]
    rows, width = x0.shape
    seq = rows * tp
    count = seq // BLK
    wq = qkv_weight.T
    heads = wq.shape[0] // (3 * HEAD_DIM)
    cosine, sine = rotary_tables(seq)
    place = jnp.stack([lax.axis_index("tensor"), lax.axis_index("dp")]).astype(i32)

    x1 = swap(x0, "tensor", tp, 1)
    x2 = swap(x0, "tensor", tp, 2)
    dy1 = swap(dy0, "tensor", tp, 1)
    dy2 = swap(dy0, "tensor", tp, 2)

    bq_column = qkv_bias.astype(f32)[:, None]
    start, lo = call(
        segments_kernel, "segments", [segment_ids, segment_ids],
        [like((1, seq), i32), like((count,), i32)], smem=(1,), smem_out=(1,), flops=cost("segments"),
    )
    (x1,) = after(start, x1)
    hidden, inner = fc_in_weight.shape[1], dense_weight.shape[0]

    def front(xs, first):
        size = rows * len(xs)
        return call(
            partial(front_kernel, first=first, pieces=len(xs)), "front",
            [place, *xs, gain1, bias1, gain2, bias2, fc_in_weight, fc_in_bias, wq, bq_column,
             cosine, sine],
            [like((size, width), bf16), like((size, hidden), bf16), like((size, hidden), bf16),
             like((heads, 3, HEAD_DIM, size), bf16)],
            smem=(0,), limit=16, flops=cost("front", len(xs)),
        )

    def ff_back(dys, act, slope, xh, carry=(), last=False):
        size = rows * len(dys)
        outs = [like((size, width), bf16), like((size, width), bf16), like((inner, size), bf16)]
        full = [like((width, hidden), f32), like((hidden, width), f32)]
        sums = [like((8, width), f32)]
        half = [like((width // 2, hidden), bf16)] * 2 + [like((hidden // 2 + 8, width), bf16)] * 2
        scratch = [
            pltpu.VMEM((width, hidden), f32), pltpu.VMEM((hidden, width), f32),
            pltpu.VMEM((width, hidden), bf16),
        ]
        return call(
            partial(ff_back_kernel, pieces=len(dys), carried=bool(carry), last=last), "ff_back",
            [place, *dys, act, slope, xh, gain2, bias2, fc_in_weight, fc_out_weight, dense_weight,
             *carry],
            outs + (half if last else full + sums), scratch if last else [],
            smem=(0,), limit=22 if last else 16, flops=cost("ff_back", len(dys)),
        )

    xh0, act0, slope0, qkv0 = front((x0, x1), 0)
    (act0,) = after(qkv0, act0)
    out0, back0, do0, *carry = ff_back((dy0, dy1), act0, slope0, xh0)
    x3 = swap(*after(carry[2], x2), "tensor", tp, 1)
    (x2,) = after(carry[2], x2)
    xh1, act1, slope1, qkv1 = front((x2,), 2)
    (x3,) = after(qkv1, x3)
    xh2, act2, slope2, qkv2 = front((x3,), 3)
    qkv, mixed, lse = call(
        attend_kernel, "attend", [place, lo, start, qkv0, qkv1, qkv2],
        [like((heads, 3, HEAD_DIM, seq), bf16), like((inner, seq), bf16), like((heads, 1, seq), f32)],
        [pltpu.VMEM((heads, seq, HEAD_DIM), bf16)],
        smem=(0, 1), limit=12, flops=cost("attend"),
    )
    dy3 = swap(*after(lse, dy2), "tensor", tp, 1)
    (dy2,) = after(lse, dy2)
    out1, back1, do1, *carry = ff_back((dy2,), act1, slope1, xh1, carry)
    (dy3,) = after(carry[2], dy3)
    out2, back2, do2, k1, s1, k2, s2 = ff_back((dy3,), act2, slope2, xh2, carry, last=True)

    run = Chain(do2)
    tail = 8
    keep, got, vectors, made = {}, {}, {}, {}

    def part(count):
        return like((count, width), bf16)

    def send(name, a, b, step):
        got[name] = [dp_swap(a, dp, ORDER_A[step]), dp_swap(b, dp, ORDER_B[step])]

    def parts(name):
        (ka, kb), (ga, gb) = keep[name], got[name]
        return [place, ka, ga, kb, gb]

    def fold(name):
        na, nb = keep[name][0].shape[0] // 16 * 8, keep[name][1].shape[0] // 2
        ka, sa, kb, sb = run(
            fold_kernel, "fold", parts(name), [part(na + tail)] * 2 + [part(nb)] * 2,
            hold=2, smem=(0,), flops=cost(f"{name}1"),
        )
        keep[name] = ka, kb
        send(name, sa, sb, 1)

    def far_fold(name):
        count = sum(k.shape[0] // 16 * 8 for k in keep[name]) + tail
        keep[name], sent = run(
            far_fold_kernel, "far_fold", parts(name), [part(count)] * 2, hold=2, smem=(0,),
            flops=cost(f"{name}2"),
        )
        got[name] = dp_swap(sent, dp, ORDER_A[2])

    def complete(name):
        total, vector = run(
            total_kernel, "total", [keep[name], got[name]],
            [part(keep[name].shape[0] - tail), like((4, width), f32)], hold=1,
            flops=cost(f"{name}3"),
        )
        keep[name], vectors[name] = rest_sum(total, dp), rest_sum(vector, dp)
        got[name] = dp_swap(keep[name], dp, ORDER_A[2])
        if len(vectors) == 2:
            near = jnp.concatenate([vectors["q"][:2], vectors["p"][:2]], axis=0)
            made["near"] = lax.all_to_all(jnp.broadcast_to(near, (tp, *near.shape)), "tensor", 0, 0)

    def far_join(name):
        keep[name] = run(
            far_join_kernel, "far_join", [place, keep[name], got[name]],
            [part(keep[name].shape[0])] * 2, hold=2, smem=(0,), flops=cost(f"{name}4"),
        )
        send(name, *keep[name], 1)

    def join(name):
        keep[name] = run(
            partial(join_kernel, step=1), "join", parts(name),
            [part(2 * k.shape[0]) for k in keep[name]], hold=2, smem=(0,), flops=cost(f"{name}5"),
        )
        send(name, *keep[name], 0)

    def finish_p():
        made["p"] = run(
            partial(join_kernel, step=0), "grads", parts("p"),
            [like((hidden, width), f32), like((width, hidden), f32)], hold=2, smem=(0,),
            flops=cost("p6"),
        )

    def finish_q():
        made["q"] = run(
            spread_kernel, "spread", parts("q"),
            [like((wq.shape[0], width), f32), like((inner, width), f32)], hold=2, smem=(0,),
            flops=cost("q6"),
        )

    def attend_back():
        (made["dqkv"],) = run(
            attend_back_kernel, "attend_back",
            [place, lo, start, qkv, mixed, do0, do1, do2, lse, cosine, sine],
            [like((heads, 3, HEAD_DIM, seq), bf16)], hold=4,
            scratch=[
                pltpu.VMEM((inner, seq), bf16),
                pltpu.VMEM((heads, seq, HEAD_DIM), bf16), pltpu.VMEM((heads, seq, HEAD_DIM), bf16),
                pltpu.VMEM((heads, HEAD_DIM, seq), f32), pltpu.VMEM((heads, HEAD_DIM, seq), f32),
            ],
            smem=(0, 1), limit=20, flops=cost("attend_back"),
        )

    def qkv_end():
        count = (wq.shape[0] + inner) // 4
        ka, sa, kb, sb = run(
            qkv_end_kernel, "qkv_end",
            [place, made["dqkv"], xh0, xh1, xh2, wq, gain1, bias1, mixed, dy0, dy1, dy2, dy3],
            [part(count + tail)] * 2 + [part(count)] * 2, hold=1,
            scratch=[pltpu.VMEM((4 * count, width), bf16)], smem=(0,), limit=12,
            flops=cost("qkv_end"),
        )
        keep["q"] = ka, kb
        send("q", sa, sb, 0)

    def sides():
        *made["sides"], sent = run(
            sides_kernel, "sides",
            [made["dqkv"], back0, back1, back2, wq, gain1, mixed, out0, out1, out2, dense_weight],
            [like((rows, width), f32)] * 4 + [like((4 * rows, width), bf16)],
            hold=0, limit=12, flops=cost("sides"),
        )
        made["crossed"] = swap(sent, "tensor", tp, 1)

    def forward():
        _, far_out, _, far_back = made["sides"]
        (sent,) = run(
            forward_kernel, "forward", [far_out, far_back, made["crossed"]],
            [like((2 * rows, width), bf16)], hold=2, flops=cost("forward"),
        )
        made["far"] = swap(sent, "tensor", tp, 2)

    def result():
        (made["result"],) = run(
            result_kernel, "result",
            [x0, made["sides"][0], made["crossed"], made["far"], dense_bias, fc_out_bias],
            [like((rows, width), bf16)], hold=3, flops=cost("result"),
        )

    def tokens_grad():
        (made["tokens_grad"],) = run(
            tokens_grad_kernel, "tokens_grad",
            [x0, dy0, made["sides"][2], made["crossed"], made["far"]],
            [like((rows, width), f32)], hold=4, flops=cost("tokens_grad"),
        )

    def finish_vectors():
        flat = like((width,), f32)
        made["vectors"] = run(
            vectors_kernel, "vectors", [made["near"], vectors["p"], vectors["q"]],
            [flat] * 7 + [like((wq.shape[0],), f32)], hold=0, flops=cost("vectors"),
        )

    steps = {
        "attend_back": attend_back, "qkv_end": qkv_end, "sides": sides, "forward": forward,
        "result": result, "tokens_grad": tokens_grad, "vectors": finish_vectors,
        "p6": finish_p, "q6": finish_q,
    }
    for name in "pq":
        for step, act in enumerate((fold, far_fold, complete, far_join, join)):
            steps[f"{name}{step + 1}"] = partial(act, name)
    keep["p"] = k2, k1
    send("p", s2, s1, 0)
    for step in SEQUENCE:
        steps[step]()
    *vectors, bq_grad = made["vectors"]
    (w2_grad, w1_grad), (wq_grad, wd_grad) = made["p"], made["q"]
    result, input_grad = made["result"], made["tokens_grad"]
    gain1_grad, bias1_grad, gain2_grad, bias2_grad, dense_sum, out_sum, du_sum = vectors
    return (
        result[None], input_grad[None], gain1_grad, bias1_grad, gain2_grad, bias2_grad,
        wq_grad.T, bq_grad, wd_grad, dense_sum, w1_grad, du_sum, w2_grad, out_sum,
    )


def solution(mesh):
    split = P("dp", "tensor", None)
    columns, stacked, vector = P(None, "tensor"), P("tensor", None), P("tensor")
    whole = P()
    return jax.shard_map(
        partial(body, mesh.shape["dp"], mesh.shape["tensor"]),
        mesh=mesh,
        in_specs=(
            split, P("dp", None), split, whole, whole, whole, whole, columns, vector, stacked,
            whole, columns, vector, stacked, whole,
        ),
        out_specs=(
            split, split, whole, whole, whole, whole, columns, vector, stacked, whole, columns,
            vector, stacked, whole,
        ),
        check_vma=False,
    )
```

```python
from functools import partial

import jax
import jax.numpy as jnp
import numpy as np
from jax import lax
from jax.experimental import pallas as pl
from jax.experimental.pallas import tpu as pltpu
from jax.sharding import PartitionSpec as P

HEAD_DIM = 64
ROT = 16
SEGS = 8
BLK = 256
NEG = -1e30
LOG2E = 1.4426950408889634
f32, bf16, i32 = jnp.float32, jnp.bfloat16, jnp.int32
VMEM = pl.BlockSpec(memory_space=pltpu.VMEM)
SMEM = pl.BlockSpec(memory_space=pltpu.SMEM)
MIB = 1 << 20
UNIT = 500_000_000
SEQUENCE = (
    "attend_back", "p1", "qkv_end", "p2", "q1", "sides", "q2", "p3",
    "forward", "p4", "q3", "p5", "q4", "result", "tokens_grad", "q5",
    "p6", "q6", "vectors",
)
COSTS = {
    "attend": 10, "attend_back": 14, "ff_back": 4, "front": 2, "p3": 150, "p4": 60,
    "segments": 8, "tokens_grad": 20,
}
ORDER_A, ORDER_B = (0, 1, 2), (1, 0, 2)


def dot(a, b):
    return jnp.dot(a, b, preferred_element_type=f32)


def dot_nt(a, b):
    return lax.dot_general(a, b, (((1,), (1,)), ((), ())), preferred_element_type=f32)


def dot_tn(a, b):
    return lax.dot_general(a, b, (((0,), (0,)), ((), ())), preferred_element_type=f32)


def like(shape, dtype):
    return jax.ShapeDtypeStruct(shape, dtype)


def call(kernel, name, inputs, outs, scratch=(), limit=8, smem=(), smem_out=(), flops=1000):
    return pl.pallas_call(
        kernel,
        out_shape=tuple(outs),
        in_specs=[SMEM if i in smem else VMEM for i in range(len(inputs))],
        out_specs=tuple(SMEM if i in smem_out else VMEM for i in range(len(outs))),
        scratch_shapes=list(scratch),
        compiler_params=pltpu.CompilerParams(vmem_limit_bytes=limit * MIB),
        cost_estimate=pl.CostEstimate(flops=flops, bytes_accessed=1000, transcendentals=0),
        name=name,
    )(*inputs)


def cost(name, times=1):
    return int(COSTS.get(name, 0.002) * times * UNIT)


def after(token, *values):
    return lax.optimization_barrier((token, *values))[1:]


class Chain:
    def __init__(self, token):
        self.token = token

    def __call__(self, kernel, name, inputs, outs, hold, **options):
        inputs = list(inputs)
        (inputs[hold],) = after(self.token, inputs[hold])
        outs = call(kernel, name, inputs, outs, **options)
        self.token = outs[0]
        return outs


def row_of(ref):
    return ref[...].astype(f32).reshape(1, -1)


def column_of(row):
    return jnp.broadcast_to(row, (128, row.shape[1])).T[:, 0:1]


def pair_rows(rows):
    rows = jnp.concatenate(rows, axis=0)
    high = rows.astype(bf16)
    return jnp.concatenate([high, (rows - high.astype(f32)).astype(bf16)], axis=0)


def segments_kernel(ids_ref, first_ref, start_ref, lo_ref):
    ids = ids_ref[...]
    start = jnp.zeros_like(ids)
    begins = []
    for s in range(SEGS):
        begin = jnp.sum(jnp.where(ids < s, 1.0, 0.0)).astype(i32)
        begins.append(begin)
        start = jnp.where(ids == s, begin, start)
    start_ref[...] = start
    for i in range(lo_ref.shape[0]):
        seg = first_ref[0, i * BLK]
        lo = begins[0]
        for s in range(1, SEGS):
            lo = jnp.where(seg == s, begins[s], lo)
        lo_ref[i] = lax.div(lo, BLK)


def front_kernel(place_ref, *refs, first, pieces):
    x_refs, refs = refs[:pieces], refs[pieces:]
    g1_ref, b1_ref, g2_ref, b2_ref, w1_ref, c1_ref, wq_ref, bq_ref, cos_ref, sin_ref = refs[:10]
    xh_ref, act_ref, slope_ref, qkv_ref = refs[10:]
    heads = qkv_ref.shape[0]
    half = ROT // 2
    rows = x_refs[0].shape[0]
    g1, b1, g2, b2, c1 = [row_of(r) for r in (g1_ref, b1_ref, g2_ref, b2_ref, c1_ref)]
    for piece, x_ref in enumerate(x_refs):
        out = slice(piece * rows, (piece + 1) * rows)
        at = (place_ref[0] ^ (first + piece)) * rows
        here = pl.ds(pl.multiple_of(at, 128), rows)
        x = x_ref[...].astype(f32)
        c = x - jnp.mean(x, axis=1, keepdims=True)
        xh = c * lax.rsqrt(jnp.mean(c * c, axis=1, keepdims=True) + 1e-05)
        xh_ref[out, :] = xh.astype(bf16)
        h1 = (xh * g1 + b1).astype(bf16)
        h2 = (xh * g2 + b2).astype(bf16)
        pre = dot(h2, w1_ref[...]) + c1
        qkv = dot_nt(wq_ref[...], h1) + bq_ref[...]
        cosine, sine = cos_ref[:, here], sin_ref[:, here]
        for h in range(heads):
            for part in range(3):
                at = (3 * h + part) * HEAD_DIM
                v = qkv[at : at + HEAD_DIM]
                if part < 2:
                    one, two = v[:half], v[half:ROT]
                    v = jnp.concatenate(
                        [one * cosine - two * sine, two * cosine + one * sine, v[ROT:]], axis=0
                    )
                if part == 0:
                    v = v * HEAD_DIM ** (-0.5)
                qkv_ref[h, part, :, out] = v.astype(bf16)
        cdf = 0.5 + 0.5 * lax.erf(pre * 0.5**0.5)
        pdf = jnp.exp(pre * pre * -0.5) * (2.0 * np.pi) ** -0.5
        act_ref[out, :] = (pre * cdf).astype(bf16)
        slope_ref[out, :] = (cdf + pre * pdf).astype(bf16)


def halves(payload_ref, keep_ref, send_ref, side):
    rows = keep_ref.shape[0]
    keep_ref[...] = payload_ref[pl.ds(pl.multiple_of(side * rows, 16), rows), :]
    send_ref[...] = payload_ref[pl.ds(pl.multiple_of((1 - side) * rows, 16), rows), :]


def bit_of(place_ref, bit):
    return lax.rem(lax.div(place_ref[1], 1 << bit), 2)


def ff_back_kernel(place_ref, *refs, pieces, carried, last):
    dy_refs, refs = refs[:pieces], refs[pieces:]
    act_ref, slope_ref, xh_ref, g2_ref, b2_ref, w1_ref, w2_ref, wd_ref = refs[:8]
    refs = refs[8:]
    if carried:
        w1_in, w2_in, sums_in = refs[:3]
        refs = refs[3:]
    if last:
        out_ref, back_ref, do_ref, k1_ref, s1_ref, k2_ref, s2_ref = refs[:7]
        w1g_ref, w2g_ref, pay_ref = refs[7:]
    else:
        out_ref, back_ref, do_ref, w1g_ref, w2g_ref, sums_ref = refs
    rows = dy_refs[0].shape[0]
    g2 = row_of(g2_ref)
    sums = [sums_in[i : i + 1, :] for i in range(2)] if carried else [0.0, 0.0]
    for piece, dy_ref in enumerate(dy_refs):
        r = slice(piece * rows, (piece + 1) * rows)
        dy = dy_ref[...]
        act = act_ref[r, :]
        du = (dot_nt(dy, w2_ref[...]) * slope_ref[r, :].astype(f32)).astype(bf16)
        w2_part = dot_tn(act, dy)
        w1_part = dot_tn(xh_ref[r, :], du)
        if piece == 0:
            w2g_ref[...] = w2_in[...] + w2_part if carried else w2_part
            w1g_ref[...] = w1_in[...] + w1_part if carried else w1_part
        else:
            w2g_ref[...] += w2_part
            w1g_ref[...] += w1_part
        out_ref[r, :] = dot(act, w2_ref[...]).astype(bf16)
        back_ref[r, :] = (dot_nt(du, w1_ref[...]) * g2).astype(bf16)
        do_ref[:, r] = dot_nt(wd_ref[...], dy).astype(bf16)
        sums[0] = sums[0] + jnp.sum(du.astype(f32), axis=0, keepdims=True)
        sums[1] = sums[1] + jnp.sum(dy.astype(f32), axis=0, keepdims=True)
    if not last:
        sums_ref[0:1, :] = sums[0]
        sums_ref[1:2, :] = sums[1]
    else:
        pay_ref[...] = w2g_ref[...].astype(bf16)
        half = pay_ref.shape[0] // 2
        halves(pay_ref, k2_ref.at[0:half], s2_ref.at[0:half], bit_of(place_ref, ORDER_A[0]))
        du_sum = jnp.broadcast_to(sums[0], (8, sums[0].shape[1]))
        high = du_sum.astype(bf16)
        low = (du_sum - high.astype(f32)).astype(bf16)
        bias = (dot_nt(high, w1_ref[...]) + dot_nt(low, w1_ref[...]))[0:1]
        raw = w1g_ref[...]
        gain = jnp.sum(raw * w1_ref[...].astype(f32), axis=1, keepdims=True)
        gain = jnp.broadcast_to(gain, (gain.shape[0], 128)).T[0:1, :]
        vectors = pair_rows([gain, bias, sums[1], sums[0]])
        k2_ref[half:, :] = vectors
        s2_ref[half:, :] = vectors
        pay_ref[...] = (raw * column_of(g2) + column_of(row_of(b2_ref)) * sums[0]).astype(bf16)
        halves(pay_ref, k1_ref, s1_ref, bit_of(place_ref, ORDER_B[0]))


def blocks(place_ref, count, per):
    def phys(j):
        return pl.ds(
            pl.multiple_of(((lax.div(j, per) ^ place_ref[0]) * per + lax.rem(j, per)) * BLK, BLK),
            BLK,
        )

    return phys


def spans(refs, axis):
    at = 0
    for ref in refs:
        size = ref.shape[axis]
        yield slice(at, at + size), ref
        at += size


def attend_kernel(
    place_ref, lo_ref, start_ref, part0_ref, part1_ref, part2_ref,
    qkv_ref, o_ref, lse_ref, kn_ref,
):
    heads, seq = qkv_ref.shape[0], qkv_ref.shape[3]
    count = seq // BLK
    phys = blocks(place_ref, count, count // 4)
    for at, ref in spans((part0_ref, part1_ref, part2_ref), 3):
        qkv_ref[:, :, :, at] = ref[...]
    for h in range(heads):
        for b in range(count):
            r = slice(b * BLK, (b + 1) * BLK)
            kn_ref[h, r, :] = qkv_ref[h, 1, :, r].T
    ik = lax.broadcasted_iota(i32, (BLK, BLK), 0)
    iq = lax.broadcasted_iota(i32, (BLK, BLK), 1)

    @pl.loop(0, count)
    def _(i):
        qs = phys(i)
        start = start_ref[0:1, pl.ds(pl.multiple_of(i * BLK, BLK), BLK)]

        def step(ks, mask, carry):
            scores = [
                jnp.where(mask, dot(kn_ref[h, ks, :], qkv_ref[h, 0, :, qs]), NEG)
                for h in range(heads)
            ]
            out = []
            for h in range(heads):
                top = jnp.max(scores[h], axis=0, keepdims=True)
                if carry is not None:
                    top = jnp.maximum(top, carry[h][0])
                expo = jnp.exp2(scores[h] * LOG2E - top * LOG2E)
                total = jnp.sum(expo, axis=0, keepdims=True)
                mixed = dot(qkv_ref[h, 2, :, ks], expo.astype(bf16))
                if carry is not None:
                    fade = jnp.exp2((carry[h][0] - top) * LOG2E)
                    total = total + carry[h][1] * fade
                    mixed = mixed + carry[h][2] * fade
                out.append((top, total, mixed))
            return tuple(out)

        carry = step(qs, (ik <= iq) & (ik >= start - i * BLK), None)
        carry = lax.fori_loop(
            lo_ref[i], i, lambda j, c: step(phys(j), ik >= start - j * BLK, c), carry
        )
        for h in range(heads):
            top, total, mixed = carry[h]
            at = slice(h * HEAD_DIM, (h + 1) * HEAD_DIM)
            o_ref[at, qs] = (mixed * (1.0 / total)).astype(bf16)
            lse_ref[h, 0:1, qs] = top * LOG2E + jnp.log2(total)


def chunk(refs, k, rows):
    for at, ref in spans(refs, 0):
        if at.start <= k * rows < at.stop:
            return ref[k * rows - at.start : (k + 1) * rows - at.start, :]


def attend_back_kernel(
    place_ref, lo_ref, start_ref, qkv_ref, o_ref, do0_ref, do1_ref, do2_ref, lse_ref, cos_ref,
    sin_ref, dqkv_ref, do_ref, kn_ref, vn_ref, dk_ref, dv_ref,
):
    heads, seq = qkv_ref.shape[0], qkv_ref.shape[3]
    count = seq // BLK
    phys = blocks(place_ref, count, count // 4)
    half = ROT // 2
    for at, ref in spans((do0_ref, do1_ref, do2_ref), 1):
        do_ref[:, at] = ref[...]
    for h in range(heads):
        for b in range(count):
            r = slice(b * BLK, (b + 1) * BLK)
            kn_ref[h, r, :] = qkv_ref[h, 1, :, r].T
            vn_ref[h, r, :] = qkv_ref[h, 2, :, r].T
    dk_ref[...] = jnp.zeros_like(dk_ref)
    dv_ref[...] = jnp.zeros_like(dv_ref)
    ik = lax.broadcasted_iota(i32, (BLK, BLK), 0)
    iq = lax.broadcasted_iota(i32, (BLK, BLK), 1)

    def unrotate(grad, cosine, sine):
        one, two = grad[:half], grad[half:ROT]
        return jnp.concatenate(
            [one * cosine + two * sine, two * cosine - one * sine, grad[ROT:]], axis=0
        )

    @pl.loop(0, count)
    def _(i):
        qs = phys(i)
        here = pl.ds(pl.multiple_of(i * BLK, BLK), BLK)
        start = start_ref[0:1, here]
        dos = [do_ref[h * HEAD_DIM : (h + 1) * HEAD_DIM, qs] for h in range(heads)]
        delta = [
            jnp.sum(
                dos[h].astype(f32) * o_ref[h * HEAD_DIM : (h + 1) * HEAD_DIM, qs].astype(f32),
                axis=0, keepdims=True,
            )
            for h in range(heads)
        ]
        lse = [lse_ref[h, 0:1, qs] for h in range(heads)]

        def step(ks, mask, carry):
            scores = [
                jnp.where(mask, dot(kn_ref[h, ks, :], qkv_ref[h, 0, :, qs]), NEG)
                for h in range(heads)
            ]
            dprobs = [dot(vn_ref[h, ks, :], dos[h]) for h in range(heads)]
            probs = [jnp.exp2(scores[h] * LOG2E - lse[h]) for h in range(heads)]
            dscores = [(probs[h] * (dprobs[h] - delta[h])).astype(bf16) for h in range(heads)]
            out = []
            for h in range(heads):
                dv_ref[h, :, ks] += dot_nt(dos[h], probs[h].astype(bf16))
                dk_ref[h, :, ks] += dot_nt(qkv_ref[h, 0, :, qs], dscores[h])
                dq = dot(qkv_ref[h, 1, :, ks], dscores[h])
                out.append(dq if carry is None else carry[h] + dq)
            return tuple(out)

        carry = step(qs, (ik <= iq) & (ik >= start - i * BLK), None)
        carry = lax.fori_loop(
            lo_ref[i], i, lambda j, c: step(phys(j), ik >= start - j * BLK, c), carry
        )
        for h in range(heads):
            dq = unrotate(carry[h] * HEAD_DIM ** (-0.5), cos_ref[:, here], sin_ref[:, here])
            dqkv_ref[h, 0, :, qs] = dq.astype(bf16)

    @pl.loop(0, count)
    def _(i):
        qs = phys(i)
        here = pl.ds(pl.multiple_of(i * BLK, BLK), BLK)
        for h in range(heads):
            dk = unrotate(dk_ref[h, :, qs], cos_ref[:, here], sin_ref[:, here])
            dqkv_ref[h, 1, :, qs] = dk.astype(bf16)
            dqkv_ref[h, 2, :, qs] = dv_ref[h, :, qs].astype(bf16)


def qkv_end_kernel(
    place_ref, dqkv_ref, xh0_ref, xh1_ref, xh2_ref, wq_ref, g1_ref, b1_ref,
    o_ref, dy0_ref, dy1_ref, dy2_ref, dy3_ref, ka_ref, sa_ref, kb_ref, sb_ref, pay_ref,
):
    heads, seq = dqkv_ref.shape[0], dqkv_ref.shape[3]
    g1, b1 = row_of(g1_ref), row_of(b1_ref)
    cols = 3 * HEAD_DIM
    gain, bias, bq = 0.0, 0.0, []
    for h in range(heads):
        grad = dqkv_ref[h].reshape(cols, seq)
        raw = None
        for at, ref in spans((xh0_ref, xh1_ref, xh2_ref), 0):
            part = dot(grad[:, at], ref[...])
            raw = part if raw is None else raw + part
        total = jnp.sum(grad.astype(f32), axis=1, keepdims=True)
        bq.append(jnp.broadcast_to(total, (cols, 128)).T[0:1, :])
        pay_ref[h * cols : (h + 1) * cols, :] = (raw * g1 + total * b1).astype(bf16)
        weight = wq_ref[h * cols : (h + 1) * cols, :].astype(f32)
        gain = gain + jnp.sum(weight * raw, axis=0, keepdims=True)
        bias = bias + jnp.sum(weight * total, axis=0, keepdims=True)
    dense = None
    for at, ref in spans((dy0_ref, dy1_ref, dy2_ref, dy3_ref), 0):
        part = dot(o_ref[:, at], ref[...])
        dense = part if dense is None else dense + part
    pay_ref[heads * cols :, :] = dense.astype(bf16)
    width = pay_ref.shape[1]
    zeros = jnp.zeros((1, width - heads * cols), f32)
    vectors = pair_rows([gain, bias, jnp.concatenate(bq + [zeros], axis=1), jnp.zeros((1, width), f32)])
    rows = kb_ref.shape[0]
    top, bottom = pay_ref.at[0 : 2 * rows], pay_ref.at[2 * rows : 4 * rows]
    halves(top, ka_ref.at[0:rows], sa_ref.at[0:rows], bit_of(place_ref, ORDER_A[0]))
    halves(bottom, kb_ref, sb_ref, bit_of(place_ref, ORDER_B[0]))
    ka_ref[rows:, :] = vectors
    sa_ref[rows:, :] = vectors


def sides_kernel(
    dqkv_ref, back0_ref, back1_ref, back2_ref, wq_ref, g1_ref,
    o_ref, out0_ref, out1_ref, out2_ref, wd_ref,
    outn_ref, outf_ref, backn_ref, backf_ref, send_ref,
):
    rows = outn_ref.shape[0]
    g1 = row_of(g1_ref)
    cols = wq_ref.shape[0]
    for k in range(4):
        r = slice(k * rows, (k + 1) * rows)
        back = chunk((back0_ref, back1_ref, back2_ref), k, rows).astype(f32)
        back = back + dot_tn(dqkv_ref[:, :, :, r].reshape(cols, rows), wq_ref[...]) * g1
        out = chunk((out0_ref, out1_ref, out2_ref), k, rows).astype(f32)
        out = out + dot_tn(o_ref[:, r], wd_ref[...])
        for value, keep, place in ((out, (outn_ref, outf_ref), 0), (back, (backn_ref, backf_ref), 2)):
            if k % 2:
                at = (place + k // 2) * rows
                send_ref[at : at + rows, :] = value.astype(bf16)
            else:
                keep[k // 2][...] = value


def forward_kernel(outf_ref, backf_ref, got_ref, sent_ref):
    rows = outf_ref.shape[0]
    for i, ref in enumerate((outf_ref, backf_ref)):
        got = got_ref[(2 * i + 1) * rows : (2 * i + 2) * rows, :].astype(f32)
        sent_ref[i * rows : (i + 1) * rows, :] = (ref[...] + got).astype(bf16)


def result_kernel(x_ref, keep_ref, got_ref, far_ref, bd_ref, c2_ref, out_ref):
    rows = x_ref.shape[0]
    summed = keep_ref[...] + got_ref[:rows, :].astype(f32) + far_ref[:rows, :].astype(f32)
    out_ref[...] = (x_ref[...].astype(f32) + summed + (row_of(bd_ref) + row_of(c2_ref))).astype(bf16)


def tokens_grad_kernel(x_ref, dy_ref, keep_ref, got_ref, far_ref, out_ref):
    rows = x_ref.shape[0]
    grad = keep_ref[...] + got_ref[2 * rows : 3 * rows, :].astype(f32) + far_ref[rows:, :].astype(f32)
    x = x_ref[...].astype(f32)
    c = x - jnp.mean(x, axis=1, keepdims=True)
    inverse = lax.rsqrt(jnp.mean(c * c, axis=1, keepdims=True) + 1e-05)
    xh = c * inverse
    term = grad - jnp.mean(grad, axis=1, keepdims=True)
    term = term - xh * jnp.mean(grad * xh, axis=1, keepdims=True)
    out_ref[...] = dy_ref[...].astype(f32) + inverse * term


def swap(value, axis, size, distance):
    return lax.ppermute(value, axis, [(i, i ^ distance) for i in range(size)])


def unpair(rows):
    rows = rows.astype(f32)
    return rows[0:4, :] + rows[4:8, :]


def half_sum(keep_ref, got_ref, half, rows):
    at = pl.ds(pl.multiple_of(half * rows, 16), rows)
    return (keep_ref[at, :].astype(f32) + got_ref[at, :].astype(f32)).astype(bf16)


def vector_sum(keep_ref, got_ref):
    return unpair(keep_ref[-8:, :]) + unpair(got_ref[-8:, :])


def fold_kernel(place_ref, ka_ref, ga_ref, kb_ref, gb_ref, *outs):
    for keep_ref, got_ref, next_ref, send_ref, order in (
        (ka_ref, ga_ref, outs[0], outs[1], ORDER_A), (kb_ref, gb_ref, outs[2], outs[3], ORDER_B),
    ):
        rows = keep_ref.shape[0] // 16 * 8
        side = bit_of(place_ref, order[1])
        for half, out_ref in ((side, next_ref), (1 - side, send_ref)):
            out_ref[0:rows, :] = half_sum(keep_ref, got_ref, half, rows)
    vectors = pair_rows([vector_sum(ka_ref, ga_ref)])
    outs[0][-8:, :] = vectors
    outs[1][-8:, :] = vectors


def far_fold_kernel(place_ref, ka_ref, ga_ref, kb_ref, gb_ref, next_ref, send_ref):
    side = bit_of(place_ref, ORDER_A[2])
    first = 0
    for keep_ref, got_ref in ((ka_ref, ga_ref), (kb_ref, gb_ref)):
        rows = keep_ref.shape[0] // 16 * 8
        for half, out_ref in ((side, next_ref), (1 - side, send_ref)):
            out_ref[first : first + rows, :] = half_sum(keep_ref, got_ref, half, rows)
        first += rows
    vectors = pair_rows([vector_sum(ka_ref, ga_ref)])
    next_ref[first:, :] = vectors
    send_ref[first:, :] = vectors


def total_kernel(keep_ref, got_ref, out_ref, vector_ref):
    rows = out_ref.shape[0]
    total = keep_ref[0:rows, :].astype(f32) + got_ref[0:rows, :].astype(f32)
    out_ref[...] = total.astype(bf16)
    vector_ref[...] = vector_sum(keep_ref, got_ref)


def put_halves(out_ref, mine, got, side):
    rows = mine.shape[0]
    for half, value in ((side, mine), (1 - side, got)):
        out_ref[pl.ds(pl.multiple_of(half * rows, 16), rows), :] = value.astype(out_ref.dtype)


def far_join_kernel(place_ref, mine_ref, got_ref, a_ref, b_ref):
    side = bit_of(place_ref, ORDER_A[2])
    first = 0
    for out_ref in (a_ref, b_ref):
        r = slice(first, first + out_ref.shape[0] // 2)
        put_halves(out_ref, mine_ref[r, :], got_ref[r, :], side)
        first = r.stop


def join_kernel(place_ref, ma_ref, ga_ref, mb_ref, gb_ref, a_ref, b_ref, *, step):
    put_halves(a_ref, ma_ref[...], ga_ref[...], bit_of(place_ref, ORDER_A[step]))
    put_halves(b_ref, mb_ref[...], gb_ref[...], bit_of(place_ref, ORDER_B[step]))


def spread_kernel(place_ref, ma_ref, ga_ref, mb_ref, gb_ref, wq_ref, wd_ref):
    rows = ma_ref.shape[0]
    put_halves(wq_ref.at[0 : 2 * rows], ma_ref[...], ga_ref[...], bit_of(place_ref, ORDER_A[0]))
    side = bit_of(place_ref, ORDER_B[0])
    mine, got = mb_ref[...].astype(f32), gb_ref[...].astype(f32)
    wq_ref[2 * rows :, :] = jnp.where(side == 0, mine, got)
    wd_ref[...] = jnp.where(side == 0, got, mine)


def vectors_kernel(n0_ref, n1_ref, n2_ref, n3_ref, a_ref, c_ref, *out_refs):
    near = (n0_ref[...] + n1_ref[...]) + (n2_ref[...] + n3_ref[...])
    for i in range(4):
        out_refs[i][...] = near[i : i + 1, :].reshape(-1)
    out_refs[4][...] = a_ref[2:3, :].reshape(-1)
    out_refs[5][...] = a_ref[2:3, :].reshape(-1)
    out_refs[6][...] = a_ref[3:4, :].reshape(-1)
    out_refs[7][...] = c_ref[2:3, : out_refs[7].shape[0]].reshape(-1)


def dp_swap(value, dp, bit):
    return swap(value, "dp", dp, 1 << bit)


def rest_sum(value, dp):
    if dp == 8:
        return value
    groups = [[i + 8 * j for j in range(dp // 8)] for i in range(8)]
    return lax.psum(value.astype(f32), "dp", axis_index_groups=groups).astype(value.dtype)


def rotary_tables(length):
    half = ROT // 2
    freq = np.float32(10000.0) ** (-(np.arange(half, dtype=np.float32) * 2.0) / ROT)
    angle = freq.astype(np.float32)[:, None] * np.arange(length, dtype=np.float32)[None, :]
    return np.cos(angle).astype(np.float32), np.sin(angle).astype(np.float32)


def body(dp, tp, tokens, segment_ids, cotangent, gain1, bias1, gain2, bias2,
         qkv_weight, qkv_bias, dense_weight, dense_bias, fc_in_weight, fc_in_bias,
         fc_out_weight, fc_out_bias):
    assert tp == 4 and dp % 8 == 0
    x0, dy0 = tokens[0], cotangent[0]
    rows, width = x0.shape
    seq = rows * tp
    count = seq // BLK
    wq = qkv_weight.T
    heads = wq.shape[0] // (3 * HEAD_DIM)
    cosine, sine = rotary_tables(seq)
    place = jnp.stack([lax.axis_index("tensor"), lax.axis_index("dp")]).astype(i32)

    x1 = swap(x0, "tensor", tp, 1)
    x2 = swap(x0, "tensor", tp, 2)
    dy1 = swap(dy0, "tensor", tp, 1)
    dy2 = swap(dy0, "tensor", tp, 2)

    bq_column = qkv_bias.astype(f32)[:, None]
    start, lo = call(
        segments_kernel, "segments", [segment_ids, segment_ids],
        [like((1, seq), i32), like((count,), i32)], smem=(1,), smem_out=(1,), flops=cost("segments"),
    )
    (x1,) = after(start, x1)
    hidden, inner = fc_in_weight.shape[1], dense_weight.shape[0]

    def front(xs, first):
        size = rows * len(xs)
        return call(
            partial(front_kernel, first=first, pieces=len(xs)), "front",
            [place, *xs, gain1, bias1, gain2, bias2, fc_in_weight, fc_in_bias, wq, bq_column,
             cosine, sine],
            [like((size, width), bf16), like((size, hidden), bf16), like((size, hidden), bf16),
             like((heads, 3, HEAD_DIM, size), bf16)],
            smem=(0,), limit=16, flops=cost("front", len(xs)),
        )

    def ff_back(dys, act, slope, xh, carry=(), last=False):
        size = rows * len(dys)
        outs = [like((size, width), bf16), like((size, width), bf16), like((inner, size), bf16)]
        full = [like((width, hidden), f32), like((hidden, width), f32)]
        sums = [like((8, width), f32)]
        half = [like((width // 2, hidden), bf16)] * 2 + [like((hidden // 2 + 8, width), bf16)] * 2
        scratch = [
            pltpu.VMEM((width, hidden), f32), pltpu.VMEM((hidden, width), f32),
            pltpu.VMEM((width, hidden), bf16),
        ]
        return call(
            partial(ff_back_kernel, pieces=len(dys), carried=bool(carry), last=last), "ff_back",
            [place, *dys, act, slope, xh, gain2, bias2, fc_in_weight, fc_out_weight, dense_weight,
             *carry],
            outs + (half if last else full + sums), scratch if last else [],
            smem=(0,), limit=22 if last else 16, flops=cost("ff_back", len(dys)),
        )

    xh0, act0, slope0, qkv0 = front((x0, x1), 0)
    (act0,) = after(qkv0, act0)
    out0, back0, do0, *carry = ff_back((dy0, dy1), act0, slope0, xh0)
    x3 = swap(*after(carry[2], x2), "tensor", tp, 1)
    (x2,) = after(carry[2], x2)
    xh1, act1, slope1, qkv1 = front((x2,), 2)
    (x3,) = after(qkv1, x3)
    xh2, act2, slope2, qkv2 = front((x3,), 3)
    qkv, mixed, lse = call(
        attend_kernel, "attend", [place, lo, start, qkv0, qkv1, qkv2],
        [like((heads, 3, HEAD_DIM, seq), bf16), like((inner, seq), bf16), like((heads, 1, seq), f32)],
        [pltpu.VMEM((heads, seq, HEAD_DIM), bf16)],
        smem=(0, 1), limit=12, flops=cost("attend"),
    )
    dy3 = swap(*after(lse, dy2), "tensor", tp, 1)
    (dy2,) = after(lse, dy2)
    out1, back1, do1, *carry = ff_back((dy2,), act1, slope1, xh1, carry)
    (dy3,) = after(carry[2], dy3)
    out2, back2, do2, k1, s1, k2, s2 = ff_back((dy3,), act2, slope2, xh2, carry, last=True)

    run = Chain(do2)
    tail = 8
    keep, got, vectors, made = {}, {}, {}, {}

    def part(count):
        return like((count, width), bf16)

    def send(name, a, b, step):
        got[name] = [dp_swap(a, dp, ORDER_A[step]), dp_swap(b, dp, ORDER_B[step])]

    def parts(name):
        (ka, kb), (ga, gb) = keep[name], got[name]
        return [place, ka, ga, kb, gb]

    def fold(name):
        na, nb = keep[name][0].shape[0] // 16 * 8, keep[name][1].shape[0] // 2
        ka, sa, kb, sb = run(
            fold_kernel, "fold", parts(name), [part(na + tail)] * 2 + [part(nb)] * 2,
            hold=2, smem=(0,), flops=cost(f"{name}1"),
        )
        keep[name] = ka, kb
        send(name, sa, sb, 1)

    def far_fold(name):
        count = sum(k.shape[0] // 16 * 8 for k in keep[name]) + tail
        keep[name], sent = run(
            far_fold_kernel, "far_fold", parts(name), [part(count)] * 2, hold=2, smem=(0,),
            flops=cost(f"{name}2"),
        )
        got[name] = dp_swap(sent, dp, ORDER_A[2])

    def complete(name):
        total, vector = run(
            total_kernel, "total", [keep[name], got[name]],
            [part(keep[name].shape[0] - tail), like((4, width), f32)], hold=1,
            flops=cost(f"{name}3"),
        )
        keep[name], vectors[name] = rest_sum(total, dp), rest_sum(vector, dp)
        got[name] = dp_swap(keep[name], dp, ORDER_A[2])
        if len(vectors) == 2:
            near = jnp.concatenate([vectors["q"][:2], vectors["p"][:2]], axis=0)
            made["near"] = [near] + [swap(near, "tensor", tp, k) for k in range(1, tp)]

    def far_join(name):
        keep[name] = run(
            far_join_kernel, "far_join", [place, keep[name], got[name]],
            [part(keep[name].shape[0])] * 2, hold=2, smem=(0,), flops=cost(f"{name}4"),
        )
        send(name, *keep[name], 1)

    def join(name):
        keep[name] = run(
            partial(join_kernel, step=1), "join", parts(name),
            [part(2 * k.shape[0]) for k in keep[name]], hold=2, smem=(0,), flops=cost(f"{name}5"),
        )
        send(name, *keep[name], 0)

    def finish_p():
        made["p"] = run(
            partial(join_kernel, step=0), "grads", parts("p"),
            [like((hidden, width), f32), like((width, hidden), f32)], hold=2, smem=(0,),
            flops=cost("p6"),
        )

    def finish_q():
        made["q"] = run(
            spread_kernel, "spread", parts("q"),
            [like((wq.shape[0], width), f32), like((inner, width), f32)], hold=2, smem=(0,),
            flops=cost("q6"),
        )

    def attend_back():
        (made["dqkv"],) = run(
            attend_back_kernel, "attend_back",
            [place, lo, start, qkv, mixed, do0, do1, do2, lse, cosine, sine],
            [like((heads, 3, HEAD_DIM, seq), bf16)], hold=4,
            scratch=[
                pltpu.VMEM((inner, seq), bf16),
                pltpu.VMEM((heads, seq, HEAD_DIM), bf16), pltpu.VMEM((heads, seq, HEAD_DIM), bf16),
                pltpu.VMEM((heads, HEAD_DIM, seq), f32), pltpu.VMEM((heads, HEAD_DIM, seq), f32),
            ],
            smem=(0, 1), limit=20, flops=cost("attend_back"),
        )

    def qkv_end():
        count = (wq.shape[0] + inner) // 4
        ka, sa, kb, sb = run(
            qkv_end_kernel, "qkv_end",
            [place, made["dqkv"], xh0, xh1, xh2, wq, gain1, bias1, mixed, dy0, dy1, dy2, dy3],
            [part(count + tail)] * 2 + [part(count)] * 2, hold=1,
            scratch=[pltpu.VMEM((4 * count, width), bf16)], smem=(0,), limit=12,
            flops=cost("qkv_end"),
        )
        keep["q"] = ka, kb
        send("q", sa, sb, 0)

    def sides():
        *made["sides"], sent = run(
            sides_kernel, "sides",
            [made["dqkv"], back0, back1, back2, wq, gain1, mixed, out0, out1, out2, dense_weight],
            [like((rows, width), f32)] * 4 + [like((4 * rows, width), bf16)],
            hold=0, limit=12, flops=cost("sides"),
        )
        made["crossed"] = swap(sent, "tensor", tp, 1)

    def forward():
        _, far_out, _, far_back = made["sides"]
        (sent,) = run(
            forward_kernel, "forward", [far_out, far_back, made["crossed"]],
            [like((2 * rows, width), bf16)], hold=2, flops=cost("forward"),
        )
        made["far"] = swap(sent, "tensor", tp, 2)

    def result():
        (made["result"],) = run(
            result_kernel, "result",
            [x0, made["sides"][0], made["crossed"], made["far"], dense_bias, fc_out_bias],
            [like((rows, width), bf16)], hold=3, flops=cost("result"),
        )

    def tokens_grad():
        (made["tokens_grad"],) = run(
            tokens_grad_kernel, "tokens_grad",
            [x0, dy0, made["sides"][2], made["crossed"], made["far"]],
            [like((rows, width), f32)], hold=4, flops=cost("tokens_grad"),
        )

    def finish_vectors():
        flat = like((width,), f32)
        made["vectors"] = run(
            vectors_kernel, "vectors", [*made["near"], vectors["p"], vectors["q"]],
            [flat] * 7 + [like((wq.shape[0],), f32)], hold=0, flops=cost("vectors"),
        )

    steps = {
        "attend_back": attend_back, "qkv_end": qkv_end, "sides": sides, "forward": forward,
        "result": result, "tokens_grad": tokens_grad, "vectors": finish_vectors,
        "p6": finish_p, "q6": finish_q,
    }
    for name in "pq":
        for step, act in enumerate((fold, far_fold, complete, far_join, join)):
            steps[f"{name}{step + 1}"] = partial(act, name)
    keep["p"] = k2, k1
    send("p", s2, s1, 0)
    for step in SEQUENCE:
        steps[step]()
    *vectors, bq_grad = made["vectors"]
    (w2_grad, w1_grad), (wq_grad, wd_grad) = made["p"], made["q"]
    result, input_grad = made["result"], made["tokens_grad"]
    gain1_grad, bias1_grad, gain2_grad, bias2_grad, dense_sum, out_sum, du_sum = vectors
    return (
        result[None], input_grad[None], gain1_grad, bias1_grad, gain2_grad, bias2_grad,
        wq_grad.T, bq_grad, wd_grad, dense_sum, w1_grad, du_sum, w2_grad, out_sum,
    )


def solution(mesh):
    split = P("dp", "tensor", None)
    columns, stacked, vector = P(None, "tensor"), P("tensor", None), P("tensor")
    whole = P()
    return jax.shard_map(
        partial(body, mesh.shape["dp"], mesh.shape["tensor"]),
        mesh=mesh,
        in_specs=(
            split, P("dp", None), split, whole, whole, whole, whole, columns, vector, stacked,
            whole, columns, vector, stacked, whole,
        ),
        out_specs=(
            split, split, whole, whole, whole, whole, columns, vector, stacked, whole, columns,
            vector, stacked, whole,
        ),
        check_vma=False,
    )
```
